32 devices in a mesh: outer: 4 (over y, x), inner: 8 (over z, core).
Axes of the slice: x: 2, y: 2, z: 4, core: 2. Of those that a mesh axis runs over, the one named last changes fastest.
Arguments:
- inputs: bfloat16 [8192, 8192], P(('outer', 'inner')), may hold values from -6 to 6
- step_size: float32 [8192, 128], P(('outer', 'inner')), may hold values from 0 to 1
- log_decay: float32 [8192, 128], P(('outer', 'inner')), may hold values from -1.25 to 0
- b_matrix: bfloat16 [8192, 1024], P(('outer', 'inner')), may hold values from -1 to 1
- c_matrix: bfloat16 [8192, 1024], P(('outer', 'inner')), may hold values from -1 to 1
- skip_gain: float32 [128], replicated, may hold values from 0.5 to 1.5
Outputs:
- mixed: bfloat16 [8192, 8192], P(('outer', 'inner'))
The draws below stay inside these ranges and needn't reach their ends.
All inputs are finite; a program needn't handle non-finite values.
Results may differ from the reference program's by a relative error of at most 0.006.
Values may be sent and summed in bfloat16 or wider, within the bound.
No kernel may reach another device: no remote copies, remote signals or barrier semaphores. Data moves between devices by JAX's collectives and lax.ppermute only.
A program may use at most 128 MiB of HBM per device.

```python
import math
import jax
import jax.numpy as jnp
from jax import lax

HEAD_COUNT_ALL = 128
HEAD_DIM = 64
STATE = 128
GROUPS = 8
BLOCK_LENGTH = 256
TOKEN_COUNT_ALL = 8192


def decay_law(key):
    key_pick = jax.random.fold_in(key, 21)
    random_key_period = jax.random.fold_in(key, 22)
    random_key_starts = jax.random.fold_in(key, 23)
    key_depth = jax.random.fold_in(key, 24)
    key_regime = jax.random.fold_in(key, 25)
    slow_cut = 4
    slowly_decaying_heads = jax.random.randint(key_pick, (HEAD_COUNT_ALL,), 0, 8) < slow_cut
    spike_period = jax.random.randint(random_key_period, (HEAD_COUNT_ALL,), BLOCK_LENGTH // 2, 2 * BLOCK_LENGTH + 1)
    spike_starts = (jax.random.randint(random_key_starts, (TOKEN_COUNT_ALL, HEAD_COUNT_ALL), 0, spike_period[None, :]) == 0).astype(jnp.int32)
    extended_index = jnp.cumsum(spike_starts, axis=0).astype(jnp.int32)
    delayed_index = jnp.pad(extended_index, ((8, 0), (0, 0)))[:TOKEN_COUNT_ALL]
    spike_count = (extended_index - delayed_index).astype(jnp.float32)
    depth_lookup = jax.random.uniform(key_depth, (TOKEN_COUNT_ALL + 1, HEAD_COUNT_ALL), jnp.float32, 2.5, 10.0)
    spike_depth = jnp.take_along_axis(depth_lookup, extended_index, axis=0)
    regime_table = jnp.exp(jax.random.uniform(key_regime, (TOKEN_COUNT_ALL + 1, HEAD_COUNT_ALL), jnp.float32, math.log(0.02), math.log(0.4)))
    regime_factor = jnp.take_along_axis(regime_table, extended_index, axis=0)
    return (slowly_decaying_heads, spike_count, spike_depth, regime_factor)


def draw_log_decay(key, part):
    decay_law_terms = decay_law(jax.random.fold_in(key, 7))
    slowly_decaying_heads = decay_law_terms[0]
    spike_count = decay_law_terms[1]
    spike_depth = decay_law_terms[2]
    key_slow = jax.random.fold_in(key, 12)
    key_base = jax.random.fold_in(key, 13)
    key_rough = jax.random.fold_in(key, 14)
    key_for_spike = jax.random.fold_in(key, 15)
    key_for_decrease = jax.random.fold_in(key, 16)
    slow_rate = math.log(10.0) / TOKEN_COUNT_ALL * jax.random.uniform(key_slow, (HEAD_COUNT_ALL,), jnp.float32, 0.05, 0.3)
    baseline_rate = jnp.exp(jax.random.uniform(key_base, (HEAD_COUNT_ALL,), jnp.float32, math.log(0.0005), math.log(0.004)))
    roughness_level = jnp.exp(jax.random.uniform(key_rough, (TOKEN_COUNT_ALL, HEAD_COUNT_ALL), jnp.float32, -math.log(2.0), math.log(2.0)))
    spike_position = jax.random.randint(key_for_spike, (2,), 0, TOKEN_COUNT_ALL)
    spike_row_set = jnp.any(jnp.arange(TOKEN_COUNT_ALL)[:, None] == spike_position[None, :], axis=1)
    spike_decrease = jax.random.uniform(key_for_decrease, (TOKEN_COUNT_ALL, HEAD_COUNT_ALL), jnp.float32, 0.2, 0.7)
    spike_addend = jnp.where(spike_row_set[:, None], jnp.log(1.0 - spike_decrease), 0.0)
    gradual_value = -slow_rate[None, :] * roughness_level + spike_addend
    spike_value = -baseline_rate[None, :] * roughness_level - spike_count * spike_depth / 8.0
    merged_result = jnp.where(slowly_decaying_heads[None, :], gradual_value, spike_value)
    return jnp.maximum(merged_result, -1.25).astype(jnp.float32)


def draw_step_size(key, part):
    decay_law_terms = decay_law(jax.random.fold_in(key, 7))
    slowly_decaying_heads = decay_law_terms[0]
    regime_factor = decay_law_terms[3]
    key_head = jax.random.fold_in(key, 31)
    key_jitter = jax.random.fold_in(key, 32)
    slow_base = 3.0 / math.sqrt(TOKEN_COUNT_ALL) * jnp.exp(jax.random.uniform(key_head, (HEAD_COUNT_ALL,), jnp.float32, -0.5, 0.5))
    jitter = jnp.exp(jax.random.uniform(key_jitter, (TOKEN_COUNT_ALL, HEAD_COUNT_ALL), jnp.float32, -math.log(2.0), math.log(2.0)))
    level = jnp.where(slowly_decaying_heads[None, :], slow_base[None, :], regime_factor)
    return (level * jitter).astype(jnp.float32)


def shard_levels(rng, extent, cuts, low, high):
    level = 1.0
    for position, blocks in cuts:
        heights = jax.random.uniform(jax.random.fold_in(jax.random.fold_in(rng, 6), position), (blocks,), jnp.float32, low / len(cuts), high / len(cuts))
        level = level * jnp.repeat(jnp.exp(heights), extent[position] // blocks).reshape((-1,) + (1,) * (len(extent) - 1 - position))
    return level


def gaussian(key, dims, width, most, shards=(), kind=jnp.bfloat16):
    factor_of = shard_levels(key, dims, shards, -0.22, 0.18) if shards else 1.0
    values = jax.random.normal(key, dims, jnp.float32) * width * factor_of
    return jnp.minimum(jnp.maximum(values, -most), most).astype(kind)


def setup_inputs(seed: int = 0) -> dict:
    key_of = jax.random.split(jax.random.key(seed), 7)
    return {
        "inputs": gaussian(key_of[0], (TOKEN_COUNT_ALL, HEAD_COUNT_ALL * HEAD_DIM), 1.0, 6.0, ((0, 32),)),
        "step_size": draw_step_size(jax.random.fold_in(key_of[6], 71), 0),
        "log_decay": draw_log_decay(jax.random.fold_in(key_of[6], 71), 0),
        "b_matrix": gaussian(key_of[3], (TOKEN_COUNT_ALL, GROUPS * STATE), (STATE // 4) ** -0.5, 1.0, ((0, 32),)),
        "c_matrix": gaussian(key_of[4], (TOKEN_COUNT_ALL, GROUPS * STATE), (STATE // 4) ** -0.5, 1.0, ((0, 32),)),
        "skip_gain": jnp.clip(jax.random.uniform(key_of[5], (HEAD_COUNT_ALL,), jnp.float32, 0.5, 1.5), 0.5, 1.5),
    }


def reference(inputs, step_size, log_decay, b_matrix, c_matrix, skip_gain):
    seq_rows = inputs.shape[0]
    block_rows = min(BLOCK_LENGTH, seq_rows)
    block_count = seq_rows // block_rows
    per_group = HEAD_COUNT_ALL // GROUPS
    lower_mask = jnp.tril(jnp.ones((block_rows, block_rows), dtype=bool))
    skip_cols = jnp.repeat(skip_gain, HEAD_DIM)
    highest = lax.Precision.HIGHEST
    mixed_prec = lax.Precision.HIGH

    def advance(carried, pieces):
        in_block, rate_block, log_block, b_block, c_block = pieces
        scaled = (in_block.reshape(block_rows, HEAD_COUNT_ALL, HEAD_DIM).astype(jnp.float32) * rate_block[:, :, None]).astype(jnp.bfloat16)
        as_float = scaled.astype(jnp.float32)
        running = jnp.cumsum(log_block, axis=0)
        b_groups = b_block.reshape(block_rows, GROUPS, STATE).astype(jnp.float32)
        c_groups = c_block.reshape(block_rows, GROUPS, STATE).astype(jnp.float32)
        scores = jnp.einsum('tgn,sgn->gts', c_groups, b_groups, precision=highest)
        scores_h = jnp.repeat(scores, per_group, axis=0)
        spread = running.T[:, :, None] - running.T[:, None, :]
        decays = jnp.exp(jnp.where(lower_mask[None], spread, -jnp.inf))
        diagonal_part = jnp.einsum('hts,shp->thp', scores_h * decays, as_float, precision=mixed_prec)
        c_heads = jnp.repeat(c_groups, per_group, axis=1)
        b_heads = jnp.repeat(b_groups, per_group, axis=1)
        carried_part = jnp.einsum('thn,hpn->thp', c_heads, carried, precision=mixed_prec) * jnp.exp(running)[:, :, None]
        to_end = jnp.exp(running[-1][None, :] - running)
        updated = jnp.exp(running[-1])[:, None, None] * carried + jnp.einsum('shp,shn->hpn', as_float * to_end[:, :, None], b_heads, precision=mixed_prec)
        ssd = (diagonal_part + carried_part).reshape(block_rows, HEAD_COUNT_ALL * HEAD_DIM)
        mixed_block = (ssd + skip_cols[None, :] * in_block.astype(jnp.float32)).astype(jnp.bfloat16)
        return updated, mixed_block

    start_state = jnp.zeros((HEAD_COUNT_ALL, HEAD_DIM, STATE), jnp.float32)
    pieces = (inputs.reshape(block_count, block_rows, HEAD_COUNT_ALL * HEAD_DIM),
              step_size.reshape(block_count, block_rows, HEAD_COUNT_ALL),
              log_decay.reshape(block_count, block_rows, HEAD_COUNT_ALL),
              b_matrix.reshape(block_count, block_rows, GROUPS * STATE),
              c_matrix.reshape(block_count, block_rows, GROUPS * STATE))
    _, mixed_blocks = lax.scan(advance, start_state, pieces)
    return mixed_blocks.reshape(seq_rows, HEAD_COUNT_ALL * HEAD_DIM)
```

```python
import functools
import math

import jax
import jax.numpy as jnp
from jax import lax
from jax.experimental import pallas as pl
from jax.experimental.pallas import tpu as pltpu
from jax.sharding import Mesh, PartitionSpec as P

GROUPS = 8
CORES = 2
LANES = 128
ROW_TILE = 8
HALF_ROWS = 128
ROW_BLOCK = 32
LOG2E = 1.0 / math.log(2.0)

F32 = jnp.float32
BF16 = jnp.bfloat16


def dot(a, b, contract=(1, 0), precision=None):
    dims = (((contract[0],), (contract[1],)), ((), ()))
    return lax.dot_general(a, b, dims, precision=precision, preferred_element_type=F32)


def spreader(heads, lanes, width):
    shape = (2 * lanes, heads * width)
    row = lax.broadcasted_iota(jnp.int32, shape, 0)
    col = lax.broadcasted_iota(jnp.int32, shape, 1)
    row = jnp.where(row >= lanes, row - lanes, row)
    return jnp.where(row == col // width, 1.0, 0.0).astype(BF16)


def high_low(values):
    high = values.astype(BF16)
    low = (values - high.astype(F32)).astype(BF16)
    return high, low


def spread(values, matrix):
    return dot(jnp.concatenate(high_low(values), axis=1), matrix)


def group_first(values, group, per_group):
    lanes = values.shape[1]
    return pltpu.roll(values, lax.rem(lanes - group * per_group, lanes), 1)


def params():
    return pltpu.CompilerParams(dimension_semantics=("arbitrary",))


def state_rows(x, b, factor, total, matrix):
    scaled = (x.astype(F32) * spread(factor, matrix)).astype(BF16)
    return dot(b, scaled, (0, 0)), spread(total, matrix)


def send_state_kernel(half, x, b, step, log, out, run_out, run_t_out, factor_out, total_out, matrix, *, dims):
    per_half, per_group, width = dims
    turn = pl.program_id(0)

    @pl.when(turn == 0)
    def _():
        rows = log.shape[0]
        upto = lax.broadcasted_iota(jnp.int32, (rows, rows), 1) <= lax.broadcasted_iota(jnp.int32, (rows, rows), 0)
        running = dot(upto.astype(F32), log[...], precision=lax.Precision.HIGHEST) * LOG2E
        last = running[rows - 1 :, :]
        run_out[...] = running
        run_t_out[...] = running.T
        factor_out[...] = step[...] * jnp.exp2(last - running)
        total_out[...] = jnp.broadcast_to(jnp.exp2(last), total_out.shape)
        matrix[...] = spreader(per_group, log.shape[1], width)

    group = half[0] * per_half + turn
    factor = group_first(factor_out[...], group, per_group)
    total = group_first(total_out[...], group, per_group)
    state, decay = state_rows(x[...], b[...], factor, total, matrix[...])
    states = state.shape[0]
    out[:states, :] = state.astype(BF16)
    high, low = high_low(decay)
    total_high, total_low = high_low(total_out[...])
    heads = total_high.shape[1]
    row = lax.broadcasted_iota(jnp.int32, decay.shape, 0)
    out[states:, :] = jnp.where(row == 0, high.astype(F32), low.astype(F32)).astype(BF16)
    tail = out[states:, :heads].astype(F32)
    packed = jnp.where(row[:, :heads] == 2, total_high.astype(F32), total_low.astype(F32))
    out[states:, :heads] = jnp.where(row[:, :heads] < 2, tail, packed).astype(BF16)


def own_state_kernel(half, x, b, factor_in, total_in, out, matrix, *, dims):
    per_half, per_group, width = dims
    turn = pl.program_id(0)

    @pl.when(turn == 0)
    def _():
        matrix[...] = spreader(per_group, factor_in.shape[1], width)

    group = half[0] * per_half + turn
    factor = group_first(factor_in[...], group, per_group)
    total = group_first(total_in[...], group, per_group)
    state, decay = state_rows(x[...], b[...], factor, total, matrix[...])
    states = state.shape[0]
    out[:states, :] = state
    out[states:, :] = decay


def both_decays(own_tail, got_tail):
    own_decay = own_tail[:1, :]
    got_decay = got_tail[:1, :].astype(F32) + got_tail[1:2, :].astype(F32)
    return own_decay, got_decay


def chip_total_kernel(core, own, own_tail, got, got_tail, total, out):
    first = core[0] == 0
    cols = own.shape[1]
    own_decay, got_decay = both_decays(own_tail[...], got_tail[...])
    on_own = jnp.where(first, got_decay, jnp.ones_like(got_decay))
    on_got = jnp.where(first, jnp.ones_like(own_decay), own_decay)
    out[:, :cols] = (on_own * own[...] + on_got * got[...].astype(F32)).astype(BF16)
    lanes = total.shape[1]
    half = lanes // CORES
    other_total = got_tail[2:3, :lanes].astype(F32) + got_tail[3:4, :lanes].astype(F32)
    both = total[...] * other_total
    both = jnp.where(first, both, pltpu.roll(both, half, 1))
    high, low = high_low(both)
    lane = lax.broadcasted_iota(jnp.int32, both.shape, 1)
    packed = jnp.where(lane < half, high.astype(F32), pltpu.roll(low.astype(F32), half, 1))
    out[:, cols:] = jnp.concatenate([packed] * (out.shape[0] // packed.shape[0]), axis=0).astype(BF16)


def prefix_kernel(sent, decays, out, *, width):
    chips, rows, lanes = sent.shape
    heads_here = lanes // width
    block = pl.program_id(0)
    half = decays.shape[2] // 2
    packed = decays[...]
    first_rows = jnp.concatenate([packed[k, :1, :].astype(F32) for k in range(chips)], axis=0)
    values = first_rows + pltpu.roll(first_rows, half, 1)
    values = pltpu.roll(values, lax.rem(2 * half - block * heads_here, 2 * half), 1)
    decay = spread(values, spreader(heads_here, 2 * half, width))
    state = jnp.zeros((rows, lanes), F32)
    for k in range(chips):
        out[k] = state.astype(BF16)
        state = decay[k : k + 1, :] * state + sent[k].astype(F32)


def incoming_kernel(core, own, own_tail, got, got_tail, entering, mine, send):
    first = core[0] == 0
    own_decay, got_decay = both_decays(own_tail[...], got_tail[...])
    state = entering[...].astype(F32)
    decay = jnp.where(first, own_decay, got_decay)
    later = decay * state + jnp.where(first, own[...], got[...].astype(F32))
    mine[...] = jnp.where(first, state, later).astype(BF16)
    send[...] = jnp.where(first, later, state).astype(BF16)


def within_kernel(x_ref, b_ref, c_ref, step_ref, run_ref, run_t_ref, skip_ref, out, matrix, *, dims):
    per_group, width = dims
    group = pl.program_id(0)
    rows = x_ref.shape[0]

    @pl.when(group == 0)
    def _():
        matrix[...] = spreader(per_group, step_ref.shape[1], width)

    spreading = matrix[...]
    step = group_first(step_ref[...], group, per_group)
    run = group_first(run_ref[...], group, per_group)
    skip = group_first(jnp.broadcast_to(skip_ref[...], (ROW_TILE, skip_ref.shape[1])), group, per_group)
    run_t = run_t_ref[pl.ds(pl.multiple_of(group * per_group, per_group), per_group), :]
    x = x_ref[...].astype(F32)
    scaled = (x * spread(step, spreading)).astype(BF16)
    skipped = spread(skip, spreading)[:1, :] * x
    pair = LANES // width
    lane = lax.broadcasted_iota(jnp.int32, (HALF_ROWS, LANES), 1) // width
    lower = lax.broadcasted_iota(jnp.int32, (HALF_ROWS, HALF_ROWS), 1) <= lax.broadcasted_iota(
        jnp.int32, (HALF_ROWS, HALF_ROWS), 0
    )
    b = b_ref[...]
    c = c_ref[...]
    for start in range(0, rows, HALF_ROWS):
        stop = start + HALF_ROWS
        scores = jnp.where(lower, dot(c[start:stop, :], b[start:stop, :], (1, 1)), 0.0)
        if start:
            edge = run[start - 1 : start, :]
            before = step[:start, :] * jnp.exp2(edge - run[:start, :])
            before = (x[:start, :] * spread(before, spreading)).astype(BF16)
            cross = dot(c[start:stop, :], b[:start, :], (1, 1)).astype(BF16)
            after = spread(jnp.exp2(run[start:stop, :] - edge), spreading)
            base = skipped[start:stop, :] + after * dot(cross, before)
        else:
            base = skipped[start:stop, :]
        for first in range(0, per_group, pair):
            cols = slice(first * width, (first + pair) * width)
            here = scaled[start:stop, cols]
            weights = []
            values = []
            for k in range(pair):
                head = first + k
                gap = run[start:stop, head : head + 1] - run_t[head : head + 1, start:stop]
                weights.append((scores * jnp.exp2(jnp.minimum(gap, 0.0))).astype(BF16))
                values.append(jnp.where(lane == k, here, jnp.zeros_like(here)))
            part = dot(jnp.concatenate(weights, axis=1), jnp.concatenate(values, axis=0))
            out[start:stop, cols] = base[:, cols] + part


def final_kernel(half, within, c, state, run_ref, *rest, dims):
    per_half, per_group, width = dims
    out, matrix = rest[-2:]
    turn = pl.program_id(0)

    @pl.when(turn == 0)
    def _():
        matrix[...] = spreader(per_group, run_ref.shape[1], width)

    group = half[0] * per_half + turn
    grown = spread(jnp.exp2(group_first(run_ref[...], group, per_group)), matrix[...])
    out[...] = (within[...] + grown * dot(c[...], state[...])).astype(BF16)


def local(inputs, step_size, log_decay, b_matrix, c_matrix, skip_gain, *, chip_axes, core_axis):
    tokens, channels = inputs.shape
    heads = step_size.shape[1]
    width = channels // heads
    states = b_matrix.shape[1] // GROUPS
    per_group = heads // GROUPS
    group_cols = per_group * width
    per_half = GROUPS // CORES
    half_cols = channels // CORES
    half_heads = heads // CORES
    chips = lax.axis_size(chip_axes)
    rows = states // chips
    tall = states + ROW_TILE

    core = lax.axis_index(core_axis).astype(jnp.int32)
    mine = core.reshape(1)
    other = (1 - core).reshape(1)

    def of_half(block_rows):
        return pl.BlockSpec((block_rows, group_cols), lambda i, half: (0, half[0] * per_half + i))

    def matrix_of_half():
        return pl.BlockSpec((tokens, states), lambda i, half: (0, half[0] * per_half + i))

    def by_turn(block_rows):
        return pl.BlockSpec((block_rows, group_cols), lambda i, half: (0, i))

    def whole(shape):
        return pl.BlockSpec(shape, lambda i, *_: (0,) * len(shape))

    spread_scratch = pltpu.VMEM((2 * heads, group_cols), BF16)
    half_dims = (per_half, per_group, width)

    send, run, run_t, factor, total = pl.pallas_call(
        functools.partial(send_state_kernel, dims=half_dims),
        grid_spec=pltpu.PrefetchScalarGridSpec(
            num_scalar_prefetch=1,
            grid=(per_half,),
            in_specs=[of_half(tokens), matrix_of_half(), whole((tokens, heads)), whole((tokens, heads))],
            out_specs=[
                by_turn(tall),
                whole((tokens, heads)),
                whole((heads, tokens)),
                whole((tokens, heads)),
                whole((ROW_TILE, heads)),
            ],
            scratch_shapes=[spread_scratch],
        ),
        out_shape=[
            jax.ShapeDtypeStruct((tall, half_cols), BF16),
            jax.ShapeDtypeStruct((tokens, heads), F32),
            jax.ShapeDtypeStruct((heads, tokens), F32),
            jax.ShapeDtypeStruct((tokens, heads), F32),
            jax.ShapeDtypeStruct((ROW_TILE, heads), F32),
        ],
        compiler_params=params(),
        name="send_state",
    )(other, inputs, b_matrix, step_size, log_decay)

    swap = [(0, 1), (1, 0)]
    got = lax.ppermute(send, core_axis, swap)

    own = pl.pallas_call(
        functools.partial(own_state_kernel, dims=half_dims),
        grid_spec=pltpu.PrefetchScalarGridSpec(
            num_scalar_prefetch=1,
            grid=(per_half,),
            in_specs=[of_half(tokens), matrix_of_half(), whole((tokens, heads)), whole((ROW_TILE, heads))],
            out_specs=by_turn(tall),
            scratch_shapes=[spread_scratch],
        ),
        out_shape=jax.ShapeDtypeStruct((tall, half_cols), F32),
        compiler_params=params(),
        name="own_state",
    )(mine, inputs, b_matrix, factor, total)

    def row_block(cols):
        return pl.BlockSpec((ROW_BLOCK, cols), lambda i, _: (i, 0))

    def tail():
        return pl.BlockSpec((ROW_TILE, half_cols), lambda i, _: (states // ROW_TILE, 0))

    state_specs = [row_block(half_cols), tail(), row_block(half_cols), tail()]
    chip_total = pl.pallas_call(
        chip_total_kernel,
        grid_spec=pltpu.PrefetchScalarGridSpec(
            num_scalar_prefetch=1,
            grid=(states // ROW_BLOCK,),
            in_specs=state_specs + [whole((ROW_TILE, heads))],
            out_specs=row_block(half_cols + heads),
        ),
        out_shape=jax.ShapeDtypeStruct((states, half_cols + heads), BF16),
        compiler_params=params(),
        name="chip_total",
    )(mine, own, own, got, got, total)

    sent = lax.all_to_all(
        chip_total.reshape(chips, rows, half_cols + heads), chip_axes, split_axis=0, concat_axis=0, tiled=True
    )

    within = pl.pallas_call(
        functools.partial(within_kernel, dims=(per_group, width)),
        grid=(GROUPS,),
        in_specs=[
            pl.BlockSpec((tokens, group_cols), lambda i: (0, i)),
            pl.BlockSpec((tokens, states), lambda i: (0, i)),
            pl.BlockSpec((tokens, states), lambda i: (0, i)),
            whole((tokens, heads)),
            whole((tokens, heads)),
            whole((heads, tokens)),
            whole((1, heads)),
        ],
        out_specs=pl.BlockSpec((tokens, group_cols), lambda i: (0, i)),
        out_shape=jax.ShapeDtypeStruct((tokens, channels), F32),
        scratch_shapes=[spread_scratch],
        compiler_params=params(),
        name="within",
    )(inputs, b_matrix, c_matrix, step_size, run, run_t, skip_gain.reshape(1, heads))

    entering = pl.pallas_call(
        functools.partial(prefix_kernel, width=width),
        grid=(per_half,),
        in_specs=[
            pl.BlockSpec((chips, rows, group_cols), lambda i: (0, 0, i)),
            pl.BlockSpec((chips, rows, heads), lambda i: (0, 0, half_cols // heads)),
        ],
        out_specs=pl.BlockSpec((chips, rows, group_cols), lambda i: (0, 0, i)),
        out_shape=jax.ShapeDtypeStruct((chips, rows, half_cols), BF16),
        compiler_params=params(),
        name="prefix",
    )(sent, sent)
    entering = lax.all_to_all(entering, chip_axes, split_axis=0, concat_axis=0, tiled=True)
    entering = entering.reshape(states, half_cols)

    own_entering, send_entering = pl.pallas_call(
        incoming_kernel,
        grid_spec=pltpu.PrefetchScalarGridSpec(
            num_scalar_prefetch=1,
            grid=(states // ROW_BLOCK,),
            in_specs=state_specs + [row_block(half_cols)],
            out_specs=[row_block(half_cols)] * 2,
        ),
        out_shape=[jax.ShapeDtypeStruct((states, half_cols), BF16)] * 2,
        compiler_params=params(),
        name="incoming",
    )(mine, own, own, got, got, entering)
    got_entering = lax.ppermute(send_entering, core_axis, swap)

    def finish(half, state, *result):
        return pl.pallas_call(
            functools.partial(final_kernel, dims=half_dims),
            grid_spec=pltpu.PrefetchScalarGridSpec(
                num_scalar_prefetch=1,
                grid=(per_half,),
                in_specs=[of_half(tokens), matrix_of_half(), by_turn(states), whole((tokens, heads))]
                + [pl.BlockSpec(memory_space=pl.ANY)] * len(result),
                out_specs=of_half(tokens),
                scratch_shapes=[spread_scratch],
            ),
            out_shape=jax.ShapeDtypeStruct((tokens, channels), BF16),
            input_output_aliases={5: 0} if result else {},
            compiler_params=params(),
            name="finish",
        )(half, within, c_matrix, state, run, *result)

    result = finish(mine, own_entering)
    return finish(other, got_entering, result)


def solution(mesh):
    outer, inner = mesh.axis_names
    chip_mesh = Mesh(
        mesh.devices.reshape(mesh.shape[outer], mesh.shape[inner] // CORES, CORES), (outer, "chip", "core")
    )
    placed = P((outer, "chip", "core"), None)
    return jax.shard_map(
        functools.partial(local, chip_axes=(outer, "chip"), core_axis="core"),
        mesh=chip_mesh,
        in_specs=(placed,) * 5 + (P(),),
        out_specs=placed,
        check_vma=False,
    )
```

```python
import functools
import math

import jax
import jax.numpy as jnp
from jax import lax
from jax.experimental import pallas as pl
from jax.experimental.pallas import tpu as pltpu
from jax.sharding import Mesh, PartitionSpec as P

GROUPS = 8
CORES = 2
LANES = 128
ROW_TILE = 8
HALF_ROWS = 128
ROW_BLOCK = 16
VMEM_LIMIT = 24 * 1024 * 1024
LOG2E = 1.0 / math.log(2.0)

F32 = jnp.float32
BF16 = jnp.bfloat16


def dot(a, b, contract=(1, 0), precision=None):
    dims = (((contract[0],), (contract[1],)), ((), ()))
    return lax.dot_general(a, b, dims, precision=precision, preferred_element_type=F32)


def spreader(heads, width):
    shape = (2 * heads, heads * width)
    row = lax.broadcasted_iota(jnp.int32, shape, 0)
    col = lax.broadcasted_iota(jnp.int32, shape, 1)
    row = jnp.where(row >= heads, row - heads, row)
    return jnp.where(row == col // width, 1.0, 0.0).astype(BF16)


def high_low(values):
    high = values.astype(BF16).astype(F32)
    return high, values - high


def spread(values, matrix):
    heads = matrix.shape[0] // 2
    high, low = high_low(values)
    lane = lax.broadcasted_iota(jnp.int32, values.shape, 1)
    packed = jnp.where(lane < heads, high, pltpu.roll(low, heads, 1))
    return dot(packed.astype(BF16)[:, : 2 * heads], matrix)


def group_first(values, group, per_group):
    lanes = values.shape[1]
    return pltpu.roll(values, lax.rem(lanes - group * per_group, lanes), 1)


def params():
    return pltpu.CompilerParams(dimension_semantics=("arbitrary",), vmem_limit_bytes=VMEM_LIMIT)


def running_sums(step, log, run_out, run_t_out, factor_out, total_out):
    rows = log.shape[0]
    upto = lax.broadcasted_iota(jnp.int32, (rows, rows), 1) <= lax.broadcasted_iota(jnp.int32, (rows, rows), 0)
    running = dot(upto.astype(F32), log[...], precision=lax.Precision.HIGHEST) * LOG2E
    last = running[rows - 1 :, :]
    run_out[...] = running
    run_t_out[...] = running.T
    factor_out[...] = step[...] * jnp.exp2(last - running)
    total_out[...] = jnp.broadcast_to(last, total_out.shape)


def state_block(group, per_group, x, b, factor_ref, total_ref, matrix, out):
    factor = group_first(factor_ref[...], group, per_group)
    log_total = total_ref[...]
    decay = spread(jnp.exp2(group_first(log_total, group, per_group)), matrix)
    scaled = (x.astype(F32) * spread(factor, matrix)).astype(BF16)
    state = dot(b, scaled, (0, 0))
    out[: state.shape[0], :] = state.astype(BF16)
    row = lax.broadcasted_iota(jnp.int32, decay.shape, 0)
    heads = log_total.shape[1]
    high, low = high_low(decay)
    tail = jnp.where(row == 0, high, low)
    high, low = high_low(log_total)
    low_high, low_low = high_low(low)
    logs = jnp.where(row[:, :heads] == 2, high, jnp.where(row[:, :heads] == 3, low_high, low_low))
    logs = jnp.where(row[:, :heads] < 2, tail[:, :heads], logs)
    out[state.shape[0] :, :] = jnp.concatenate([logs, tail[:, heads:]], axis=1).astype(BF16)


def send_state_kernel(half, x, b, step, log, out, run_out, run_t_out, factor_out, total_out, matrix, *, dims):
    per_half, per_group, width = dims
    turn = pl.program_id(0)

    @pl.when(turn == 0)
    def _():
        running_sums(step, log, run_out, run_t_out, factor_out, total_out)
        matrix[...] = spreader(per_group, width)

    group = half[0] * per_half + turn
    state_block(group, per_group, x[...], b[...], factor_out, total_out, matrix[...], out)


def own_state_kernel(half, x, b, factor, total, out, matrix, *, dims):
    per_half, per_group, width = dims
    turn = pl.program_id(0)

    @pl.when(turn == 0)
    def _():
        matrix[...] = spreader(per_group, width)

    group = half[0] * per_half + turn
    state_block(group, per_group, x[...], b[...], factor, total, matrix[...], out)


def other_log(got, states, heads):
    return (
        got[states + 2 : states + 3, :heads].astype(F32)
        + got[states + 3 : states + 4, :heads].astype(F32)
        + got[states + 4 : states + 5, :heads].astype(F32)
    )


def chip_total_kernel(core, own, got, total, out, base_out):
    first = core[0] == 0
    cols = own.shape[1]
    states = out.shape[0]
    heads = total.shape[1]
    half = heads // CORES
    own_tail = own[states : states + 2, :].astype(F32)
    got_tail = got[states : states + 2, :].astype(F32)
    decay = jnp.where(first, got_tail, own_tail)
    decay = decay[:1, :] + decay[1:, :]
    one = jnp.ones_like(decay)
    on_own = jnp.where(first, decay, one)
    on_got = jnp.where(first, one, decay)
    for row in range(0, states, ROW_BLOCK):
        rows = slice(row, row + ROW_BLOCK)
        out[rows, :cols] = (on_own * own[rows, :].astype(F32) + on_got * got[rows, :].astype(F32)).astype(BF16)
    partner = jnp.broadcast_to(other_log(got, states, heads), total.shape)
    base_out[...] = jnp.where(first, jnp.zeros_like(partner), partner)
    both = jnp.exp2(total[...] + partner)
    both = jnp.where(first, both, pltpu.roll(both, half, 1))
    high, low = high_low(both)
    lane = lax.broadcasted_iota(jnp.int32, both.shape, 1)
    packed = jnp.where(lane < half, high, pltpu.roll(low, half, 1))
    out[:, cols:] = jnp.concatenate([packed] * (states // packed.shape[0]), axis=0).astype(BF16)


def prefix_kernel(sent, ready, out, *, width, group_cols):
    del ready
    chips, rows, cols = out.shape
    heads_here = group_cols // width
    half = (sent.shape[2] - cols) // 2
    first_rows = jnp.concatenate([sent[k, :1, cols:].astype(F32) for k in range(chips)], axis=0)
    values = first_rows + pltpu.roll(first_rows, half, 1)
    matrix = spreader(heads_here, width)
    for start in range(0, cols, group_cols):
        here = slice(start, start + group_cols)
        shift = (2 * half - start // width) % (2 * half)
        decay = spread(pltpu.roll(values, shift, 1) if shift else values, matrix)
        state = jnp.zeros((rows, group_cols), F32)
        for k in range(chips):
            out[k, :, here] = state.astype(BF16)
            state = decay[k : k + 1, :] * state + sent[k, :, here].astype(F32)


def within_kernel(
    core, x_ref, b_ref, c_ref, step_ref, run_ref, run_t_ref, skip_ref, low_ref, high_ref, out, ready, matrix, *, dims
):
    per_half, per_group, width = dims
    group = pl.program_id(0)
    rows = x_ref.shape[0]

    @pl.when(group == 0)
    def _():
        matrix[...] = spreader(per_group, width)
        ready[...] = jnp.zeros_like(ready)

    spreading = matrix[...]
    step = group_first(step_ref[...], group, per_group)
    run = group_first(run_ref[...], group, per_group)
    skip = group_first(jnp.broadcast_to(skip_ref[...], (ROW_TILE, skip_ref.shape[1])), group, per_group)
    run_t = run_t_ref[pl.ds(pl.multiple_of(group * per_group, per_group), per_group), :]
    x = x_ref[...].astype(F32)
    scaled = (x * spread(step, spreading)).astype(BF16)
    skipped = spread(skip, spreading)[:1, :] * x
    upper = high_ref[...] * core[0].astype(BF16)
    before_state = jnp.where(group < per_half, low_ref[...], upper)
    skipped = skipped + spread(jnp.exp2(run), spreading) * dot(c_ref[...], before_state)
    pair = LANES // width
    lane = lax.broadcasted_iota(jnp.int32, (HALF_ROWS, LANES), 1) // width
    lower = lax.broadcasted_iota(jnp.int32, (HALF_ROWS, HALF_ROWS), 1) <= lax.broadcasted_iota(
        jnp.int32, (HALF_ROWS, HALF_ROWS), 0
    )
    b = b_ref[...]
    c = c_ref[...]
    for start in range(0, rows, HALF_ROWS):
        stop = start + HALF_ROWS
        scores = jnp.where(lower, dot(c[start:stop, :], b[start:stop, :], (1, 1)), 0.0)
        if start:
            edge = run[start - 1 : start, :]
            before = step[:start, :] * jnp.exp2(edge - run[:start, :])
            before = (x[:start, :] * spread(before, spreading)).astype(BF16)
            cross = dot(c[start:stop, :], b[:start, :], (1, 1)).astype(BF16)
            after = spread(jnp.exp2(run[start:stop, :] - edge), spreading)
            base = skipped[start:stop, :] + after * dot(cross, before)
        else:
            base = skipped[start:stop, :]
        for first in range(0, per_group, pair):
            cols = slice(first * width, (first + pair) * width)
            here = scaled[start:stop, cols]
            weights = []
            values = []
            for k in range(pair):
                head = first + k
                gap = run[start:stop, head : head + 1] - run_t[head : head + 1, start:stop]
                weights.append((scores * jnp.exp2(jnp.minimum(gap, 0.0))).astype(BF16))
                values.append(jnp.where(lane == k, here, jnp.zeros_like(here)))
            part = dot(jnp.concatenate(weights, axis=1), jnp.concatenate(values, axis=0))
            out[start:stop, cols] = base[:, cols] + part


def final_kernel(half, within, c, state, run_ref, base_ref, *rest, dims):
    per_half, per_group, width = dims
    out, matrix = rest[-2:]
    turn = pl.program_id(0)

    @pl.when(turn == 0)
    def _():
        matrix[...] = spreader(per_group, width)

    group = half[0] * per_half + turn
    grown = jnp.exp2(group_first(run_ref[...] + base_ref[:1, :], group, per_group))
    out[...] = (within[...] + spread(grown, matrix[...]) * dot(c[...], state[...])).astype(BF16)


def local(inputs, step_size, log_decay, b_matrix, c_matrix, skip_gain, *, chip_axes, core_axis):
    tokens, channels = inputs.shape
    heads = step_size.shape[1]
    width = channels // heads
    states = b_matrix.shape[1] // GROUPS
    per_group = heads // GROUPS
    group_cols = per_group * width
    per_half = GROUPS // CORES
    half_cols = channels // CORES
    half_heads = heads // CORES
    chips = lax.axis_size(chip_axes)
    rows = states // chips
    tall = states + ROW_TILE

    core = lax.axis_index(core_axis).astype(jnp.int32)
    mine = core.reshape(1)
    other = (1 - core).reshape(1)

    def of_half(block_rows):
        return pl.BlockSpec((block_rows, group_cols), lambda i, half: (0, half[0] * per_half + i))

    def matrix_of_half():
        return pl.BlockSpec((tokens, states), lambda i, half: (0, half[0] * per_half + i))

    def by_turn(block_rows):
        return pl.BlockSpec((block_rows, group_cols), lambda i, half: (0, i))

    def whole(shape):
        return pl.BlockSpec(shape, lambda i, *_: (0,) * len(shape))

    spread_scratch = pltpu.VMEM((2 * per_group, group_cols), BF16)
    half_dims = (per_half, per_group, width)

    send, run, run_t, factor, total = pl.pallas_call(
        functools.partial(send_state_kernel, dims=half_dims),
        grid_spec=pltpu.PrefetchScalarGridSpec(
            num_scalar_prefetch=1,
            grid=(per_half,),
            in_specs=[of_half(tokens), matrix_of_half(), whole((tokens, heads)), whole((tokens, heads))],
            out_specs=[
                by_turn(tall),
                whole((tokens, heads)),
                whole((heads, tokens)),
                whole((tokens, heads)),
                whole((ROW_TILE, heads)),
            ],
            scratch_shapes=[spread_scratch],
        ),
        out_shape=[
            jax.ShapeDtypeStruct((tall, half_cols), BF16),
            jax.ShapeDtypeStruct((tokens, heads), F32),
            jax.ShapeDtypeStruct((heads, tokens), F32),
            jax.ShapeDtypeStruct((tokens, heads), F32),
            jax.ShapeDtypeStruct((ROW_TILE, heads), F32),
        ],
        compiler_params=params(),
        name="send_state",
    )(other, inputs, b_matrix, step_size, log_decay)

    swap = [(0, 1), (1, 0)]
    got = lax.ppermute(send, core_axis, swap)

    own = pl.pallas_call(
        functools.partial(own_state_kernel, dims=half_dims),
        grid_spec=pltpu.PrefetchScalarGridSpec(
            num_scalar_prefetch=1,
            grid=(per_half,),
            in_specs=[of_half(tokens), matrix_of_half(), whole((tokens, heads)), whole((ROW_TILE, heads))],
            out_specs=by_turn(tall),
            scratch_shapes=[spread_scratch],
        ),
        out_shape=jax.ShapeDtypeStruct((tall, half_cols), BF16),
        compiler_params=params(),
        name="own_state",
    )(mine, inputs, b_matrix, factor, total)

    smem = pl.BlockSpec(memory_space=pltpu.SMEM)
    vmem = pl.BlockSpec(memory_space=pltpu.VMEM)
    anywhere = pl.BlockSpec(memory_space=pl.ANY)
    chip_total, base = pl.pallas_call(
        chip_total_kernel,
        in_specs=[smem, vmem, vmem, vmem],
        out_specs=[vmem, vmem],
        out_shape=[
            jax.ShapeDtypeStruct((states, half_cols + heads), BF16),
            jax.ShapeDtypeStruct((ROW_TILE, heads), F32),
        ],
        compiler_params=pltpu.CompilerParams(vmem_limit_bytes=VMEM_LIMIT),
        name="chip_total",
    )(mine, own, got, total)

    sent = lax.all_to_all(
        chip_total.reshape(chips, rows, half_cols + heads), chip_axes, split_axis=0, concat_axis=0, tiled=True
    )
    late = lax.ppermute(own, core_axis, swap[:1])

    def by_group(block_rows, cols):
        return pl.BlockSpec((block_rows, cols), lambda i, *_: (0, i))

    within, ready = pl.pallas_call(
        functools.partial(within_kernel, dims=half_dims),
        grid_spec=pltpu.PrefetchScalarGridSpec(
            num_scalar_prefetch=1,
            grid=(GROUPS,),
            in_specs=[
                by_group(tokens, group_cols),
                by_group(tokens, states),
                by_group(tokens, states),
                whole((tokens, heads)),
                whole((tokens, heads)),
                whole((heads, tokens)),
                whole((1, heads)),
                pl.BlockSpec((states, group_cols), lambda i, _: (0, jnp.minimum(i, per_half - 1))),
                pl.BlockSpec((states, group_cols), lambda i, _: (0, jnp.maximum(i - per_half, 0))),
            ],
            out_specs=[by_group(tokens, group_cols), whole((ROW_TILE, LANES))],
            scratch_shapes=[spread_scratch],
        ),
        out_shape=[jax.ShapeDtypeStruct((tokens, channels), F32), jax.ShapeDtypeStruct((ROW_TILE, LANES), F32)],
        compiler_params=params(),
        name="within",
    )(mine, inputs, b_matrix, c_matrix, step_size, run, run_t, skip_gain.reshape(1, heads), late, got)

    entering = pl.pallas_call(
        functools.partial(prefix_kernel, width=width, group_cols=group_cols),
        in_specs=[vmem, anywhere],
        out_specs=vmem,
        out_shape=jax.ShapeDtypeStruct((chips, rows, half_cols), BF16),
        compiler_params=pltpu.CompilerParams(vmem_limit_bytes=VMEM_LIMIT),
        name="prefix",
    )(sent, ready)
    entering = lax.all_to_all(entering, chip_axes, split_axis=0, concat_axis=0, tiled=True)
    entering = entering.reshape(states, half_cols)
    got_entering = lax.ppermute(entering, core_axis, swap)

    def finish(half, state, *result):
        return pl.pallas_call(
            functools.partial(final_kernel, dims=half_dims),
            grid_spec=pltpu.PrefetchScalarGridSpec(
                num_scalar_prefetch=1,
                grid=(per_half,),
                in_specs=[
                    of_half(tokens),
                    matrix_of_half(),
                    by_turn(states),
                    whole((tokens, heads)),
                    whole((ROW_TILE, heads)),
                ]
                + [anywhere] * len(result),
                out_specs=of_half(tokens),
                scratch_shapes=[spread_scratch],
            ),
            out_shape=jax.ShapeDtypeStruct((tokens, channels), BF16),
            input_output_aliases={6: 0} if result else {},
            compiler_params=params(),
            name="finish",
        )(half, within, c_matrix, state, run, base, *result)

    result = finish(mine, entering)
    return finish(other, got_entering, result)


def solution(mesh):
    outer, inner = mesh.axis_names
    chip_mesh = Mesh(
        mesh.devices.reshape(mesh.shape[outer], mesh.shape[inner] // CORES, CORES), (outer, "chip", "core")
    )
    placed = P((outer, "chip", "core"), None)
    return jax.shard_map(
        functools.partial(local, chip_axes=(outer, "chip"), core_axis="core"),
        mesh=chip_mesh,
        in_specs=(placed,) * 5 + (P(),),
        out_specs=placed,
        check_vma=False,
    )
```

```python
import functools
import math

import jax
import jax.numpy as jnp
from jax import lax
from jax.experimental import pallas as pl
from jax.experimental.pallas import tpu as pltpu
from jax.sharding import Mesh, PartitionSpec as P


GROUPS = 8
CORES = 2
LANES = 128
ROW_TILE = 8
HALF_ROWS = 128
ROW_BLOCK = 16
VMEM_LIMIT = 24 * 1024 * 1024
LOG2E = 1.0 / math.log(2.0)

F32 = jnp.float32
BF16 = jnp.bfloat16


def dot(a, b, contract=(1, 0)):
    dims = (((contract[0],), (contract[1],)), ((), ()))
    return lax.dot_general(a, b, dims, preferred_element_type=F32)


def high_low(values):
    high = values.astype(BF16).astype(F32)
    return high, values - high


def head_lanes(values, first_head, width):
    lane = lax.broadcasted_iota(jnp.int32, (values.shape[0], LANES), 1)
    return jnp.take_along_axis(values, first_head + lane // width, axis=1)


def spread(values, first_head, heads, width):
    pair = LANES // width
    return jnp.concatenate([head_lanes(values, first_head + k, width) for k in range(0, heads, pair)], axis=1)


def params():
    return pltpu.CompilerParams(dimension_semantics=("arbitrary",), vmem_limit_bytes=VMEM_LIMIT)


def plain_params():
    return pltpu.CompilerParams(vmem_limit_bytes=VMEM_LIMIT)


def state_copies(half, x, b, x_here, b_here, sems, dims):
    per_half, group_cols, states = dims
    copies = []
    for k in range(per_half):
        group = half * per_half + k
        copies.append(
            pltpu.make_async_copy(
                x.at[:, pl.ds(pl.multiple_of(group * group_cols, group_cols), group_cols)],
                x_here.at[:, pl.ds(k * group_cols, group_cols)],
                sems.at[2 * k],
            )
        )
        copies.append(
            pltpu.make_async_copy(
                b.at[:, pl.ds(pl.multiple_of(group * states, states), states)],
                b_here.at[:, pl.ds(k * states, states)],
                sems.at[2 * k + 1],
            )
        )
    return copies


def half_states(half, x_here, b_here, copies, factor, log_total, out, dims):
    per_half, group_cols, states = dims
    heads = factor.shape[1]
    half_heads = heads // CORES
    per_group = half_heads // per_half
    width = group_cols // per_group
    first = half * half_heads
    row = lax.broadcasted_iota(jnp.int32, (ROW_TILE, LANES), 0)
    high, low = high_low(log_total)
    middle, low = high_low(low)
    logs = jnp.where(row == 2, high, jnp.where(row == 3, middle, low))
    total = jnp.exp2(log_total)
    for k in range(per_half):
        copies[2 * k].wait()
        copies[2 * k + 1].wait()
        b = b_here[:, k * states : (k + 1) * states]
        scaled = []
        for j in range(0, group_cols, LANES):
            start = k * group_cols + j
            part = head_lanes(factor, first + start // width, width)
            scaled.append((x_here[:, start : start + LANES].astype(F32) * part).astype(BF16))
            high, low = high_low(head_lanes(total, first + start // width, width))
            tail = jnp.where(row == 0, high, low)
            if start == 0:
                tail = jnp.where(row < 2, tail, logs)
            out[states:, start : start + LANES] = tail.astype(BF16)
        cols = slice(k * group_cols, (k + 1) * group_cols)
        out[:states, cols] = dot(b, jnp.concatenate(scaled, axis=1), (0, 0)).astype(BF16)


def send_state_kernel(
    half, x, b, step, log, out, run_out, run_t_out, factor_out, total_out, x_here, b_here, step_here, log_here, sems, *, dims
):
    first = pltpu.make_async_copy(log, log_here, sems.at[2 * dims[0]])
    second = pltpu.make_async_copy(step, step_here, sems.at[2 * dims[0] + 1])
    first.start()
    second.start()
    copies = state_copies(half[0], x, b, x_here, b_here, sems, dims)
    for copy in copies:
        copy.start()
    rows, heads = log_here.shape
    upto = lax.broadcasted_iota(jnp.int32, (rows, rows), 1) <= lax.broadcasted_iota(jnp.int32, (rows, rows), 0)
    first.wait()
    high, rest = high_low(log_here[...])
    middle, low = high_low(rest)
    parts = jnp.concatenate([high, middle, low], axis=1).astype(BF16)
    sums = dot(jnp.where(upto, 1.0, 0.0).astype(BF16), parts)
    running = (sums[:, :heads] + sums[:, heads : 2 * heads] + sums[:, 2 * heads :]) * LOG2E
    last = running[rows - 1 :, :]
    run_out[...] = running
    run_t_out[...] = running.T
    second.wait()
    factor = step_here[...] * jnp.exp2(last - running)
    total = jnp.broadcast_to(last, total_out.shape)
    factor_out[...] = factor
    total_out[...] = total
    half_states(half[0], x_here, b_here, copies, factor, total, out, dims)


def own_state_kernel(half, x, b, factor, total, out, x_here, b_here, sems, *, dims):
    copies = state_copies(half[0], x, b, x_here, b_here, sems, dims)
    for copy in copies:
        copy.start()
    half_states(half[0], x_here, b_here, copies, factor[...], total[...], out, dims)


def chip_total_kernel(core, own, got, total, out, base_out):
    first = core[0] == 0
    cols = own.shape[1]
    states = out.shape[0]
    heads = total.shape[1]
    half = heads // CORES
    own_tail = own[states : states + 2, :].astype(F32)
    got_tail = got[states : states + 2, :].astype(F32)
    decay = jnp.where(first, got_tail, own_tail)
    decay = decay[:1, :] + decay[1:, :]
    one = jnp.ones_like(decay)
    on_own = jnp.where(first, decay, one)
    on_got = jnp.where(first, one, decay)
    for row in range(0, states, ROW_BLOCK):
        rows = slice(row, row + ROW_BLOCK)
        out[rows, :cols] = (on_own * own[rows, :].astype(F32) + on_got * got[rows, :].astype(F32)).astype(BF16)
    partner = got[states + 2 : states + 3, :heads].astype(F32) + got[states + 3 : states + 4, :heads].astype(F32)
    partner = partner + got[states + 4 : states + 5, :heads].astype(F32)
    partner = jnp.broadcast_to(partner, total.shape)
    base_out[...] = jnp.where(first, jnp.zeros_like(partner), partner)
    both = jnp.exp2(total[...] + partner)
    both = jnp.where(first, both, pltpu.roll(both, half, 1))
    high, low = high_low(both)
    lane = lax.broadcasted_iota(jnp.int32, both.shape, 1)
    packed = jnp.where(lane < half, high, pltpu.roll(low, half, 1))
    out[:, cols:] = jnp.concatenate([packed] * (states // packed.shape[0]), axis=0).astype(BF16)


def prefix_kernel(sent, out, ready, here, sems, *, width, blocks):
    chips, rows, cols = here.shape
    heads = ready.shape[1]
    half = heads // CORES
    step = cols // blocks
    ready[...] = jnp.zeros_like(ready)
    first_rows = jnp.concatenate([sent[k, :1, cols:].astype(F32) for k in range(chips)], axis=0)
    values = first_rows + pltpu.roll(first_rows, half, 1)
    copies = []
    for block in range(blocks):
        lanes = slice(block * step, (block + 1) * step)
        decay = spread(values, block * step // width, step // width, width)
        state = jnp.zeros((rows, step), F32)
        for k in range(chips):
            here[k, :, lanes] = state.astype(BF16)
            state = decay[k : k + 1, :] * state + sent[k, :, lanes].astype(F32)
        copies.append(
            pltpu.make_async_copy(
                here.at[:, :, pl.ds(block * step, step)], out.at[:, :, pl.ds(block * step, step)], sems.at[block]
            )
        )
        copies[-1].start()
    for copy in copies:
        copy.wait()


def within_kernel(
    core, x_ref, b_ref, c_ref, step_ref, run_ref, run_t_ref, skip_ref, low_ref, high_ref, ready, out, *, dims
):
    del ready
    per_half, per_group, width = dims
    group = pl.program_id(0)
    head = group * per_group
    rows = x_ref.shape[0]
    pair = LANES // width
    run = run_ref[...]
    own_run = pltpu.roll(run, lax.rem(run.shape[1] - head, run.shape[1]), 1)
    run_t = run_t_ref[pl.ds(pl.multiple_of(head, per_group), per_group), :]
    step = step_ref[...]
    skip = jnp.broadcast_to(skip_ref[...], (ROW_TILE, skip_ref.shape[1]))
    grown = jnp.exp2(run)
    upper = high_ref[...] * core[0].astype(BF16)
    from_before = dot(c_ref[...], jnp.where(group < per_half, low_ref[...], upper))
    lane = lax.broadcasted_iota(jnp.int32, (HALF_ROWS, LANES), 1) // width
    lower = lax.broadcasted_iota(jnp.int32, (HALF_ROWS, HALF_ROWS), 1) <= lax.broadcasted_iota(
        jnp.int32, (HALF_ROWS, HALF_ROWS), 0
    )
    b = b_ref[...]
    c = c_ref[...]
    for start in range(0, rows, HALF_ROWS):
        stop = start + HALF_ROWS
        scores = jnp.where(lower, dot(c[start:stop, :], b[start:stop, :], (1, 1)), 0.0)
        if start:
            edge = run[start - 1 : start, :]
            lead = spread(step[:start, :] * jnp.exp2(edge - run[:start, :]), head, per_group, width)
            lead = (x_ref[:start, :].astype(F32) * lead).astype(BF16)
            cross = dot(dot(c[start:stop, :], b[:start, :], (1, 1)).astype(BF16), lead)
            after = jnp.exp2(run[start:stop, :] - edge)
        for first in range(0, per_group, pair):
            cols = slice(first * width, (first + pair) * width)
            x = x_ref[start:stop, cols].astype(F32)
            here = (x * head_lanes(step[start:stop, :], head + first, width)).astype(BF16)
            weights = []
            values = []
            for k in range(pair):
                at = first + k
                gap = own_run[start:stop, at : at + 1] - run_t[at : at + 1, start:stop]
                weights.append((scores * jnp.exp2(jnp.minimum(gap, 0.0))).astype(BF16))
                values.append(jnp.where(lane == k, here, jnp.zeros_like(here)))
            part = dot(jnp.concatenate(weights, axis=1), jnp.concatenate(values, axis=0))
            part = part + head_lanes(skip, head + first, width)[:1, :] * x
            part = part + head_lanes(grown[start:stop, :], head + first, width) * from_before[start:stop, cols]
            if start:
                part = part + head_lanes(after, head + first, width) * cross[:, cols]
            out[start:stop, cols] = part.astype(BF16)


def final_kernel(half, within, c, state, run_ref, base_ref, *rest, dims):
    per_half, per_group, width = dims
    out = rest[-1]
    turn = pl.program_id(0)
    head = (half[0] * per_half + turn) * per_group
    grown = jnp.exp2(run_ref[...] + base_ref[:1, :])
    rows = c[...]
    tile = 2 * LANES
    for start in range(0, out.shape[1], tile):
        carried = dot(rows, state[:, pl.ds(pl.multiple_of(turn * out.shape[1] + start, tile), tile)])
        for j in range(0, tile, LANES):
            cols = slice(start + j, start + j + LANES)
            factor = head_lanes(grown, head + (start + j) // width, width)
            out[:, cols] = (within[:, cols].astype(F32) + factor * carried[:, j : j + LANES]).astype(BF16)


def local(inputs, step_size, log_decay, b_matrix, c_matrix, skip_gain, *, chip_axes, core_axis):
    tokens, channels = inputs.shape
    heads = step_size.shape[1]
    width = channels // heads
    states = b_matrix.shape[1] // GROUPS
    per_group = heads // GROUPS
    group_cols = per_group * width
    per_half = GROUPS // CORES
    half_cols = channels // CORES
    chips = lax.axis_size(chip_axes)
    rows = states // chips
    tall = states + ROW_TILE

    core = lax.axis_index(core_axis).astype(jnp.int32)
    mine = core.reshape(1)
    other = (1 - core).reshape(1)

    smem = pl.BlockSpec(memory_space=pltpu.SMEM)
    vmem = pl.BlockSpec(memory_space=pltpu.VMEM)
    hbm = pl.BlockSpec(memory_space=pltpu.HBM)
    anywhere = pl.BlockSpec(memory_space=pl.ANY)

    def whole(shape):
        return pl.BlockSpec(shape, lambda i, *_: (0,) * len(shape))

    def by_group(cols):
        return pl.BlockSpec((tokens, cols), lambda i, *_: (0, i))

    def of_half(cols):
        return pl.BlockSpec((tokens, cols), lambda i, half: (0, half[0] * per_half + i))

    state_dims = (per_half, group_cols, states)
    half_dims = (per_half, per_group, width)
    half_scratch = [pltpu.VMEM((tokens, half_cols), BF16), pltpu.VMEM((tokens, per_half * states), BF16)]

    inputs, step_size, log_decay, b_matrix, c_matrix = (
        pltpu.with_memory_space_constraint(array, pltpu.HBM)
        for array in (inputs, step_size, log_decay, b_matrix, c_matrix)
    )
    send, run, run_t, factor, total = pl.pallas_call(
        functools.partial(send_state_kernel, dims=state_dims),
        in_specs=[smem, hbm, hbm, hbm, hbm],
        out_specs=[vmem] * 5,
        out_shape=[
            jax.ShapeDtypeStruct((tall, half_cols), BF16),
            jax.ShapeDtypeStruct((tokens, heads), F32),
            jax.ShapeDtypeStruct((heads, tokens), F32),
            jax.ShapeDtypeStruct((tokens, heads), F32),
            jax.ShapeDtypeStruct((ROW_TILE, heads), F32),
        ],
        scratch_shapes=half_scratch
        + [pltpu.VMEM((tokens, heads), F32)] * 2
        + [pltpu.SemaphoreType.DMA((2 * per_half + 2,))],
        compiler_params=plain_params(),
        name="send_state",
    )(other, inputs, b_matrix, step_size, log_decay)

    swap = [(0, 1), (1, 0)]
    got = lax.ppermute(send, core_axis, swap)

    own = pl.pallas_call(
        functools.partial(own_state_kernel, dims=state_dims),
        in_specs=[smem, hbm, hbm, vmem, vmem],
        out_specs=vmem,
        out_shape=jax.ShapeDtypeStruct((tall, half_cols), BF16),
        scratch_shapes=half_scratch + [pltpu.SemaphoreType.DMA((2 * per_half,))],
        compiler_params=plain_params(),
        name="own_state",
    )(mine, inputs, b_matrix, factor, total)

    chip_total, base = pl.pallas_call(
        chip_total_kernel,
        in_specs=[smem, vmem, vmem, vmem],
        out_specs=[vmem, vmem],
        out_shape=[
            jax.ShapeDtypeStruct((states, half_cols + heads), BF16),
            jax.ShapeDtypeStruct((ROW_TILE, heads), F32),
        ],
        compiler_params=plain_params(),
        name="chip_total",
    )(mine, own, got, total)

    sent = lax.all_to_all(
        chip_total.reshape(chips, rows, half_cols + heads), chip_axes, split_axis=0, concat_axis=0, tiled=True
    )
    late = lax.ppermute(own, core_axis, swap[:1])

    entering, ready = pl.pallas_call(
        functools.partial(prefix_kernel, width=width, blocks=per_half),
        in_specs=[vmem],
        out_specs=[hbm, vmem],
        out_shape=[
            jax.ShapeDtypeStruct((chips, rows, half_cols), BF16),
            jax.ShapeDtypeStruct((ROW_TILE, heads), F32),
        ],
        scratch_shapes=[pltpu.VMEM((chips, rows, half_cols), BF16), pltpu.SemaphoreType.DMA((per_half,))],
        compiler_params=plain_params(),
        name="prefix",
    )(sent)
    entering = lax.all_to_all(entering, chip_axes, split_axis=0, concat_axis=0, tiled=True)

    within = pl.pallas_call(
        functools.partial(within_kernel, dims=half_dims),
        grid_spec=pltpu.PrefetchScalarGridSpec(
            num_scalar_prefetch=1,
            grid=(GROUPS,),
            in_specs=[
                by_group(group_cols),
                by_group(states),
                by_group(states),
                whole((tokens, heads)),
                whole((tokens, heads)),
                whole((heads, tokens)),
                whole((1, heads)),
                pl.BlockSpec((states, group_cols), lambda i, _: (0, jnp.minimum(i, per_half - 1))),
                pl.BlockSpec((states, group_cols), lambda i, _: (0, jnp.maximum(i - per_half, 0))),
                anywhere,
            ],
            out_specs=by_group(group_cols),
        ),
        out_shape=jax.ShapeDtypeStruct((tokens, channels), BF16),
        compiler_params=params(),
        name="within",
    )(mine, inputs, b_matrix, c_matrix, step_size, run, run_t, skip_gain.reshape(1, heads), late, got, ready)

    within = pltpu.with_memory_space_constraint(within, pltpu.HBM)
    entering = entering.reshape(states, half_cols)
    got_entering = lax.ppermute(entering, core_axis, swap)

    def finish(half, state, *result):
        return pl.pallas_call(
            functools.partial(final_kernel, dims=half_dims),
            grid_spec=pltpu.PrefetchScalarGridSpec(
                num_scalar_prefetch=1,
                grid=(per_half,),
                in_specs=[
                    of_half(group_cols),
                    of_half(states),
                    vmem,
                    vmem,
                    vmem,
                ]
                + [anywhere] * len(result),
                out_specs=of_half(group_cols),
            ),
            out_shape=jax.ShapeDtypeStruct((tokens, channels), BF16),
            input_output_aliases={6: 0} if result else {},
            compiler_params=params(),
            name="finish",
        )(half, within, c_matrix, state, run, base, *result)

    result = finish(mine, entering)
    return finish(other, got_entering, result)


def solution(mesh):
    outer, inner = mesh.axis_names
    chip_mesh = Mesh(
        mesh.devices.reshape(mesh.shape[outer], mesh.shape[inner] // CORES, CORES), (outer, "chip", "core")
    )
    placed = P((outer, "chip", "core"), None)

    def body(*args):
        return local(*args, chip_axes=(outer, "chip"), core_axis="core")

    return jax.shard_map(body, mesh=chip_mesh, in_specs=(placed,) * 5 + (P(),), out_specs=placed, check_vma=False)
```

```python
import functools
import math

import jax
import jax.numpy as jnp
from jax import lax
from jax.experimental import pallas as pl
from jax.experimental.pallas import tpu as pltpu
from jax.sharding import Mesh, PartitionSpec as P


GROUPS = 8
CORES = 2
LANES = 128
TILE = 256
AHEAD = 2
ROW_TILE = 8
HALF_ROWS = 128
ROW_BLOCK = 16
VMEM_LIMIT = 24 * 1024 * 1024
LOG2E = 1.0 / math.log(2.0)

F32 = jnp.float32
BF16 = jnp.bfloat16


def dot(a, b, contract=(1, 0)):
    dims = (((contract[0],), (contract[1],)), ((), ()))
    return lax.dot_general(a, b, dims, preferred_element_type=F32)


def high_low(values):
    high = values.astype(BF16).astype(F32)
    return high, values - high


def spreader(heads, width):
    shape = (2 * heads, heads * width)
    row = lax.broadcasted_iota(jnp.int32, shape, 0)
    col = lax.broadcasted_iota(jnp.int32, shape, 1)
    row = jnp.where(row >= heads, row - heads, row)
    return jnp.where(row == col // width, 1.0, 0.0).astype(BF16)


def group_first(values, head):
    lanes = values.shape[1]
    return pltpu.roll(values, lax.rem(lanes - head, lanes), 1)


def packed(values, heads):
    high, low = high_low(values)
    lane = lax.broadcasted_iota(jnp.int32, values.shape, 1)
    return jnp.where(lane < heads, high, pltpu.roll(low, heads, 1)).astype(BF16)[:, : 2 * heads]


def half_spreader(matrix, width):
    lanes, cols = matrix.shape
    for start in range(0, cols, TILE):
        row = lax.broadcasted_iota(jnp.int32, (lanes, TILE), 0)
        col = start + lax.broadcasted_iota(jnp.int32, (lanes, TILE), 1)
        row = jnp.where(row >= lanes // 2, row - lanes // 2, row)
        matrix[:, start : start + TILE] = jnp.where(row == col // width, 1.0, 0.0).astype(BF16)


def packed_half(values, half):
    lanes = values.shape[1]
    values = group_first(values, half * (lanes // 2))
    high, low = high_low(values)
    lane = lax.broadcasted_iota(jnp.int32, values.shape, 1)
    return jnp.where(lane < lanes // 2, high, pltpu.roll(low, lanes // 2, 1)).astype(BF16)


def params():
    return pltpu.CompilerParams(dimension_semantics=("arbitrary",), vmem_limit_bytes=VMEM_LIMIT)


def plain_params():
    return pltpu.CompilerParams(vmem_limit_bytes=VMEM_LIMIT)


def state_copies(half, x, b, x_here, b_here, sems, dims):
    per_half, group_cols, states = dims
    copies = []
    for k in range(per_half):
        group = half * per_half + k
        copies.append(
            pltpu.make_async_copy(
                x.at[:, pl.ds(pl.multiple_of(group * group_cols, group_cols), group_cols)],
                x_here.at[:, pl.ds(k * group_cols, group_cols)],
                sems.at[2 * k],
            )
        )
        copies.append(
            pltpu.make_async_copy(
                b.at[:, pl.ds(pl.multiple_of(group * states, states), states)],
                b_here.at[:, pl.ds(k * states, states)],
                sems.at[2 * k + 1],
            )
        )
    return copies


def half_states(half, x_here, b_here, copies, factor, log_total, out, matrix, dims):
    _, group_cols, states = dims
    rows, heads = factor.shape
    row = lax.broadcasted_iota(jnp.int32, (ROW_TILE, TILE), 0)
    operand = packed_half(jnp.concatenate([factor, jnp.exp2(log_total)], axis=0), half)
    for copy in copies:
        copy.wait()
    tiles = out.shape[1] // TILE
    per_group = group_cols // TILE
    matrices = {}
    factors = {}
    scaled = {}
    for n in range(tiles + 2 * AHEAD):
        if n < tiles:
            factors[n] = dot(operand, matrix[:, n * TILE : (n + 1) * TILE])
        m = n - AHEAD
        if 0 <= m < tiles:
            cols = slice(m * TILE, (m + 1) * TILE)
            spread = factors.pop(m)
            scaled[m] = (x_here[:, cols].astype(F32) * spread[:rows, :]).astype(BF16)
            high, low = high_low(spread[rows:, :])
            tail = jnp.where(row == 0, high, low)
            if m == 0:
                high, low = high_low(log_total)
                middle, low = high_low(low)
                at = row[:, :heads]
                logs = jnp.where(at == 2, high, jnp.where(at == 3, middle, low))
                logs = jnp.where(at < 2, tail[:, :heads], logs)
                tail = jnp.concatenate([logs, tail[:, heads:]], axis=1)
            out[states:, cols] = tail.astype(BF16)
            if m % per_group == 0:
                k = m // per_group
                matrices[k] = b_here[:, k * states : (k + 1) * states].T
        m = n - 2 * AHEAD
        if m >= 0:
            out[:states, m * TILE : (m + 1) * TILE] = dot(matrices[m // per_group], scaled.pop(m)).astype(BF16)


def send_state_kernel(
    half,
    x,
    b,
    step,
    log,
    out,
    run_out,
    run_t_out,
    factor_out,
    total_out,
    x_here,
    b_here,
    matrix,
    step_here,
    log_here,
    sems,
    *,
    dims,
):
    first = pltpu.make_async_copy(log, log_here, sems.at[2 * dims[0]])
    second = pltpu.make_async_copy(step, step_here, sems.at[2 * dims[0] + 1])
    first.start()
    second.start()
    copies = state_copies(half[0], x, b, x_here, b_here, sems, dims)
    for copy in copies:
        copy.start()
    rows, heads = log_here.shape
    half_spreader(matrix, x_here.shape[1] * CORES // heads)
    upto = lax.broadcasted_iota(jnp.int32, (rows, rows), 1) <= lax.broadcasted_iota(jnp.int32, (rows, rows), 0)
    first.wait()
    high, rest = high_low(log_here[...])
    middle, low = high_low(rest)
    parts = jnp.concatenate([high, middle, low], axis=1).astype(BF16)
    sums = dot(jnp.where(upto, 1.0, 0.0).astype(BF16), parts)
    running = (sums[:, :heads] + sums[:, heads : 2 * heads] + sums[:, 2 * heads :]) * LOG2E
    last = running[rows - 1 :, :]
    run_out[...] = running
    run_t_out[...] = running.T
    second.wait()
    factor = step_here[...] * jnp.exp2(last - running)
    total = jnp.broadcast_to(last, total_out.shape)
    factor_out[...] = factor
    total_out[...] = total
    half_states(half[0], x_here, b_here, copies, factor, total, out, matrix, dims)


def own_state_kernel(half, x, b, factor, total, out, x_here, b_here, matrix, sems, *, dims):
    copies = state_copies(half[0], x, b, x_here, b_here, sems, dims)
    for copy in copies:
        copy.start()
    half_spreader(matrix, x_here.shape[1] * CORES // factor.shape[1])
    half_states(half[0], x_here, b_here, copies, factor[...], total[...], out, matrix, dims)


def chip_total_kernel(core, own, got, total, out, base_out):
    first = core[0] == 0
    cols = own.shape[1]
    states = out.shape[0]
    heads = total.shape[1]
    half = heads // CORES
    own_tail = own[states : states + 2, :].astype(F32)
    got_tail = got[states : states + 2, :].astype(F32)
    decay = jnp.where(first, got_tail, own_tail)
    decay = decay[:1, :] + decay[1:, :]
    one = jnp.ones_like(decay)
    on_own = jnp.where(first, decay, one)
    on_got = jnp.where(first, one, decay)
    for row in range(0, states, ROW_BLOCK):
        rows = slice(row, row + ROW_BLOCK)
        out[rows, :cols] = (on_own * own[rows, :].astype(F32) + on_got * got[rows, :].astype(F32)).astype(BF16)
    partner = got[states + 2 : states + 3, :heads].astype(F32) + got[states + 3 : states + 4, :heads].astype(F32)
    partner = partner + got[states + 4 : states + 5, :heads].astype(F32)
    partner = jnp.broadcast_to(partner, total.shape)
    base_out[...] = jnp.where(first, jnp.zeros_like(partner), partner)
    both = jnp.exp2(total[...] + partner)
    both = jnp.where(first, both, pltpu.roll(both, half, 1))
    high, low = high_low(both)
    lane = lax.broadcasted_iota(jnp.int32, both.shape, 1)
    packed = jnp.where(lane < half, high, pltpu.roll(low, half, 1))
    out[:, cols:] = jnp.concatenate([packed] * (states // packed.shape[0]), axis=0).astype(BF16)


def prefix_kernel(sent, out, ready, here, sems, *, width, blocks):
    chips, rows, cols = here.shape
    heads = ready.shape[1]
    half = heads // CORES
    step = cols // blocks
    ready[...] = jnp.zeros_like(ready)
    first_rows = jnp.concatenate([sent[k, :1, cols:].astype(F32) for k in range(chips)], axis=0)
    values = first_rows + pltpu.roll(first_rows, half, 1)
    matrix = spreader(step // width, width)
    copies = []
    for block in range(blocks):
        lanes = slice(block * step, (block + 1) * step)
        head = block * step // width
        decay = dot(packed(pltpu.roll(values, heads - head, 1) if head else values, step // width), matrix)
        state = jnp.zeros((rows, step), F32)
        for k in range(chips):
            here[k, :, lanes] = state.astype(BF16)
            state = decay[k : k + 1, :] * state + sent[k, :, lanes].astype(F32)
        copies.append(
            pltpu.make_async_copy(
                here.at[:, :, pl.ds(block * step, step)], out.at[:, :, pl.ds(block * step, step)], sems.at[block]
            )
        )
        copies[-1].start()
    for copy in copies:
        copy.wait()


def within_kernel(
    core, x_ref, b_ref, c_ref, step_ref, run_ref, run_t_ref, skip_ref, low_ref, high_ref, ready, out, matrix, *, dims
):
    del ready
    per_half, per_group, width = dims
    group = pl.program_id(0)
    head = group * per_group
    rows = x_ref.shape[0]
    pair = LANES // width

    @pl.when(group == 0)
    def _():
        matrix[...] = spreader(per_group, width)

    def spread(values):
        return dot(packed(values, per_group), matrix[...])

    step = group_first(step_ref[...], head)
    run = group_first(run_ref[...], head)
    skip = group_first(jnp.broadcast_to(skip_ref[...], (ROW_TILE, skip_ref.shape[1])), head)
    run_t = run_t_ref[pl.ds(pl.multiple_of(head, per_group), per_group), :]
    x = x_ref[...].astype(F32)
    scaled = (x * spread(step)).astype(BF16)
    upper = high_ref[...] * core[0].astype(BF16)
    before = dot(c_ref[...], jnp.where(group < per_half, low_ref[...], upper))
    outer = spread(skip)[:1, :] * x + spread(jnp.exp2(run)) * before
    lane = lax.broadcasted_iota(jnp.int32, (HALF_ROWS, LANES), 1) // width
    lower = lax.broadcasted_iota(jnp.int32, (HALF_ROWS, HALF_ROWS), 1) <= lax.broadcasted_iota(
        jnp.int32, (HALF_ROWS, HALF_ROWS), 0
    )
    b = b_ref[...]
    c = c_ref[...]
    for start in range(0, rows, HALF_ROWS):
        stop = start + HALF_ROWS
        scores = jnp.where(lower, dot(c[start:stop, :], b[start:stop, :], (1, 1)), 0.0)
        added = outer[start:stop, :]
        if start:
            edge = run[start - 1 : start, :]
            lead = spread(step[:start, :] * jnp.exp2(edge - run[:start, :]))
            lead = (x[:start, :] * lead).astype(BF16)
            cross = dot(c[start:stop, :], b[:start, :], (1, 1)).astype(BF16)
            added = added + spread(jnp.exp2(run[start:stop, :] - edge)) * dot(cross, lead)
        for first in range(0, per_group, pair):
            cols = slice(first * width, (first + pair) * width)
            here = scaled[start:stop, cols]
            weights = []
            values = []
            for k in range(pair):
                at = first + k
                gap = run[start:stop, at : at + 1] - run_t[at : at + 1, start:stop]
                weights.append((scores * jnp.exp2(jnp.minimum(gap, 0.0))).astype(BF16))
                values.append(jnp.where(lane == k, here, jnp.zeros_like(here)))
            part = dot(jnp.concatenate(weights, axis=1), jnp.concatenate(values, axis=0))
            out[start:stop, cols] = (added[:, cols] + part).astype(BF16)


def add_carried(half, within, rows_c, state, run, base, out, result, matrix, sems, dims):
    per_half, group_cols, _ = dims
    operand = packed_half(jnp.exp2(run[...] + base[:1, :]), half)
    copies = []
    for k in range(per_half):
        rows = rows_c(k)
        part = within(k)
        tiles = group_cols // TILE
        products = {}
        for n in range(tiles + AHEAD):
            if n < tiles:
                cols = slice(k * group_cols + n * TILE, k * group_cols + (n + 1) * TILE)
                products[n] = dot(rows, state[:, cols]), dot(operand, matrix[:, cols])
            m = n - AHEAD
            if m >= 0:
                cols = slice(k * group_cols + m * TILE, k * group_cols + (m + 1) * TILE)
                carried, factor = products.pop(m)
                result[:, cols] = (part[:, m * TILE : (m + 1) * TILE].astype(F32) + factor * carried).astype(BF16)
        home = pl.multiple_of((half * per_half + k) * group_cols, group_cols)
        copies.append(
            pltpu.make_async_copy(
                result.at[:, pl.ds(k * group_cols, group_cols)], out.at[:, pl.ds(home, group_cols)], sems.at[k]
            )
        )
        copies[-1].start()
    for copy in copies:
        copy.wait()


def first_final_kernel(
    half, within, c, state, run, base, out, other_within, other_c, matrix, here, c_here, result, loads, stores, *, dims
):
    per_half, group_cols, states = dims
    half_cols = per_half * group_cols
    half_rows = per_half * states
    mine = half[0]
    other = 1 - mine
    copies = []
    for k in range(per_half):
        home = pl.multiple_of((mine * per_half + k) * group_cols, group_cols)
        copies.append(
            pltpu.make_async_copy(
                within.at[:, pl.ds(home, group_cols)], here.at[:, pl.ds(k * group_cols, group_cols)], loads.at[k]
            )
        )
    home = pl.multiple_of(mine * half_rows, half_rows)
    copies.append(pltpu.make_async_copy(c.at[:, pl.ds(home, half_rows)], c_here, loads.at[per_half]))
    home = pl.multiple_of(other * half_rows, half_rows)
    copies.append(pltpu.make_async_copy(c.at[:, pl.ds(home, half_rows)], other_c, loads.at[per_half + 1]))
    home = pl.multiple_of(other * half_cols, half_cols)
    copies.append(pltpu.make_async_copy(within.at[:, pl.ds(home, half_cols)], other_within, loads.at[per_half + 2]))
    for copy in [copies[per_half]] + copies[:per_half] + copies[per_half + 1 :]:
        copy.start()
    half_spreader(matrix, out.shape[1] // run.shape[1])
    copies[per_half].wait()

    def part(k):
        copies[k].wait()
        return here[:, k * group_cols : (k + 1) * group_cols]

    def rows_c(k):
        return c_here[:, k * states : (k + 1) * states]

    add_carried(mine, part, rows_c, state, run, base, out, result, matrix, stores, dims)
    for copy in copies[per_half + 1 :]:
        copy.wait()


def second_final_kernel(half, within, c, state, run, base, matrix, filled, out, result, stores, *, dims):
    del filled
    _, group_cols, states = dims

    def part(k):
        return within[:, k * group_cols : (k + 1) * group_cols]

    def rows_c(k):
        return c[:, k * states : (k + 1) * states]

    add_carried(half[0], part, rows_c, state, run, base, out, result, matrix, stores, dims)


def local(inputs, step_size, log_decay, b_matrix, c_matrix, skip_gain, *, chip_axes, core_axis):
    tokens, channels = inputs.shape
    heads = step_size.shape[1]
    width = channels // heads
    states = b_matrix.shape[1] // GROUPS
    per_group = heads // GROUPS
    group_cols = per_group * width
    per_half = GROUPS // CORES
    half_cols = channels // CORES
    chips = lax.axis_size(chip_axes)
    rows = states // chips
    tall = states + ROW_TILE

    core = lax.axis_index(core_axis).astype(jnp.int32)
    mine = core.reshape(1)
    other = (1 - core).reshape(1)

    smem = pl.BlockSpec(memory_space=pltpu.SMEM)
    vmem = pl.BlockSpec(memory_space=pltpu.VMEM)
    hbm = pl.BlockSpec(memory_space=pltpu.HBM)
    anywhere = pl.BlockSpec(memory_space=pl.ANY)

    def whole(shape):
        return pl.BlockSpec(shape, lambda i, *_: (0,) * len(shape))

    def by_group(cols):
        return pl.BlockSpec((tokens, cols), lambda i, *_: (0, i))

    state_dims = (per_half, group_cols, states)
    half_dims = (per_half, per_group, width)
    half_scratch = [
        pltpu.VMEM((tokens, half_cols), BF16),
        pltpu.VMEM((tokens, per_half * states), BF16),
        pltpu.VMEM((heads, half_cols), BF16),
    ]

    inputs, step_size, log_decay, b_matrix, c_matrix = (
        pltpu.with_memory_space_constraint(array, pltpu.HBM)
        for array in (inputs, step_size, log_decay, b_matrix, c_matrix)
    )
    send, run, run_t, factor, total = pl.pallas_call(
        functools.partial(send_state_kernel, dims=state_dims),
        in_specs=[smem, hbm, hbm, hbm, hbm],
        out_specs=[vmem] * 5,
        out_shape=[
            jax.ShapeDtypeStruct((tall, half_cols), BF16),
            jax.ShapeDtypeStruct((tokens, heads), F32),
            jax.ShapeDtypeStruct((heads, tokens), F32),
            jax.ShapeDtypeStruct((tokens, heads), F32),
            jax.ShapeDtypeStruct((ROW_TILE, heads), F32),
        ],
        scratch_shapes=half_scratch
        + [pltpu.VMEM((tokens, heads), F32)] * 2
        + [pltpu.SemaphoreType.DMA((2 * per_half + 2,))],
        compiler_params=plain_params(),
        name="send_state",
    )(other, inputs, b_matrix, step_size, log_decay)

    swap = [(0, 1), (1, 0)]
    got = lax.ppermute(send, core_axis, swap)

    own = pl.pallas_call(
        functools.partial(own_state_kernel, dims=state_dims),
        in_specs=[smem, hbm, hbm, vmem, vmem],
        out_specs=vmem,
        out_shape=jax.ShapeDtypeStruct((tall, half_cols), BF16),
        scratch_shapes=half_scratch + [pltpu.SemaphoreType.DMA((2 * per_half,))],
        compiler_params=plain_params(),
        name="own_state",
    )(mine, inputs, b_matrix, factor, total)

    chip_total, base = pl.pallas_call(
        chip_total_kernel,
        in_specs=[smem, vmem, vmem, vmem],
        out_specs=[vmem, vmem],
        out_shape=[
            jax.ShapeDtypeStruct((states, half_cols + heads), BF16),
            jax.ShapeDtypeStruct((ROW_TILE, heads), F32),
        ],
        compiler_params=plain_params(),
        name="chip_total",
    )(mine, own, got, total)

    sent = lax.all_to_all(
        chip_total.reshape(chips, rows, half_cols + heads), chip_axes, split_axis=0, concat_axis=0, tiled=True
    )
    late = lax.ppermute(own, core_axis, swap[:1])

    entering, ready = pl.pallas_call(
        functools.partial(prefix_kernel, width=width, blocks=per_half),
        in_specs=[vmem],
        out_specs=[hbm, vmem],
        out_shape=[
            pltpu.HBM((chips, rows, half_cols), BF16),
            jax.ShapeDtypeStruct((ROW_TILE, heads), F32),
        ],
        scratch_shapes=[pltpu.VMEM((chips, rows, half_cols), BF16), pltpu.SemaphoreType.DMA((per_half,))],
        compiler_params=plain_params(),
        name="prefix",
    )(sent)
    entering = lax.all_to_all(entering, chip_axes, split_axis=0, concat_axis=0, tiled=True)

    within = pl.pallas_call(
        functools.partial(within_kernel, dims=half_dims),
        grid_spec=pltpu.PrefetchScalarGridSpec(
            num_scalar_prefetch=1,
            grid=(GROUPS,),
            in_specs=[
                by_group(group_cols),
                by_group(states),
                by_group(states),
                whole((tokens, heads)),
                whole((tokens, heads)),
                whole((heads, tokens)),
                whole((1, heads)),
                pl.BlockSpec((states, group_cols), lambda i, _: (0, jnp.minimum(i, per_half - 1))),
                pl.BlockSpec((states, group_cols), lambda i, _: (0, jnp.maximum(i - per_half, 0))),
                anywhere,
            ],
            out_specs=by_group(group_cols),
            scratch_shapes=[pltpu.VMEM((2 * per_group, group_cols), BF16)],
        ),
        out_shape=pltpu.HBM((tokens, channels), BF16),
        compiler_params=params(),
        name="within",
    )(mine, inputs, b_matrix, c_matrix, step_size, run, run_t, skip_gain.reshape(1, heads), late, got, ready)

    within = pltpu.with_memory_space_constraint(within, pltpu.HBM)
    entering = entering.reshape(states, half_cols)
    got_entering = lax.ppermute(entering, core_axis, swap)

    mixed = jax.ShapeDtypeStruct((tokens, channels), BF16)
    result, other_within, other_c, matrix = pl.pallas_call(
        functools.partial(first_final_kernel, dims=state_dims),
        in_specs=[smem, hbm, hbm, vmem, vmem, vmem],
        out_specs=[hbm, vmem, vmem, vmem],
        out_shape=[
            mixed,
            jax.ShapeDtypeStruct((tokens, half_cols), BF16),
            jax.ShapeDtypeStruct((tokens, per_half * states), BF16),
            jax.ShapeDtypeStruct((heads, half_cols), BF16),
        ],
        scratch_shapes=[
            pltpu.VMEM((tokens, half_cols), BF16),
            pltpu.VMEM((tokens, per_half * states), BF16),
            pltpu.VMEM((tokens, half_cols), BF16),
            pltpu.SemaphoreType.DMA((per_half + 3,)),
            pltpu.SemaphoreType.DMA((per_half,)),
        ],
        compiler_params=plain_params(),
        name="finish_own",
    )(mine, within, c_matrix, entering, run, base)
    return pl.pallas_call(
        functools.partial(second_final_kernel, dims=state_dims),
        in_specs=[smem] + [vmem] * 6 + [hbm],
        out_specs=hbm,
        out_shape=mixed,
        scratch_shapes=[pltpu.VMEM((tokens, half_cols), BF16), pltpu.SemaphoreType.DMA((per_half,))],
        input_output_aliases={7: 0},
        compiler_params=plain_params(),
        name="finish_other",
    )(other, other_within, other_c, got_entering, run, base, matrix, result)


def solution(mesh):
    outer, inner = mesh.axis_names
    chip_mesh = Mesh(
        mesh.devices.reshape(mesh.shape[outer], mesh.shape[inner] // CORES, CORES), (outer, "chip", "core")
    )
    placed = P((outer, "chip", "core"), None)

    def body(*args):
        return local(*args, chip_axes=(outer, "chip"), core_axis="core")

    return jax.shard_map(body, mesh=chip_mesh, in_specs=(placed,) * 5 + (P(),), out_specs=placed, check_vma=False)
```

```python
import functools
import math

import jax
import jax.numpy as jnp
from jax import lax
from jax.experimental import pallas as pl
from jax.experimental.pallas import tpu as pltpu
from jax.sharding import Mesh, PartitionSpec as P


GROUPS = 8
CORES = 2
LANES = 128
TILE = 256
AHEAD = 2
CHUNKS = 2
ROW_TILE = 8
HALF_ROWS = 128
ROW_BLOCK = 16
VMEM_LIMIT = 24 * 1024 * 1024
LOG2E = 1.0 / math.log(2.0)

F32 = jnp.float32
BF16 = jnp.bfloat16


def dot(a, b, contract=(1, 0)):
    dims = (((contract[0],), (contract[1],)), ((), ()))
    return lax.dot_general(a, b, dims, preferred_element_type=F32)


def high_low(values):
    high = values.astype(BF16).astype(F32)
    return high, values - high


def spreader(heads, width):
    shape = (2 * heads, heads * width)
    row = lax.broadcasted_iota(jnp.int32, shape, 0)
    col = lax.broadcasted_iota(jnp.int32, shape, 1)
    row = jnp.where(row >= heads, row - heads, row)
    return jnp.where(row == col // width, 1.0, 0.0).astype(BF16)


def group_first(values, head):
    lanes = values.shape[1]
    return pltpu.roll(values, lax.rem(lanes - head, lanes), 1)


def packed(values, heads):
    high, low = high_low(values)
    lane = lax.broadcasted_iota(jnp.int32, values.shape, 1)
    return jnp.where(lane < heads, high, pltpu.roll(low, heads, 1)).astype(BF16)[:, : 2 * heads]


def half_spreader(matrix, width):
    lanes, cols = matrix.shape
    for start in range(0, cols, TILE):
        row = lax.broadcasted_iota(jnp.int32, (lanes, TILE), 0)
        col = start + lax.broadcasted_iota(jnp.int32, (lanes, TILE), 1)
        row = jnp.where(row >= lanes // 2, row - lanes // 2, row)
        matrix[:, start : start + TILE] = jnp.where(row == col // width, 1.0, 0.0).astype(BF16)


def packed_half(values, half):
    lanes = values.shape[1]
    values = group_first(values, half * (lanes // 2))
    high, low = high_low(values)
    lane = lax.broadcasted_iota(jnp.int32, values.shape, 1)
    return jnp.where(lane < lanes // 2, high, pltpu.roll(low, lanes // 2, 1)).astype(BF16)


def params():
    return pltpu.CompilerParams(dimension_semantics=("arbitrary",), vmem_limit_bytes=VMEM_LIMIT)


def plain_params():
    return pltpu.CompilerParams(vmem_limit_bytes=VMEM_LIMIT)


def state_copies(half, x, b, x_here, b_here, sems, dims):
    per_half, group_cols, states = dims
    copies = []
    for k in range(per_half):
        group = half * per_half + k
        copies.append(
            pltpu.make_async_copy(
                x.at[:, pl.ds(pl.multiple_of(group * group_cols, group_cols), group_cols)],
                x_here.at[:, pl.ds(k * group_cols, group_cols)],
                sems.at[2 * k],
            )
        )
        copies.append(
            pltpu.make_async_copy(
                b.at[:, pl.ds(pl.multiple_of(group * states, states), states)],
                b_here.at[:, pl.ds(k * states, states)],
                sems.at[2 * k + 1],
            )
        )
    return copies


def half_states(half, x_here, b_here, copies, factor, log_total, out, matrix, dims):
    _, group_cols, states = dims
    rows, heads = factor.shape
    row = lax.broadcasted_iota(jnp.int32, (ROW_TILE, TILE), 0)
    operand = packed_half(jnp.concatenate([factor, jnp.exp2(log_total)], axis=0), half)
    for copy in copies:
        copy.wait()
    tiles = out.shape[1] // TILE
    per_group = group_cols // TILE
    matrices = {}
    factors = {}
    scaled = {}
    for n in range(tiles + 2 * AHEAD):
        if n < tiles:
            factors[n] = dot(operand, matrix[:, n * TILE : (n + 1) * TILE])
        m = n - AHEAD
        if 0 <= m < tiles:
            cols = slice(m * TILE, (m + 1) * TILE)
            spread = factors.pop(m)
            scaled[m] = (x_here[:, cols].astype(F32) * spread[:rows, :]).astype(BF16)
            high, low = high_low(spread[rows:, :])
            tail = jnp.where(row == 0, high, low)
            if m == 0:
                high, low = high_low(log_total)
                middle, low = high_low(low)
                at = row[:, :heads]
                logs = jnp.where(at == 2, high, jnp.where(at == 3, middle, low))
                logs = jnp.where(at < 2, tail[:, :heads], logs)
                tail = jnp.concatenate([logs, tail[:, heads:]], axis=1)
            out[states:, cols] = tail.astype(BF16)
            if m % per_group == 0:
                k = m // per_group
                matrices[k] = b_here[:, k * states : (k + 1) * states].T
        m = n - 2 * AHEAD
        if m >= 0:
            out[:states, m * TILE : (m + 1) * TILE] = dot(matrices[m // per_group], scaled.pop(m)).astype(BF16)


def send_state_kernel(
    half,
    x,
    b,
    step,
    log,
    out,
    run_out,
    run_t_out,
    factor_out,
    total_out,
    x_here,
    b_here,
    matrix,
    step_here,
    log_here,
    sems,
    *,
    dims,
):
    first = pltpu.make_async_copy(log, log_here, sems.at[2 * dims[0]])
    second = pltpu.make_async_copy(step, step_here, sems.at[2 * dims[0] + 1])
    first.start()
    second.start()
    copies = state_copies(half[0], x, b, x_here, b_here, sems, dims)
    for copy in copies:
        copy.start()
    rows, heads = log_here.shape
    half_spreader(matrix, x_here.shape[1] * CORES // heads)
    upto = lax.broadcasted_iota(jnp.int32, (rows, rows), 1) <= lax.broadcasted_iota(jnp.int32, (rows, rows), 0)
    first.wait()
    high, rest = high_low(log_here[...])
    middle, low = high_low(rest)
    parts = jnp.concatenate([high, middle, low], axis=1).astype(BF16)
    sums = dot(jnp.where(upto, 1.0, 0.0).astype(BF16), parts)
    running = (sums[:, :heads] + sums[:, heads : 2 * heads] + sums[:, 2 * heads :]) * LOG2E
    last = running[rows - 1 :, :]
    run_out[...] = running
    run_t_out[...] = running.T
    second.wait()
    factor = step_here[...] * jnp.exp2(last - running)
    total = jnp.broadcast_to(last, total_out.shape)
    factor_out[...] = factor
    total_out[...] = total
    half_states(half[0], x_here, b_here, copies, factor, total, out, matrix, dims)


def own_state_kernel(half, x, b, factor, total, out, matrix, x_here, b_here, sems, *, dims):
    copies = state_copies(half[0], x, b, x_here, b_here, sems, dims)
    for copy in copies:
        copy.start()
    half_spreader(matrix, x_here.shape[1] * CORES // factor.shape[1])
    half_states(half[0], x_here, b_here, copies, factor[...], total[...], out, matrix, dims)


def mixing_rows(first, own, got, states, cols):
    own_tail = own[states : states + 2, cols].astype(F32)
    got_tail = got[states : states + 2, cols].astype(F32)
    decay = jnp.where(first, got_tail, own_tail)
    decay = decay[:1, :] + decay[1:, :]
    one = jnp.ones_like(decay)
    return jnp.where(first, decay, one), jnp.where(first, one, decay)


def side_by_side(values, half):
    high, low = high_low(values)
    lane = lax.broadcasted_iota(jnp.int32, values.shape, 1)
    return jnp.where(lane < half, high, pltpu.roll(low, half, 1))


def chip_decay(first, got, total, states, base_out):
    heads = total.shape[1]
    half = heads // CORES
    partner = got[states + 2 : states + 3, :heads].astype(F32) + got[states + 3 : states + 4, :heads].astype(F32)
    partner = partner + got[states + 4 : states + 5, :heads].astype(F32)
    partner = jnp.broadcast_to(partner, total.shape)
    base_out[...] = jnp.where(first, jnp.zeros_like(partner), partner)
    both = jnp.exp2(total[...] + partner)
    both = jnp.where(first, both, pltpu.roll(both, half, 1))
    return side_by_side(both, half)


def chip_total_kernel(at, own, got, total, out, base_out):
    first = at[0] == 0
    cols = own.shape[1]
    states = out.shape[0]
    on_own, on_got = mixing_rows(first, own, got, states, slice(0, cols))
    for row in range(0, states, ROW_BLOCK):
        rows = slice(row, row + ROW_BLOCK)
        out[rows, :cols] = (on_own * own[rows, :].astype(F32) + on_got * got[rows, :].astype(F32)).astype(BF16)
    packed_decay = chip_decay(first, got, total, states, base_out)
    out[:, cols:] = jnp.concatenate([packed_decay] * (states // ROW_TILE), axis=0).astype(BF16)


def pieces_kernel(at, own, got, total, *outs, states, chunk):
    base_out = outs[-1]
    first = at[0] == 0
    rows, cols = outs[0].shape
    cols = cols - total.shape[1]
    here = slice(chunk * cols, (chunk + 1) * cols)
    on_own, on_got = mixing_rows(first, own, got, states, here)
    packed_decay = chip_decay(first, got, total, states, base_out)
    for k, out in enumerate(outs[:-1]):
        start = pl.multiple_of(jnp.bitwise_xor(at[1], k) * rows, rows)
        for row in range(0, rows, ROW_BLOCK):
            take = pl.ds(start + row, ROW_BLOCK)
            mixed = on_own * own[take, here].astype(F32) + on_got * got[take, here].astype(F32)
            out[row : row + ROW_BLOCK, :cols] = mixed.astype(BF16)
        out[:, cols:] = jnp.concatenate([packed_decay] * (rows // ROW_TILE), axis=0).astype(BF16)


def decays_of(pieces, cols, first_head, width):
    lanes = pieces[0].shape[1] - cols
    sent = [piece[:ROW_TILE, cols:].astype(F32)[:1, :] for piece in pieces]
    sent = jnp.concatenate(sent + [jnp.zeros((ROW_TILE - len(sent), lanes), F32)], axis=0)
    values = sent + pltpu.roll(sent, lanes // CORES, 1)
    heads = cols // width
    here = pltpu.roll(values, lanes - first_head, 1) if first_head else values
    return values, dot(packed(here, heads), spreader(heads, width))


def column_kernel(at, *refs, first_head, width, count, parts):
    pieces, outs, decay_out, total = refs[:count], refs[count : count + parts], refs[-2], refs[-1]
    rows, cols = total.shape
    values, decay = decays_of(pieces, cols, first_head, width)
    decay_out[...] = decay
    for place in range(count):

        @pl.when(at[1] == place)
        def _():
            state = jnp.zeros((rows, cols), F32)
            for k in range(count):
                k = k ^ place
                state = decay[k : k + 1, :] * state + pieces[k][:, :cols].astype(F32)
            total[...] = state

    product = values[:1, :]
    for k in range(1, count):
        product = product * values[k : k + 1, :]
    product = side_by_side(jnp.broadcast_to(product, (ROW_TILE, product.shape[1])), product.shape[1] // CORES)
    part = rows // parts
    for k, out in enumerate(outs):
        start = pl.multiple_of(jnp.bitwise_xor(at[2], k) * part, part)
        out[:, :cols] = total[pl.ds(start, part), :].astype(BF16)
        out[:, cols:] = jnp.concatenate([product] * (part // ROW_TILE), axis=0).astype(BF16)


def outer_kernel(at, *refs, first_head, width, count):
    pieces, outs = refs[:count], refs[count:]
    rows, cols = outs[0].shape
    _, decay = decays_of(pieces, cols, first_head, width)
    for place in range(count):

        @pl.when(at[2] == place)
        def _():
            state = jnp.zeros((rows, cols), F32)
            for k in range(count):
                k = k ^ place
                outs[k][...] = state.astype(BF16)
                state = decay[k : k + 1, :] * state + pieces[k][:, :cols].astype(F32)


def chips_kernel(at, *refs, count, parts):
    pieces, decay, carries = refs[:count], refs[count], refs[count + 1 : count + 1 + parts]
    outs, carry = refs[count + 1 + parts : -1], refs[-1]
    rows, cols = carry.shape
    part = rows // parts
    for k, piece in enumerate(carries):
        start = pl.multiple_of(jnp.bitwise_xor(at[2], k) * part, part)
        carry[pl.ds(start, part), :] = piece[...].astype(F32)
    for place in range(count):

        @pl.when(at[1] == place)
        def _():
            state = carry[...]
            for k in range(count):
                k = k ^ place
                outs[k][...] = state.astype(BF16)
                state = decay[k : k + 1, :] * state + pieces[k][:, :cols].astype(F32)


def assemble_kernel(at, *refs, count):
    out = refs[-1]
    for n, piece in enumerate(refs[:-1]):
        rows, cols = piece.shape
        start = pl.multiple_of(jnp.bitwise_xor(at[1], n % count) * rows, rows)
        out[pl.ds(start, rows), n // count * cols : (n // count + 1) * cols] = piece[...]


def prefix_kernel(sent, out, here, sems, *, width, blocks):
    chips, rows, cols = here.shape
    heads = sent.shape[2] - cols
    half = heads // CORES
    step = cols // blocks
    first_rows = jnp.concatenate([sent[k, :1, cols:].astype(F32) for k in range(chips)], axis=0)
    values = first_rows + pltpu.roll(first_rows, half, 1)
    matrix = spreader(step // width, width)
    copies = []
    for block in range(blocks):
        lanes = slice(block * step, (block + 1) * step)
        head = block * step // width
        decay = dot(packed(pltpu.roll(values, heads - head, 1) if head else values, step // width), matrix)
        state = jnp.zeros((rows, step), F32)
        for k in range(chips):
            here[k, :, lanes] = state.astype(BF16)
            state = decay[k : k + 1, :] * state + sent[k, :, lanes].astype(F32)
        copies.append(
            pltpu.make_async_copy(
                here.at[:, :, pl.ds(block * step, step)], out.at[:, :, pl.ds(block * step, step)], sems.at[block]
            )
        )
        copies[-1].start()
    for copy in copies:
        copy.wait()


def within_kernel(
    at, x_ref, b_ref, c_ref, step_ref, run_ref, run_t_ref, skip_ref, before_ref, out, matrix, *, dims
):
    per_half, per_group, width = dims
    turn = pl.program_id(0)
    group = at[0] * per_half + turn
    head = group * per_group
    rows = x_ref.shape[0]
    pair = LANES // width

    @pl.when(turn == 0)
    def _():
        matrix[...] = spreader(per_group, width)

    def spread(values):
        return dot(packed(values, per_group), matrix[...])

    step = group_first(step_ref[...], head)
    run = group_first(run_ref[...], head)
    skip = group_first(jnp.broadcast_to(skip_ref[...], (ROW_TILE, skip_ref.shape[1])), head)
    run_t = run_t_ref[pl.ds(pl.multiple_of(head, per_group), per_group), :]
    x = x_ref[...].astype(F32)
    scaled = (x * spread(step)).astype(BF16)
    before = dot(c_ref[...], before_ref[...] * at[1].astype(BF16))
    outer = spread(skip)[:1, :] * x + spread(jnp.exp2(run)) * before
    lane = lax.broadcasted_iota(jnp.int32, (HALF_ROWS, LANES), 1) // width
    lower = lax.broadcasted_iota(jnp.int32, (HALF_ROWS, HALF_ROWS), 1) <= lax.broadcasted_iota(
        jnp.int32, (HALF_ROWS, HALF_ROWS), 0
    )
    b = b_ref[...]
    c = c_ref[...]
    for start in range(0, rows, HALF_ROWS):
        stop = start + HALF_ROWS
        scores = jnp.where(lower, dot(c[start:stop, :], b[start:stop, :], (1, 1)), 0.0)
        added = outer[start:stop, :]
        if start:
            edge = run[start - 1 : start, :]
            lead = spread(step[:start, :] * jnp.exp2(edge - run[:start, :]))
            lead = (x[:start, :] * lead).astype(BF16)
            cross = dot(c[start:stop, :], b[:start, :], (1, 1)).astype(BF16)
            added = added + spread(jnp.exp2(run[start:stop, :] - edge)) * dot(cross, lead)
        for first in range(0, per_group, pair):
            cols = slice(first * width, (first + pair) * width)
            here = scaled[start:stop, cols]
            weights = []
            values = []
            for k in range(pair):
                at = first + k
                gap = run[start:stop, at : at + 1] - run_t[at : at + 1, start:stop]
                weights.append((scores * jnp.exp2(jnp.minimum(gap, 0.0))).astype(BF16))
                values.append(jnp.where(lane == k, here, jnp.zeros_like(here)))
            part = dot(jnp.concatenate(weights, axis=1), jnp.concatenate(values, axis=0))
            out[start:stop, cols] = (added[:, cols] + part).astype(BF16)


def add_carried(half, within, rows_c, state, run, base, out, result, matrix, sems, dims):
    per_half, group_cols, _ = dims
    operand = packed_half(jnp.exp2(run[...] + base[:1, :]), half)
    copies = []
    for k in range(per_half):
        rows = rows_c(k)
        part = within(k)
        tiles = group_cols // TILE
        products = {}
        for n in range(tiles + AHEAD):
            if n < tiles:
                cols = slice(k * group_cols + n * TILE, k * group_cols + (n + 1) * TILE)
                products[n] = dot(rows, state[:, cols]), dot(operand, matrix[:, cols])
            m = n - AHEAD
            if m >= 0:
                cols = slice(k * group_cols + m * TILE, k * group_cols + (m + 1) * TILE)
                carried, factor = products.pop(m)
                result[:, cols] = (part[:, m * TILE : (m + 1) * TILE].astype(F32) + factor * carried).astype(BF16)
        home = pl.multiple_of((half * per_half + k) * group_cols, group_cols)
        copies.append(
            pltpu.make_async_copy(
                result.at[:, pl.ds(k * group_cols, group_cols)], out.at[:, pl.ds(home, group_cols)], sems.at[k]
            )
        )
        copies[-1].start()
    for copy in copies:
        copy.wait()


def final_kernel(half, within, c, state, run, base, matrix, filled, out, result, stores, *, dims):
    del filled
    per_half, group_cols, states = dims

    def part(k):
        return within[:, k * group_cols : (k + 1) * group_cols]

    def rows_c(k):
        return c[:, pl.ds(pl.multiple_of((half[0] * per_half + k) * states, states), states)]

    add_carried(half[0], part, rows_c, state, run, base, out, result, matrix, stores, dims)


def first_final_kernel(half, within, c, state, run, base, matrix, out, result, stores, *, dims):
    final_kernel(half, within, c, state, run, base, matrix, None, out, result, stores, dims=dims)


def small_call(kernel, in_specs, out_shape, scratch=(), out_specs=None):
    return pl.pallas_call(
        kernel,
        in_specs=in_specs,
        out_specs=out_specs or [pl.BlockSpec(memory_space=pltpu.VMEM)] * len(out_shape),
        out_shape=out_shape,
        scratch_shapes=list(scratch),
        compiler_params=plain_params(),
    )


def xor_route(size, k):
    return [(i, i ^ k) for i in range(size)]


def swapped(arrays, axis):
    size = lax.axis_size(axis)
    order = sorted(range(1, size), key=lambda k: -(k.bit_length()))
    done = {0: arrays[0]}
    for k in order:
        done[k] = lax.ppermute(arrays[k], axis, xor_route(size, k))
    return [done[k] for k in range(size)]


def entering_by_swaps(at, own, got, total, width, states, outer_axis, chip_axis):
    half_cols = own.shape[1]
    heads = total.shape[1]
    count = lax.axis_size(chip_axis)
    parts = lax.axis_size(outer_axis)
    rows = states // count
    part = rows // parts
    cols = half_cols // CHUNKS
    smem = pl.BlockSpec(memory_space=pltpu.SMEM)
    vmem = pl.BlockSpec(memory_space=pltpu.VMEM)
    shape = jax.ShapeDtypeStruct
    gathered = []
    for chunk in range(CHUNKS):
        *pieces, base = small_call(
            functools.partial(pieces_kernel, states=states, chunk=chunk),
            [smem] + [vmem] * 3,
            [shape((rows, cols + heads), BF16)] * count + [shape((ROW_TILE, heads), F32)],
        )(at, own, got, total)
        gathered.append(swapped(pieces, chip_axis))
    entering = []
    for chunk in range(CHUNKS):
        first_head = chunk * cols // width
        pieces = gathered[chunk]
        *totals, decay = small_call(
            functools.partial(column_kernel, first_head=first_head, width=width, count=count, parts=parts),
            [smem] + [vmem] * count,
            [shape((part, cols + heads), BF16)] * parts + [shape((ROW_TILE, cols), F32)],
            [pltpu.VMEM((rows, cols), F32)],
        )(at, *pieces)
        totals = swapped(totals, outer_axis)
        carries = small_call(
            functools.partial(outer_kernel, first_head=first_head, width=width, count=parts),
            [smem] + [vmem] * parts,
            [shape((part, cols), BF16)] * parts,
        )(at, *totals)
        carries = swapped(carries, outer_axis)
        states_out = small_call(
            functools.partial(chips_kernel, count=count, parts=parts),
            [smem] + [vmem] * (count + 1 + parts),
            [shape((rows, cols), BF16)] * count,
            [pltpu.VMEM((rows, cols), F32)],
        )(at, *pieces, decay, *carries)
        entering += swapped(states_out, chip_axis)
    (entering,) = small_call(
        functools.partial(assemble_kernel, count=count),
        [smem] + [vmem] * len(entering),
        [shape((states, half_cols), BF16)],
    )(at, *entering)
    return entering, base


def entering_by_all_to_all(at, own, got, total, width, states, outer_axis, chip_axis):
    half_cols = own.shape[1]
    heads = total.shape[1]
    chips = lax.axis_size((outer_axis, chip_axis))
    rows = states // chips
    smem = pl.BlockSpec(memory_space=pltpu.SMEM)
    vmem = pl.BlockSpec(memory_space=pltpu.VMEM)
    chip_total, base = small_call(
        chip_total_kernel,
        [smem] + [vmem] * 3,
        [jax.ShapeDtypeStruct((states, half_cols + heads), BF16), jax.ShapeDtypeStruct((ROW_TILE, heads), F32)],
    )(at, own, got, total)
    sent = lax.all_to_all(
        chip_total.reshape(chips, rows, half_cols + heads),
        (outer_axis, chip_axis),
        split_axis=0,
        concat_axis=0,
        tiled=True,
    )
    blocks = GROUPS // CORES
    (entering,) = small_call(
        functools.partial(prefix_kernel, width=width, blocks=blocks),
        [vmem],
        [pltpu.HBM((chips, rows, half_cols), BF16)],
        [pltpu.VMEM((chips, rows, half_cols), BF16), pltpu.SemaphoreType.DMA((blocks,))],
        [pl.BlockSpec(memory_space=pltpu.HBM)],
    )(sent)
    entering = lax.all_to_all(entering, (outer_axis, chip_axis), split_axis=0, concat_axis=0, tiled=True)
    return entering.reshape(states, half_cols), base


def local(inputs, step_size, log_decay, b_matrix, c_matrix, skip_gain, *, outer_axis, chip_axis, core_axis):
    tokens, channels = inputs.shape
    heads = step_size.shape[1]
    width = channels // heads
    states = b_matrix.shape[1] // GROUPS
    per_group = heads // GROUPS
    group_cols = per_group * width
    per_half = GROUPS // CORES
    half_cols = channels // CORES
    chips = lax.axis_size((outer_axis, chip_axis))
    by_swaps = chips & (chips - 1) == 0 and states % (chips * ROW_TILE) == 0
    tall = states + ROW_TILE

    core = lax.axis_index(core_axis).astype(jnp.int32)
    mine = core.reshape(1)
    other = (1 - core).reshape(1)
    at = jnp.stack([core, lax.axis_index(chip_axis).astype(jnp.int32), lax.axis_index(outer_axis).astype(jnp.int32)])

    smem = pl.BlockSpec(memory_space=pltpu.SMEM)
    vmem = pl.BlockSpec(memory_space=pltpu.VMEM)
    hbm = pl.BlockSpec(memory_space=pltpu.HBM)

    def whole(shape):
        return pl.BlockSpec(shape, lambda i, *_: (0,) * len(shape))

    def by_group(cols):
        return pl.BlockSpec((tokens, cols), lambda i, at: (0, at[0] * per_half + i))

    state_dims = (per_half, group_cols, states)
    half_dims = (per_half, per_group, width)
    half_scratch = [
        pltpu.VMEM((tokens, half_cols), BF16),
        pltpu.VMEM((tokens, per_half * states), BF16),
    ]

    inputs, step_size, log_decay, b_matrix = (
        pltpu.with_memory_space_constraint(array, pltpu.HBM) for array in (inputs, step_size, log_decay, b_matrix)
    )
    send, run, run_t, factor, total = pl.pallas_call(
        functools.partial(send_state_kernel, dims=state_dims),
        in_specs=[smem, hbm, hbm, hbm, hbm],
        out_specs=[vmem] * 5,
        out_shape=[
            jax.ShapeDtypeStruct((tall, half_cols), BF16),
            jax.ShapeDtypeStruct((tokens, heads), F32),
            jax.ShapeDtypeStruct((heads, tokens), F32),
            jax.ShapeDtypeStruct((tokens, heads), F32),
            jax.ShapeDtypeStruct((ROW_TILE, heads), F32),
        ],
        scratch_shapes=half_scratch
        + [pltpu.VMEM((heads, half_cols), BF16)]
        + [pltpu.VMEM((tokens, heads), F32)] * 2
        + [pltpu.SemaphoreType.DMA((2 * per_half + 2,))],
        compiler_params=plain_params(),
        name="send_state",
    )(other, inputs, b_matrix, step_size, log_decay)

    swap = [(0, 1), (1, 0)]
    got = lax.ppermute(send, core_axis, swap)

    own, matrix = small_call(
        functools.partial(own_state_kernel, dims=state_dims),
        [smem, hbm, hbm, vmem, vmem],
        [jax.ShapeDtypeStruct((tall, half_cols), BF16), jax.ShapeDtypeStruct((heads, half_cols), BF16)],
        half_scratch + [pltpu.SemaphoreType.DMA((2 * per_half,))],
    )(mine, inputs, b_matrix, factor, total)

    find_entering = entering_by_swaps if by_swaps else entering_by_all_to_all
    entering, base = find_entering(at, own, got, total, width, states, outer_axis, chip_axis)
    late = lax.ppermute(own, core_axis, swap[:1])

    def within(half, before):
        return pl.pallas_call(
            functools.partial(within_kernel, dims=half_dims),
            grid_spec=pltpu.PrefetchScalarGridSpec(
                num_scalar_prefetch=1,
                grid=(per_half,),
                in_specs=[
                    by_group(group_cols),
                    by_group(states),
                    by_group(states),
                    whole((tokens, heads)),
                    whole((tokens, heads)),
                    whole((heads, tokens)),
                    whole((1, heads)),
                    pl.BlockSpec((states, group_cols), lambda i, at: (0, i)),
                ],
                out_specs=pl.BlockSpec((tokens, group_cols), lambda i, at: (0, i)),
                scratch_shapes=[pltpu.VMEM((2 * per_group, group_cols), BF16)],
            ),
            out_shape=jax.ShapeDtypeStruct((tokens, half_cols), BF16),
            compiler_params=params(),
            name="within",
        )(
            jnp.concatenate([half, mine]),
            inputs,
            b_matrix,
            c_matrix,
            step_size,
            run,
            run_t,
            skip_gain.reshape(1, heads),
            before,
        )

    own_within = within(mine, got)
    other_within = within(other, late)

    got_entering = lax.ppermute(entering, core_axis, swap)
    mixed = jax.ShapeDtypeStruct((tokens, channels), BF16)
    final_scratch = [pltpu.VMEM((tokens, half_cols), BF16), pltpu.SemaphoreType.DMA((per_half,))]
    (result,) = small_call(
        functools.partial(first_final_kernel, dims=state_dims), [smem] + [vmem] * 6, [mixed], final_scratch, [hbm]
    )(mine, own_within, c_matrix, entering, run, base, matrix)
    return pl.pallas_call(
        functools.partial(final_kernel, dims=state_dims),
        in_specs=[smem] + [vmem] * 6 + [hbm],
        out_specs=hbm,
        out_shape=mixed,
        scratch_shapes=final_scratch,
        input_output_aliases={7: 0},
        compiler_params=plain_params(),
        name="finish_other",
    )(other, other_within, c_matrix, got_entering, run, base, matrix, result)


def solution(mesh):
    outer, inner = mesh.axis_names
    chip_mesh = Mesh(
        mesh.devices.reshape(mesh.shape[outer], mesh.shape[inner] // CORES, CORES), (outer, "chip", "core")
    )
    placed = P((outer, "chip", "core"), None)

    def body(*args):
        return local(*args, outer_axis=outer, chip_axis="chip", core_axis="core")

    return jax.shard_map(body, mesh=chip_mesh, in_specs=(placed,) * 5 + (P(),), out_specs=placed, check_vma=False)
```

```python
import functools
import math

import jax
import jax.numpy as jnp
from jax import lax
from jax.experimental import pallas as pl
from jax.experimental.pallas import tpu as pltpu
from jax.sharding import Mesh, PartitionSpec as P


GROUPS = 8
CORES = 2
LANES = 128
TILE = 256
AHEAD = 2
CHUNKS = 2
ROW_TILE = 8
HALF_ROWS = 128
ROW_BLOCK = 16
VMEM_LIMIT = 24 * 1024 * 1024
LOG2E = 1.0 / math.log(2.0)

F32 = jnp.float32
BF16 = jnp.bfloat16


def dot(a, b, contract=(1, 0)):
    dims = (((contract[0],), (contract[1],)), ((), ()))
    return lax.dot_general(a, b, dims, preferred_element_type=F32)


def high_low(values):
    high = values.astype(BF16).astype(F32)
    return high, values - high


def spreader(heads, width):
    shape = (2 * heads, heads * width)
    row = lax.broadcasted_iota(jnp.int32, shape, 0)
    col = lax.broadcasted_iota(jnp.int32, shape, 1)
    row = jnp.where(row >= heads, row - heads, row)
    return jnp.where(row == col // width, 1.0, 0.0).astype(BF16)


def group_first(values, head):
    lanes = values.shape[1]
    return pltpu.roll(values, lax.rem(lanes - head, lanes), 1)


def packed(values, heads):
    high, low = high_low(values)
    lane = lax.broadcasted_iota(jnp.int32, values.shape, 1)
    return jnp.where(lane < heads, high, pltpu.roll(low, heads, 1)).astype(BF16)[:, : 2 * heads]


def half_spreader(matrix, width):
    lanes, cols = matrix.shape
    for start in range(0, cols, TILE):
        row = lax.broadcasted_iota(jnp.int32, (lanes, TILE), 0)
        col = start + lax.broadcasted_iota(jnp.int32, (lanes, TILE), 1)
        row = jnp.where(row >= lanes // 2, row - lanes // 2, row)
        matrix[:, start : start + TILE] = jnp.where(row == col // width, 1.0, 0.0).astype(BF16)


def packed_half(values, half):
    lanes = values.shape[1]
    values = group_first(values, half * (lanes // 2))
    high, low = high_low(values)
    lane = lax.broadcasted_iota(jnp.int32, values.shape, 1)
    return jnp.where(lane < lanes // 2, high, pltpu.roll(low, lanes // 2, 1)).astype(BF16)


def params():
    return pltpu.CompilerParams(dimension_semantics=("arbitrary",), vmem_limit_bytes=VMEM_LIMIT)


def plain_params():
    return pltpu.CompilerParams(vmem_limit_bytes=VMEM_LIMIT)


def state_copies(half, x, b, x_here, b_here, sems, dims):
    per_half, group_cols, states = dims
    copies = []
    for k in range(per_half):
        group = half * per_half + k
        copies.append(
            pltpu.make_async_copy(
                x.at[:, pl.ds(pl.multiple_of(group * group_cols, group_cols), group_cols)],
                x_here.at[:, pl.ds(k * group_cols, group_cols)],
                sems.at[2 * k],
            )
        )
        copies.append(
            pltpu.make_async_copy(
                b.at[:, pl.ds(pl.multiple_of(group * states, states), states)],
                b_here.at[:, pl.ds(k * states, states)],
                sems.at[2 * k + 1],
            )
        )
    return copies


def half_states(half, x_here, b_here, copies, factor, log_total, out, matrix, dims):
    _, group_cols, states = dims
    rows, heads = factor.shape
    row = lax.broadcasted_iota(jnp.int32, (ROW_TILE, TILE), 0)
    operand = packed_half(jnp.concatenate([factor, jnp.exp2(log_total)], axis=0), half)
    for copy in copies:
        copy.wait()
    tiles = out.shape[1] // TILE
    per_group = group_cols // TILE
    matrices = {}
    factors = {}
    scaled = {}
    for n in range(tiles + 2 * AHEAD):
        if n < tiles:
            factors[n] = dot(operand, matrix[:, n * TILE : (n + 1) * TILE])
        m = n - AHEAD
        if 0 <= m < tiles:
            cols = slice(m * TILE, (m + 1) * TILE)
            spread = factors.pop(m)
            scaled[m] = (x_here[:, cols].astype(F32) * spread[:rows, :]).astype(BF16)
            high, low = high_low(spread[rows:, :])
            tail = jnp.where(row == 0, high, low)
            if m == 0:
                high, low = high_low(log_total)
                middle, low = high_low(low)
                at = row[:, :heads]
                logs = jnp.where(at == 2, high, jnp.where(at == 3, middle, low))
                logs = jnp.where(at < 2, tail[:, :heads], logs)
                tail = jnp.concatenate([logs, tail[:, heads:]], axis=1)
            out[states:, cols] = tail.astype(BF16)
            if m % per_group == 0:
                k = m // per_group
                matrices[k] = b_here[:, k * states : (k + 1) * states].T
        m = n - 2 * AHEAD
        if m >= 0:
            out[:states, m * TILE : (m + 1) * TILE] = dot(matrices[m // per_group], scaled.pop(m)).astype(BF16)


def send_state_kernel(
    half,
    x,
    b,
    step,
    log,
    out,
    run_out,
    run_t_out,
    factor_out,
    total_out,
    x_here,
    b_here,
    matrix,
    step_here,
    log_here,
    sems,
    *,
    dims,
):
    first = pltpu.make_async_copy(log, log_here, sems.at[2 * dims[0]])
    second = pltpu.make_async_copy(step, step_here, sems.at[2 * dims[0] + 1])
    first.start()
    second.start()
    copies = state_copies(half[0], x, b, x_here, b_here, sems, dims)
    for copy in copies:
        copy.start()
    rows, heads = log_here.shape
    half_spreader(matrix, x_here.shape[1] * CORES // heads)
    upto = lax.broadcasted_iota(jnp.int32, (rows, rows), 1) <= lax.broadcasted_iota(jnp.int32, (rows, rows), 0)
    first.wait()
    high, rest = high_low(log_here[...])
    middle, low = high_low(rest)
    parts = jnp.concatenate([high, middle, low], axis=1).astype(BF16)
    sums = dot(jnp.where(upto, 1.0, 0.0).astype(BF16), parts)
    running = (sums[:, :heads] + sums[:, heads : 2 * heads] + sums[:, 2 * heads :]) * LOG2E
    last = running[rows - 1 :, :]
    run_out[...] = running
    run_t_out[...] = running.T
    second.wait()
    factor = step_here[...] * jnp.exp2(last - running)
    total = jnp.broadcast_to(last, total_out.shape)
    factor_out[...] = factor
    total_out[...] = total
    half_states(half[0], x_here, b_here, copies, factor, total, out, matrix, dims)


def own_state_kernel(half, x, b, factor, total, out, matrix, x_here, b_here, sems, *, dims):
    copies = state_copies(half[0], x, b, x_here, b_here, sems, dims)
    for copy in copies:
        copy.start()
    half_spreader(matrix, x_here.shape[1] * CORES // factor.shape[1])
    half_states(half[0], x_here, b_here, copies, factor[...], total[...], out, matrix, dims)


def mixing_rows(first, own, got, states, cols):
    own_tail = own[states : states + 2, cols].astype(F32)
    got_tail = got[states : states + 2, cols].astype(F32)
    decay = jnp.where(first, got_tail, own_tail)
    decay = decay[:1, :] + decay[1:, :]
    one = jnp.ones_like(decay)
    return jnp.where(first, decay, one), jnp.where(first, one, decay)


def side_by_side(values, half):
    high, low = high_low(values)
    lane = lax.broadcasted_iota(jnp.int32, values.shape, 1)
    return jnp.where(lane < half, high, pltpu.roll(low, half, 1))


def chip_decay(first, got, total, states, base_out):
    heads = total.shape[1]
    half = heads // CORES
    partner = got[states + 2 : states + 3, :heads].astype(F32) + got[states + 3 : states + 4, :heads].astype(F32)
    partner = partner + got[states + 4 : states + 5, :heads].astype(F32)
    partner = jnp.broadcast_to(partner, total.shape)
    base_out[...] = jnp.where(first, jnp.zeros_like(partner), partner)
    both = jnp.exp2(total[...] + partner)
    both = jnp.where(first, both, pltpu.roll(both, half, 1))
    return side_by_side(both, half)


def chip_total_kernel(at, own, got, total, out, base_out):
    first = at[0] == 0
    cols = own.shape[1]
    states = out.shape[0]
    on_own, on_got = mixing_rows(first, own, got, states, slice(0, cols))
    for row in range(0, states, ROW_BLOCK):
        rows = slice(row, row + ROW_BLOCK)
        out[rows, :cols] = (on_own * own[rows, :].astype(F32) + on_got * got[rows, :].astype(F32)).astype(BF16)
    packed_decay = chip_decay(first, got, total, states, base_out)
    out[:, cols:] = jnp.concatenate([packed_decay] * (states // ROW_TILE), axis=0).astype(BF16)


def pieces_kernel(at, own, got, total, *outs, states, chunk):
    base_out = outs[-1]
    first = at[0] == 0
    rows, cols = outs[0].shape
    cols = cols - total.shape[1]
    here = slice(chunk * cols, (chunk + 1) * cols)
    on_own, on_got = mixing_rows(first, own, got, states, here)
    packed_decay = chip_decay(first, got, total, states, base_out)
    for k, out in enumerate(outs[:-1]):
        start = pl.multiple_of(jnp.bitwise_xor(at[1], k) * rows, rows)
        for row in range(0, rows, ROW_BLOCK):
            take = pl.ds(start + row, ROW_BLOCK)
            mixed = on_own * own[take, here].astype(F32) + on_got * got[take, here].astype(F32)
            out[row : row + ROW_BLOCK, :cols] = mixed.astype(BF16)
        out[:, cols:] = jnp.concatenate([packed_decay] * (rows // ROW_TILE), axis=0).astype(BF16)


def decays_of(pieces, cols, first_head, width):
    lanes = pieces[0].shape[1] - cols
    sent = [piece[:ROW_TILE, cols:].astype(F32)[:1, :] for piece in pieces]
    sent = jnp.concatenate(sent + [jnp.zeros((ROW_TILE - len(sent), lanes), F32)], axis=0)
    values = sent + pltpu.roll(sent, lanes // CORES, 1)
    heads = cols // width
    here = pltpu.roll(values, lanes - first_head, 1) if first_head else values
    return values, dot(packed(here, heads), spreader(heads, width))


def column_kernel(at, *refs, first_head, width, count):
    pieces, out, decay_out = refs[:count], refs[count], refs[count + 1]
    cols = decay_out.shape[1]
    rows = out.shape[0]
    values, decay = decays_of(pieces, cols, first_head, width)
    decay_out[...] = decay
    for place in range(count):

        @pl.when(at[1] == place)
        def _():
            state = jnp.zeros((rows, cols), F32)
            for k in range(count):
                k = k ^ place
                state = decay[k : k + 1, :] * state + pieces[k][:, :cols].astype(F32)
            out[:, :cols] = state.astype(BF16)

    fill_decay(out, cols, values, count)


def fill_decay(out, cols, values, count):
    product = values[:1, :]
    for k in range(1, count):
        product = product * values[k : k + 1, :]
    product = side_by_side(jnp.broadcast_to(product, (ROW_TILE, product.shape[1])), product.shape[1] // CORES)
    out[:, cols:] = jnp.concatenate([product] * (out.shape[0] // ROW_TILE), axis=0).astype(BF16)


def pair_kernel(at, mine, theirs, out, *, first_head, width, cols):
    odd = jnp.bitwise_and(at[2], 1) == 1
    values, decay = decays_of((mine, theirs), cols, first_head, width)
    one = jnp.ones_like(decay[:1, :])
    on_mine = jnp.where(odd, one, decay[1:2, :])
    on_theirs = jnp.where(odd, decay[:1, :], one)
    out[:, :cols] = (on_mine * mine[:, :cols].astype(F32) + on_theirs * theirs[:, :cols].astype(F32)).astype(BF16)
    fill_decay(out, cols, values, 2)


def chips_kernel(at, neighbour, lower_pair, decay, *refs, first_head, width, count):
    pieces, outs = refs[:count], refs[count:]
    _, cols = outs[0].shape
    odd = jnp.bitwise_and(at[2], 1) == 1
    late = at[2] >= 2
    _, passed = decays_of((neighbour,), cols, first_head, width)
    on_pair = jnp.where(late, jnp.where(odd, passed[:1, :], jnp.ones_like(passed[:1, :])), 0.0)
    carry = on_pair * lower_pair[:, :cols].astype(F32) + jnp.where(odd, neighbour[:, :cols].astype(F32), 0.0)
    for place in range(count):

        @pl.when(at[1] == place)
        def _():
            state = carry
            for k in range(count):
                k = k ^ place
                outs[k][...] = state.astype(BF16)
                state = decay[k : k + 1, :] * state + pieces[k][:, :cols].astype(F32)


def assemble_kernel(at, *refs, count):
    out = refs[-1]
    for n, piece in enumerate(refs[:-1]):
        rows, cols = piece.shape
        start = pl.multiple_of(jnp.bitwise_xor(at[1], n % count) * rows, rows)
        out[pl.ds(start, rows), n // count * cols : (n // count + 1) * cols] = piece[...]


def prefix_kernel(sent, out, here, sems, *, width, blocks):
    chips, rows, cols = here.shape
    heads = sent.shape[2] - cols
    half = heads // CORES
    step = cols // blocks
    first_rows = jnp.concatenate([sent[k, :1, cols:].astype(F32) for k in range(chips)], axis=0)
    values = first_rows + pltpu.roll(first_rows, half, 1)
    matrix = spreader(step // width, width)
    copies = []
    for block in range(blocks):
        lanes = slice(block * step, (block + 1) * step)
        head = block * step // width
        decay = dot(packed(pltpu.roll(values, heads - head, 1) if head else values, step // width), matrix)
        state = jnp.zeros((rows, step), F32)
        for k in range(chips):
            here[k, :, lanes] = state.astype(BF16)
            state = decay[k : k + 1, :] * state + sent[k, :, lanes].astype(F32)
        copies.append(
            pltpu.make_async_copy(
                here.at[:, :, pl.ds(block * step, step)], out.at[:, :, pl.ds(block * step, step)], sems.at[block]
            )
        )
        copies[-1].start()
    for copy in copies:
        copy.wait()


def within_kernel(
    at, x_ref, b_ref, c_ref, step_ref, run_ref, run_t_ref, skip_ref, before_ref, out, matrix, *, dims
):
    per_half, per_group, width = dims
    turn = pl.program_id(0)
    group = at[0] * per_half + turn
    head = group * per_group
    rows = x_ref.shape[0]
    pair = LANES // width

    @pl.when(turn == 0)
    def _():
        matrix[...] = spreader(per_group, width)

    def spread(values):
        return dot(packed(values, per_group), matrix[...])

    step = group_first(step_ref[...], head)
    run = group_first(run_ref[...], head)
    skip = group_first(jnp.broadcast_to(skip_ref[...], (ROW_TILE, skip_ref.shape[1])), head)
    run_t = run_t_ref[pl.ds(pl.multiple_of(head, per_group), per_group), :]
    x = x_ref[...].astype(F32)
    scaled = (x * spread(step)).astype(BF16)
    before = dot(c_ref[...], before_ref[...] * at[1].astype(BF16))
    outer = spread(skip)[:1, :] * x + spread(jnp.exp2(run)) * before
    lane = lax.broadcasted_iota(jnp.int32, (HALF_ROWS, LANES), 1) // width
    lower = lax.broadcasted_iota(jnp.int32, (HALF_ROWS, HALF_ROWS), 1) <= lax.broadcasted_iota(
        jnp.int32, (HALF_ROWS, HALF_ROWS), 0
    )
    b = b_ref[...]
    c = c_ref[...]
    for start in range(0, rows, HALF_ROWS):
        stop = start + HALF_ROWS
        scores = jnp.where(lower, dot(c[start:stop, :], b[start:stop, :], (1, 1)), 0.0)
        added = outer[start:stop, :]
        if start:
            edge = run[start - 1 : start, :]
            lead = spread(step[:start, :] * jnp.exp2(edge - run[:start, :]))
            lead = (x[:start, :] * lead).astype(BF16)
            cross = dot(c[start:stop, :], b[:start, :], (1, 1)).astype(BF16)
            added = added + spread(jnp.exp2(run[start:stop, :] - edge)) * dot(cross, lead)
        for first in range(0, per_group, pair):
            cols = slice(first * width, (first + pair) * width)
            here = scaled[start:stop, cols]
            weights = []
            values = []
            for k in range(pair):
                at = first + k
                gap = run[start:stop, at : at + 1] - run_t[at : at + 1, start:stop]
                weights.append((scores * jnp.exp2(jnp.minimum(gap, 0.0))).astype(BF16))
                values.append(jnp.where(lane == k, here, jnp.zeros_like(here)))
            part = dot(jnp.concatenate(weights, axis=1), jnp.concatenate(values, axis=0))
            out[start:stop, cols] = (added[:, cols] + part).astype(BF16)


def add_carried(half, within, rows_c, state, run, base, out, result, matrix, sems, dims):
    per_half, group_cols, _ = dims
    operand = packed_half(jnp.exp2(run[...] + base[:1, :]), half)
    copies = []
    for k in range(per_half):
        rows = rows_c(k)
        part = within(k)
        tiles = group_cols // TILE
        products = {}
        for n in range(tiles + AHEAD):
            if n < tiles:
                cols = slice(k * group_cols + n * TILE, k * group_cols + (n + 1) * TILE)
                products[n] = dot(rows, state[:, cols]), dot(operand, matrix[:, cols])
            m = n - AHEAD
            if m >= 0:
                cols = slice(k * group_cols + m * TILE, k * group_cols + (m + 1) * TILE)
                carried, factor = products.pop(m)
                result[:, cols] = (part[:, m * TILE : (m + 1) * TILE].astype(F32) + factor * carried).astype(BF16)
        home = pl.multiple_of((half * per_half + k) * group_cols, group_cols)
        copies.append(
            pltpu.make_async_copy(
                result.at[:, pl.ds(k * group_cols, group_cols)], out.at[:, pl.ds(home, group_cols)], sems.at[k]
            )
        )
        copies[-1].start()
    for copy in copies:
        copy.wait()


def final_kernel(half, within, c, state, run, base, matrix, filled, out, result, stores, *, dims):
    del filled
    per_half, group_cols, states = dims

    def part(k):
        return within[:, k * group_cols : (k + 1) * group_cols]

    def rows_c(k):
        return c[:, pl.ds(pl.multiple_of((half[0] * per_half + k) * states, states), states)]

    add_carried(half[0], part, rows_c, state, run, base, out, result, matrix, stores, dims)


def first_final_kernel(half, within, c, state, run, base, matrix, out, result, stores, *, dims):
    final_kernel(half, within, c, state, run, base, matrix, None, out, result, stores, dims=dims)


def small_call(kernel, in_specs, out_shape, scratch=(), out_specs=None):
    return pl.pallas_call(
        kernel,
        in_specs=in_specs,
        out_specs=out_specs or [pl.BlockSpec(memory_space=pltpu.VMEM)] * len(out_shape),
        out_shape=out_shape,
        scratch_shapes=list(scratch),
        compiler_params=plain_params(),
    )


def xor_route(size, k):
    return [(i, i ^ k) for i in range(size)]


def swapped(arrays, axis):
    size = lax.axis_size(axis)
    order = sorted(range(1, size), key=lambda k: -(k.bit_length()))
    done = {0: arrays[0]}
    for k in order:
        done[k] = lax.ppermute(arrays[k], axis, xor_route(size, k))
    return [done[k] for k in range(size)]


def entering_by_swaps(at, own, got, total, width, states, outer_axis, chip_axis):
    half_cols = own.shape[1]
    heads = total.shape[1]
    count = lax.axis_size(chip_axis)
    rows = states // count
    cols = half_cols // CHUNKS
    smem = pl.BlockSpec(memory_space=pltpu.SMEM)
    vmem = pl.BlockSpec(memory_space=pltpu.VMEM)
    shape = jax.ShapeDtypeStruct
    gathered = []
    for chunk in range(CHUNKS):
        *pieces, base = small_call(
            functools.partial(pieces_kernel, states=states, chunk=chunk),
            [smem] + [vmem] * 3,
            [shape((rows, cols + heads), BF16)] * count + [shape((ROW_TILE, heads), F32)],
        )(at, own, got, total)
        gathered.append(swapped(pieces, chip_axis))
    entering = []
    for chunk in range(CHUNKS):
        first_head = chunk * cols // width
        pieces = gathered[chunk]
        column, decay = small_call(
            functools.partial(column_kernel, first_head=first_head, width=width, count=count),
            [smem] + [vmem] * count,
            [shape((rows, cols + heads), BF16), shape((ROW_TILE, cols), F32)],
        )(at, *pieces)
        neighbour = lax.ppermute(column, outer_axis, xor_route(4, 1))
        (pair,) = small_call(
            functools.partial(pair_kernel, first_head=first_head, width=width, cols=cols),
            [smem] + [vmem] * 2,
            [shape((rows, cols + heads), BF16)],
        )(at, column, neighbour)
        pair = lax.ppermute(pair, outer_axis, xor_route(4, 2))
        states_out = small_call(
            functools.partial(chips_kernel, first_head=first_head, width=width, count=count),
            [smem] + [vmem] * (count + 3),
            [shape((rows, cols), BF16)] * count,
        )(at, neighbour, pair, decay, *pieces)
        entering += swapped(states_out, chip_axis)
    (entering,) = small_call(
        functools.partial(assemble_kernel, count=count),
        [smem] + [vmem] * len(entering),
        [shape((states, half_cols), BF16)],
    )(at, *entering)
    return entering, base


def entering_by_all_to_all(at, own, got, total, width, states, outer_axis, chip_axis):
    half_cols = own.shape[1]
    heads = total.shape[1]
    chips = lax.axis_size((outer_axis, chip_axis))
    rows = states // chips
    smem = pl.BlockSpec(memory_space=pltpu.SMEM)
    vmem = pl.BlockSpec(memory_space=pltpu.VMEM)
    chip_total, base = small_call(
        chip_total_kernel,
        [smem] + [vmem] * 3,
        [jax.ShapeDtypeStruct((states, half_cols + heads), BF16), jax.ShapeDtypeStruct((ROW_TILE, heads), F32)],
    )(at, own, got, total)
    sent = lax.all_to_all(
        chip_total.reshape(chips, rows, half_cols + heads),
        (outer_axis, chip_axis),
        split_axis=0,
        concat_axis=0,
        tiled=True,
    )
    blocks = GROUPS // CORES
    (entering,) = small_call(
        functools.partial(prefix_kernel, width=width, blocks=blocks),
        [vmem],
        [pltpu.HBM((chips, rows, half_cols), BF16)],
        [pltpu.VMEM((chips, rows, half_cols), BF16), pltpu.SemaphoreType.DMA((blocks,))],
        [pl.BlockSpec(memory_space=pltpu.HBM)],
    )(sent)
    entering = lax.all_to_all(entering, (outer_axis, chip_axis), split_axis=0, concat_axis=0, tiled=True)
    return entering.reshape(states, half_cols), base


def local(inputs, step_size, log_decay, b_matrix, c_matrix, skip_gain, *, outer_axis, chip_axis, core_axis):
    tokens, channels = inputs.shape
    heads = step_size.shape[1]
    width = channels // heads
    states = b_matrix.shape[1] // GROUPS
    per_group = heads // GROUPS
    group_cols = per_group * width
    per_half = GROUPS // CORES
    half_cols = channels // CORES
    chips = lax.axis_size((outer_axis, chip_axis))
    by_swaps = lax.axis_size(outer_axis) == 4 and chips == 16
    tall = states + ROW_TILE

    core = lax.axis_index(core_axis).astype(jnp.int32)
    mine = core.reshape(1)
    other = (1 - core).reshape(1)
    at = jnp.stack([core, lax.axis_index(chip_axis).astype(jnp.int32), lax.axis_index(outer_axis).astype(jnp.int32)])

    smem = pl.BlockSpec(memory_space=pltpu.SMEM)
    vmem = pl.BlockSpec(memory_space=pltpu.VMEM)
    hbm = pl.BlockSpec(memory_space=pltpu.HBM)

    def whole(shape):
        return pl.BlockSpec(shape, lambda i, *_: (0,) * len(shape))

    def by_group(cols):
        return pl.BlockSpec((tokens, cols), lambda i, at: (0, at[0] * per_half + i))

    state_dims = (per_half, group_cols, states)
    half_dims = (per_half, per_group, width)
    half_scratch = [
        pltpu.VMEM((tokens, half_cols), BF16),
        pltpu.VMEM((tokens, per_half * states), BF16),
    ]

    inputs, step_size, log_decay, b_matrix = (
        pltpu.with_memory_space_constraint(array, pltpu.HBM) for array in (inputs, step_size, log_decay, b_matrix)
    )
    send, run, run_t, factor, total = pl.pallas_call(
        functools.partial(send_state_kernel, dims=state_dims),
        in_specs=[smem, hbm, hbm, hbm, hbm],
        out_specs=[vmem] * 5,
        out_shape=[
            jax.ShapeDtypeStruct((tall, half_cols), BF16),
            jax.ShapeDtypeStruct((tokens, heads), F32),
            jax.ShapeDtypeStruct((heads, tokens), F32),
            jax.ShapeDtypeStruct((tokens, heads), F32),
            jax.ShapeDtypeStruct((ROW_TILE, heads), F32),
        ],
        scratch_shapes=half_scratch
        + [pltpu.VMEM((heads, half_cols), BF16)]
        + [pltpu.VMEM((tokens, heads), F32)] * 2
        + [pltpu.SemaphoreType.DMA((2 * per_half + 2,))],
        compiler_params=plain_params(),
        name="send_state",
    )(other, inputs, b_matrix, step_size, log_decay)

    swap = [(0, 1), (1, 0)]
    got = lax.ppermute(send, core_axis, swap)

    own, matrix = small_call(
        functools.partial(own_state_kernel, dims=state_dims),
        [smem, hbm, hbm, vmem, vmem],
        [jax.ShapeDtypeStruct((tall, half_cols), BF16), jax.ShapeDtypeStruct((heads, half_cols), BF16)],
        half_scratch + [pltpu.SemaphoreType.DMA((2 * per_half,))],
    )(mine, inputs, b_matrix, factor, total)

    find_entering = entering_by_swaps if by_swaps else entering_by_all_to_all
    entering, base = find_entering(at, own, got, total, width, states, outer_axis, chip_axis)
    late = lax.ppermute(own, core_axis, swap[:1])

    def within(half, before):
        return pl.pallas_call(
            functools.partial(within_kernel, dims=half_dims),
            grid_spec=pltpu.PrefetchScalarGridSpec(
                num_scalar_prefetch=1,
                grid=(per_half,),
                in_specs=[
                    by_group(group_cols),
                    by_group(states),
                    by_group(states),
                    whole((tokens, heads)),
                    whole((tokens, heads)),
                    whole((heads, tokens)),
                    whole((1, heads)),
                    pl.BlockSpec((states, group_cols), lambda i, at: (0, i)),
                ],
                out_specs=pl.BlockSpec((tokens, group_cols), lambda i, at: (0, i)),
                scratch_shapes=[pltpu.VMEM((2 * per_group, group_cols), BF16)],
            ),
            out_shape=jax.ShapeDtypeStruct((tokens, half_cols), BF16),
            compiler_params=params(),
            name="within",
        )(
            jnp.concatenate([half, mine]),
            inputs,
            b_matrix,
            c_matrix,
            step_size,
            run,
            run_t,
            skip_gain.reshape(1, heads),
            before,
        )

    own_within = within(mine, got)
    other_within = within(other, late)

    got_entering = lax.ppermute(entering, core_axis, swap)
    mixed = jax.ShapeDtypeStruct((tokens, channels), BF16)
    final_scratch = [pltpu.VMEM((tokens, half_cols), BF16), pltpu.SemaphoreType.DMA((per_half,))]
    (result,) = small_call(
        functools.partial(first_final_kernel, dims=state_dims), [smem] + [vmem] * 6, [mixed], final_scratch, [hbm]
    )(mine, own_within, c_matrix, entering, run, base, matrix)
    return pl.pallas_call(
        functools.partial(final_kernel, dims=state_dims),
        in_specs=[smem] + [vmem] * 6 + [hbm],
        out_specs=hbm,
        out_shape=mixed,
        scratch_shapes=final_scratch,
        input_output_aliases={7: 0},
        compiler_params=plain_params(),
        name="finish_other",
    )(other, other_within, c_matrix, got_entering, run, base, matrix, result)


def solution(mesh):
    outer, inner = mesh.axis_names
    chip_mesh = Mesh(
        mesh.devices.reshape(mesh.shape[outer], mesh.shape[inner] // CORES, CORES), (outer, "chip", "core")
    )
    placed = P((outer, "chip", "core"), None)

    def body(*args):
        return local(*args, outer_axis=outer, chip_axis="chip", core_axis="core")

    return jax.shard_map(body, mesh=chip_mesh, in_specs=(placed,) * 5 + (P(),), out_specs=placed, check_vma=False)
```

```python
import functools
import math

import jax
import jax.numpy as jnp
from jax import lax
from jax.experimental import pallas as pl
from jax.experimental.pallas import tpu as pltpu
from jax.sharding import Mesh, PartitionSpec as P


GROUPS = 8
CORES = 2
LANES = 128
TILE = 256
AHEAD = 2
CHUNKS = 2
PER_CALL = 2
ROW_TILE = 8
HALF_ROWS = 128
ROW_BLOCK = 16
VMEM_LIMIT = 24 * 1024 * 1024
LOG2E = 1.0 / math.log(2.0)

F32 = jnp.float32
BF16 = jnp.bfloat16


def dot(a, b, contract=(1, 0)):
    dims = (((contract[0],), (contract[1],)), ((), ()))
    return lax.dot_general(a, b, dims, preferred_element_type=F32)


def high_low(values):
    high = values.astype(BF16).astype(F32)
    return high, values - high


def spreader(heads, width):
    shape = (2 * heads, heads * width)
    row = lax.broadcasted_iota(jnp.int32, shape, 0)
    col = lax.broadcasted_iota(jnp.int32, shape, 1)
    row = jnp.where(row >= heads, row - heads, row)
    return jnp.where(row == col // width, 1.0, 0.0).astype(BF16)


def group_first(values, head):
    lanes = values.shape[1]
    return pltpu.roll(values, lax.rem(lanes - head, lanes), 1)


def packed(values, heads):
    high, low = high_low(values)
    lane = lax.broadcasted_iota(jnp.int32, values.shape, 1)
    return jnp.where(lane < heads, high, pltpu.roll(low, heads, 1)).astype(BF16)[:, : 2 * heads]


def half_spreader(matrix, width):
    lanes, cols = matrix.shape
    for start in range(0, cols, TILE):
        row = lax.broadcasted_iota(jnp.int32, (lanes, TILE), 0)
        col = start + lax.broadcasted_iota(jnp.int32, (lanes, TILE), 1)
        row = jnp.where(row >= lanes // 2, row - lanes // 2, row)
        matrix[:, start : start + TILE] = jnp.where(row == col // width, 1.0, 0.0).astype(BF16)


def packed_half(values, half):
    lanes = values.shape[1]
    values = group_first(values, half * (lanes // 2))
    high, low = high_low(values)
    lane = lax.broadcasted_iota(jnp.int32, values.shape, 1)
    return jnp.where(lane < lanes // 2, high, pltpu.roll(low, lanes // 2, 1)).astype(BF16)


def params():
    return pltpu.CompilerParams(dimension_semantics=("arbitrary",), vmem_limit_bytes=VMEM_LIMIT)


def plain_params():
    return pltpu.CompilerParams(vmem_limit_bytes=VMEM_LIMIT)


def state_copies(half, x, b, x_here, b_here, sems, dims):
    per_half, group_cols, states = dims
    copies = []
    for k in range(per_half):
        group = half * per_half + k
        copies.append(
            pltpu.make_async_copy(
                x.at[:, pl.ds(pl.multiple_of(group * group_cols, group_cols), group_cols)],
                x_here.at[:, pl.ds(k * group_cols, group_cols)],
                sems.at[2 * k],
            )
        )
        copies.append(
            pltpu.make_async_copy(
                b.at[:, pl.ds(pl.multiple_of(group * states, states), states)],
                b_here.at[:, pl.ds(k * states, states)],
                sems.at[2 * k + 1],
            )
        )
    return copies


def half_states(half, x_here, b_here, copies, factor, log_total, out, matrix, dims):
    _, group_cols, states = dims
    rows, heads = factor.shape
    row = lax.broadcasted_iota(jnp.int32, (ROW_TILE, TILE), 0)
    operand = packed_half(jnp.concatenate([factor, jnp.exp2(log_total)], axis=0), half)
    for copy in copies:
        copy.wait()
    tiles = out.shape[1] // TILE
    per_group = group_cols // TILE
    matrices = {}
    factors = {}
    scaled = {}
    for n in range(tiles + 2 * AHEAD):
        if n < tiles:
            factors[n] = dot(operand, matrix[:, n * TILE : (n + 1) * TILE])
        m = n - AHEAD
        if 0 <= m < tiles:
            cols = slice(m * TILE, (m + 1) * TILE)
            spread = factors.pop(m)
            scaled[m] = (x_here[:, cols].astype(F32) * spread[:rows, :]).astype(BF16)
            high, low = high_low(spread[rows:, :])
            tail = jnp.where(row == 0, high, low)
            if m == 0:
                high, low = high_low(log_total)
                middle, low = high_low(low)
                at = row[:, :heads]
                logs = jnp.where(at == 2, high, jnp.where(at == 3, middle, low))
                logs = jnp.where(at < 2, tail[:, :heads], logs)
                tail = jnp.concatenate([logs, tail[:, heads:]], axis=1)
            out[states:, cols] = tail.astype(BF16)
            if m % per_group == 0:
                k = m // per_group
                matrices[k] = b_here[:, k * states : (k + 1) * states].T
        m = n - 2 * AHEAD
        if m >= 0:
            out[:states, m * TILE : (m + 1) * TILE] = dot(matrices[m // per_group], scaled.pop(m)).astype(BF16)


def send_state_kernel(
    half,
    x,
    b,
    step,
    log,
    out,
    run_out,
    run_t_out,
    factor_out,
    total_out,
    x_here,
    b_here,
    matrix,
    step_here,
    log_here,
    sems,
    *,
    dims,
):
    first = pltpu.make_async_copy(log, log_here, sems.at[2 * dims[0]])
    second = pltpu.make_async_copy(step, step_here, sems.at[2 * dims[0] + 1])
    first.start()
    second.start()
    copies = state_copies(half[0], x, b, x_here, b_here, sems, dims)
    for copy in copies:
        copy.start()
    rows, heads = log_here.shape
    half_spreader(matrix, x_here.shape[1] * CORES // heads)
    upto = lax.broadcasted_iota(jnp.int32, (rows, rows), 1) <= lax.broadcasted_iota(jnp.int32, (rows, rows), 0)
    first.wait()
    high, rest = high_low(log_here[...])
    middle, low = high_low(rest)
    parts = jnp.concatenate([high, middle, low], axis=1).astype(BF16)
    sums = dot(jnp.where(upto, 1.0, 0.0).astype(BF16), parts)
    running = (sums[:, :heads] + sums[:, heads : 2 * heads] + sums[:, 2 * heads :]) * LOG2E
    last = running[rows - 1 :, :]
    run_out[...] = running
    run_t_out[...] = running.T
    second.wait()
    factor = step_here[...] * jnp.exp2(last - running)
    total = jnp.broadcast_to(last, total_out.shape)
    factor_out[...] = factor
    total_out[...] = total
    half_states(half[0], x_here, b_here, copies, factor, total, out, matrix, dims)


def own_state_kernel(half, x, b, factor, total, out, matrix, x_here, b_here, sems, *, dims):
    copies = state_copies(half[0], x, b, x_here, b_here, sems, dims)
    for copy in copies:
        copy.start()
    half_spreader(matrix, x_here.shape[1] * CORES // factor.shape[1])
    half_states(half[0], x_here, b_here, copies, factor[...], total[...], out, matrix, dims)


def mixing_rows(first, own, got, states, cols):
    own_tail = own[states : states + 2, cols].astype(F32)
    got_tail = got[states : states + 2, cols].astype(F32)
    decay = jnp.where(first, got_tail, own_tail)
    decay = decay[:1, :] + decay[1:, :]
    one = jnp.ones_like(decay)
    return jnp.where(first, decay, one), jnp.where(first, one, decay)


def side_by_side(values, half):
    high, low = high_low(values)
    lane = lax.broadcasted_iota(jnp.int32, values.shape, 1)
    return jnp.where(lane < half, high, pltpu.roll(low, half, 1))


def chip_decay(first, got, total, states, base_out):
    heads = total.shape[1]
    half = heads // CORES
    partner = got[states + 2 : states + 3, :heads].astype(F32) + got[states + 3 : states + 4, :heads].astype(F32)
    partner = partner + got[states + 4 : states + 5, :heads].astype(F32)
    partner = jnp.broadcast_to(partner, total.shape)
    base_out[...] = jnp.where(first, jnp.zeros_like(partner), partner)
    both = jnp.exp2(total[...] + partner)
    both = jnp.where(first, both, pltpu.roll(both, half, 1))
    return side_by_side(both, half)


def chip_total_kernel(at, own, got, total, out, base_out):
    first = at[0] == 0
    cols = own.shape[1]
    states = out.shape[0]
    on_own, on_got = mixing_rows(first, own, got, states, slice(0, cols))
    for row in range(0, states, ROW_BLOCK):
        rows = slice(row, row + ROW_BLOCK)
        out[rows, :cols] = (on_own * own[rows, :].astype(F32) + on_got * got[rows, :].astype(F32)).astype(BF16)
    packed_decay = chip_decay(first, got, total, states, base_out)
    out[:, cols:] = jnp.concatenate([packed_decay] * (states // ROW_TILE), axis=0).astype(BF16)


def pieces_kernel(at, own, got, total, *outs, states, chunk):
    base_out = outs[-1]
    first = at[0] == 0
    rows, cols = outs[0].shape
    cols = cols - total.shape[1]
    here = slice(chunk * cols, (chunk + 1) * cols)
    on_own, on_got = mixing_rows(first, own, got, states, here)
    packed_decay = chip_decay(first, got, total, states, base_out)
    for k, out in enumerate(outs[:-1]):
        start = pl.multiple_of(jnp.bitwise_xor(at[1], k) * rows, rows)
        for row in range(0, rows, ROW_BLOCK):
            take = pl.ds(start + row, ROW_BLOCK)
            mixed = on_own * own[take, here].astype(F32) + on_got * got[take, here].astype(F32)
            out[row : row + ROW_BLOCK, :cols] = mixed.astype(BF16)
        out[:, cols:] = jnp.concatenate([packed_decay] * (rows // ROW_TILE), axis=0).astype(BF16)


def decays_of(pieces, cols, first_head, width):
    lanes = pieces[0].shape[1] - cols
    sent = [piece[:ROW_TILE, cols:].astype(F32)[:1, :] for piece in pieces]
    sent = jnp.concatenate(sent + [jnp.zeros((ROW_TILE - len(sent), lanes), F32)], axis=0)
    values = sent + pltpu.roll(sent, lanes // CORES, 1)
    heads = cols // width
    here = pltpu.roll(values, lanes - first_head, 1) if first_head else values
    return values, dot(packed(here, heads), spreader(heads, width))


def column_kernel(at, *refs, first_head, width, count):
    pieces, out, decay_out = refs[:count], refs[count], refs[count + 1]
    cols = decay_out.shape[1]
    rows = out.shape[0]
    values, decay = decays_of(pieces, cols, first_head, width)
    decay_out[...] = decay
    for place in range(count):

        @pl.when(at[1] == place)
        def _():
            state = jnp.zeros((rows, cols), F32)
            for k in range(count):
                k = k ^ place
                state = decay[k : k + 1, :] * state + pieces[k][:, :cols].astype(F32)
            out[:, :cols] = state.astype(BF16)

    fill_decay(out, cols, values, count)


def fill_decay(out, cols, values, count):
    product = values[:1, :]
    for k in range(1, count):
        product = product * values[k : k + 1, :]
    product = side_by_side(jnp.broadcast_to(product, (ROW_TILE, product.shape[1])), product.shape[1] // CORES)
    out[:, cols:] = jnp.concatenate([product] * (out.shape[0] // ROW_TILE), axis=0).astype(BF16)


def pair_kernel(at, mine, theirs, out, *, first_head, width, cols):
    odd = jnp.bitwise_and(at[2], 1) == 1
    values, decay = decays_of((mine, theirs), cols, first_head, width)
    one = jnp.ones_like(decay[:1, :])
    on_mine = jnp.where(odd, one, decay[1:2, :])
    on_theirs = jnp.where(odd, decay[:1, :], one)
    out[:, :cols] = (on_mine * mine[:, :cols].astype(F32) + on_theirs * theirs[:, :cols].astype(F32)).astype(BF16)
    fill_decay(out, cols, values, 2)


def chips_kernel(at, neighbour, lower_pair, decay, *refs, first_head, width, count):
    pieces, outs = refs[:count], refs[count:]
    _, cols = outs[0].shape
    odd = jnp.bitwise_and(at[2], 1) == 1
    late = at[2] >= 2
    _, passed = decays_of((neighbour,), cols, first_head, width)
    on_pair = jnp.where(late, jnp.where(odd, passed[:1, :], jnp.ones_like(passed[:1, :])), 0.0)
    carry = on_pair * lower_pair[:, :cols].astype(F32) + jnp.where(odd, neighbour[:, :cols].astype(F32), 0.0)
    for place in range(count):

        @pl.when(at[1] == place)
        def _():
            state = carry
            for k in range(count):
                k = k ^ place
                outs[k][...] = state.astype(BF16)
                state = decay[k : k + 1, :] * state + pieces[k][:, :cols].astype(F32)


def assemble_kernel(at, *refs, count):
    out = refs[-1]
    for n, piece in enumerate(refs[:-1]):
        rows, cols = piece.shape
        start = pl.multiple_of(jnp.bitwise_xor(at[1], n % count) * rows, rows)
        out[pl.ds(start, rows), n // count * cols : (n // count + 1) * cols] = piece[...]


def prefix_kernel(sent, out, here, sems, *, width, blocks):
    chips, rows, cols = here.shape
    heads = sent.shape[2] - cols
    half = heads // CORES
    step = cols // blocks
    first_rows = jnp.concatenate([sent[k, :1, cols:].astype(F32) for k in range(chips)], axis=0)
    values = first_rows + pltpu.roll(first_rows, half, 1)
    matrix = spreader(step // width, width)
    copies = []
    for block in range(blocks):
        lanes = slice(block * step, (block + 1) * step)
        head = block * step // width
        decay = dot(packed(pltpu.roll(values, heads - head, 1) if head else values, step // width), matrix)
        state = jnp.zeros((rows, step), F32)
        for k in range(chips):
            here[k, :, lanes] = state.astype(BF16)
            state = decay[k : k + 1, :] * state + sent[k, :, lanes].astype(F32)
        copies.append(
            pltpu.make_async_copy(
                here.at[:, :, pl.ds(block * step, step)], out.at[:, :, pl.ds(block * step, step)], sems.at[block]
            )
        )
        copies[-1].start()
    for copy in copies:
        copy.wait()


def within_kernel(
    at, x_ref, b_ref, c_ref, step_ref, run_ref, run_t_ref, skip_ref, before_ref, out, matrix, *, dims
):
    per_half, per_group, width = dims
    turn = pl.program_id(0)
    group = at[0] * per_half + at[2] + turn
    head = group * per_group
    rows = x_ref.shape[0]
    pair = LANES // width

    @pl.when(turn == 0)
    def _():
        matrix[...] = spreader(per_group, width)

    def spread(values):
        return dot(packed(values, per_group), matrix[...])

    step = group_first(step_ref[...], head)
    run = group_first(run_ref[...], head)
    skip = group_first(jnp.broadcast_to(skip_ref[...], (ROW_TILE, skip_ref.shape[1])), head)
    run_t = run_t_ref[pl.ds(pl.multiple_of(head, per_group), per_group), :]
    x = x_ref[...].astype(F32)
    scaled = (x * spread(step)).astype(BF16)
    before = dot(c_ref[...], before_ref[...] * at[1].astype(BF16))
    outer = spread(skip)[:1, :] * x + spread(jnp.exp2(run)) * before
    lane = lax.broadcasted_iota(jnp.int32, (HALF_ROWS, LANES), 1) // width
    lower = lax.broadcasted_iota(jnp.int32, (HALF_ROWS, HALF_ROWS), 1) <= lax.broadcasted_iota(
        jnp.int32, (HALF_ROWS, HALF_ROWS), 0
    )
    b = b_ref[...]
    c = c_ref[...]
    for start in range(0, rows, HALF_ROWS):
        stop = start + HALF_ROWS
        scores = jnp.where(lower, dot(c[start:stop, :], b[start:stop, :], (1, 1)), 0.0)
        added = outer[start:stop, :]
        if start:
            edge = run[start - 1 : start, :]
            lead = spread(step[:start, :] * jnp.exp2(edge - run[:start, :]))
            lead = (x[:start, :] * lead).astype(BF16)
            cross = dot(c[start:stop, :], b[:start, :], (1, 1)).astype(BF16)
            added = added + spread(jnp.exp2(run[start:stop, :] - edge)) * dot(cross, lead)
        for first in range(0, per_group, pair):
            cols = slice(first * width, (first + pair) * width)
            here = scaled[start:stop, cols]
            weights = []
            values = []
            for k in range(pair):
                at = first + k
                gap = run[start:stop, at : at + 1] - run_t[at : at + 1, start:stop]
                weights.append((scores * jnp.exp2(jnp.minimum(gap, 0.0))).astype(BF16))
                values.append(jnp.where(lane == k, here, jnp.zeros_like(here)))
            part = dot(jnp.concatenate(weights, axis=1), jnp.concatenate(values, axis=0))
            out[start:stop, cols] = (added[:, cols] + part).astype(BF16)


def add_carried(half, within, rows_c, state, run, base, out, result, matrix, sems, dims):
    per_half, group_cols, _ = dims
    operand = packed_half(jnp.exp2(run[...] + base[:1, :]), half)
    copies = []
    for k in range(per_half):
        rows = rows_c(k)
        part = within(k)
        tiles = group_cols // TILE
        products = {}
        for n in range(tiles + AHEAD):
            if n < tiles:
                cols = slice(k * group_cols + n * TILE, k * group_cols + (n + 1) * TILE)
                products[n] = dot(rows, state[:, cols]), dot(operand, matrix[:, cols])
            m = n - AHEAD
            if m >= 0:
                cols = slice(k * group_cols + m * TILE, k * group_cols + (m + 1) * TILE)
                carried, factor = products.pop(m)
                result[:, cols] = (part[:, m * TILE : (m + 1) * TILE].astype(F32) + factor * carried).astype(BF16)
        home = pl.multiple_of((half * per_half + k) * group_cols, group_cols)
        copies.append(
            pltpu.make_async_copy(
                result.at[:, pl.ds(k * group_cols, group_cols)], out.at[:, pl.ds(home, group_cols)], sems.at[k]
            )
        )
        copies[-1].start()
    for copy in copies:
        copy.wait()


def final_kernel(half, c, state, run, base, matrix, *refs, dims, parts):
    within = refs[:parts]
    out, result, stores = refs[-3:]
    per_half, group_cols, states = dims
    each = per_half // parts

    def part(k):
        return within[k // each][:, k % each * group_cols : (k % each + 1) * group_cols]

    def rows_c(k):
        return c[:, pl.ds(pl.multiple_of((half[0] * per_half + k) * states, states), states)]

    add_carried(half[0], part, rows_c, state, run, base, out, result, matrix, stores, dims)


def small_call(kernel, in_specs, out_shape, scratch=(), out_specs=None):
    return pl.pallas_call(
        kernel,
        in_specs=in_specs,
        out_specs=out_specs or [pl.BlockSpec(memory_space=pltpu.VMEM)] * len(out_shape),
        out_shape=out_shape,
        scratch_shapes=list(scratch),
        compiler_params=plain_params(),
    )


def xor_route(size, k):
    return [(i, i ^ k) for i in range(size)]


def swapped(arrays, axis):
    size = lax.axis_size(axis)
    done = {0: arrays[0]}
    for k in range(1, size):
        done[k] = lax.ppermute(arrays[k], axis, xor_route(size, k))
    return [done[k] for k in range(size)]


def entering_by_swaps(at, own, got, total, width, states, outer_axis, chip_axis):
    half_cols = own.shape[1]
    heads = total.shape[1]
    count = lax.axis_size(chip_axis)
    rows = states // count
    cols = half_cols // CHUNKS
    smem = pl.BlockSpec(memory_space=pltpu.SMEM)
    vmem = pl.BlockSpec(memory_space=pltpu.VMEM)
    shape = jax.ShapeDtypeStruct
    gathered = []
    for chunk in range(CHUNKS):
        *pieces, base = small_call(
            functools.partial(pieces_kernel, states=states, chunk=chunk),
            [smem] + [vmem] * 3,
            [shape((rows, cols + heads), BF16)] * count + [shape((ROW_TILE, heads), F32)],
        )(at, own, got, total)
        gathered.append(swapped(pieces, chip_axis))
    entering = []
    for chunk in range(CHUNKS):
        first_head = chunk * cols // width
        pieces = gathered[chunk]
        column, decay = small_call(
            functools.partial(column_kernel, first_head=first_head, width=width, count=count),
            [smem] + [vmem] * count,
            [shape((rows, cols + heads), BF16), shape((ROW_TILE, cols), F32)],
        )(at, *pieces)
        neighbour = lax.ppermute(column, outer_axis, xor_route(4, 1))
        (pair,) = small_call(
            functools.partial(pair_kernel, first_head=first_head, width=width, cols=cols),
            [smem] + [vmem] * 2,
            [shape((rows, cols + heads), BF16)],
        )(at, column, neighbour)
        pair = lax.ppermute(pair, outer_axis, xor_route(4, 2))
        states_out = small_call(
            functools.partial(chips_kernel, first_head=first_head, width=width, count=count),
            [smem] + [vmem] * (count + 3),
            [shape((rows, cols), BF16)] * count,
        )(at, neighbour, pair, decay, *pieces)
        entering += swapped(states_out, chip_axis)
    (entering,) = small_call(
        functools.partial(assemble_kernel, count=count),
        [smem] + [vmem] * len(entering),
        [shape((states, half_cols), BF16)],
    )(at, *entering)
    return entering, base


def entering_by_all_to_all(at, own, got, total, width, states, outer_axis, chip_axis):
    half_cols = own.shape[1]
    heads = total.shape[1]
    chips = lax.axis_size((outer_axis, chip_axis))
    rows = states // chips
    smem = pl.BlockSpec(memory_space=pltpu.SMEM)
    vmem = pl.BlockSpec(memory_space=pltpu.VMEM)
    chip_total, base = small_call(
        chip_total_kernel,
        [smem] + [vmem] * 3,
        [jax.ShapeDtypeStruct((states, half_cols + heads), BF16), jax.ShapeDtypeStruct((ROW_TILE, heads), F32)],
    )(at, own, got, total)
    sent = lax.all_to_all(
        chip_total.reshape(chips, rows, half_cols + heads),
        (outer_axis, chip_axis),
        split_axis=0,
        concat_axis=0,
        tiled=True,
    )
    blocks = GROUPS // CORES
    (entering,) = small_call(
        functools.partial(prefix_kernel, width=width, blocks=blocks),
        [vmem],
        [pltpu.HBM((chips, rows, half_cols), BF16)],
        [pltpu.VMEM((chips, rows, half_cols), BF16), pltpu.SemaphoreType.DMA((blocks,))],
        [pl.BlockSpec(memory_space=pltpu.HBM)],
    )(sent)
    entering = lax.all_to_all(entering, (outer_axis, chip_axis), split_axis=0, concat_axis=0, tiled=True)
    return entering.reshape(states, half_cols), base


def local(inputs, step_size, log_decay, b_matrix, c_matrix, skip_gain, *, outer_axis, chip_axis, core_axis):
    tokens, channels = inputs.shape
    heads = step_size.shape[1]
    width = channels // heads
    states = b_matrix.shape[1] // GROUPS
    per_group = heads // GROUPS
    group_cols = per_group * width
    per_half = GROUPS // CORES
    half_cols = channels // CORES
    chips = lax.axis_size((outer_axis, chip_axis))
    by_swaps = lax.axis_size(outer_axis) == 4 and chips == 16
    tall = states + ROW_TILE

    core = lax.axis_index(core_axis).astype(jnp.int32)
    mine = core.reshape(1)
    other = (1 - core).reshape(1)
    at = jnp.stack([core, lax.axis_index(chip_axis).astype(jnp.int32), lax.axis_index(outer_axis).astype(jnp.int32)])

    smem = pl.BlockSpec(memory_space=pltpu.SMEM)
    vmem = pl.BlockSpec(memory_space=pltpu.VMEM)
    hbm = pl.BlockSpec(memory_space=pltpu.HBM)

    def whole(shape):
        return pl.BlockSpec(shape, lambda i, *_: (0,) * len(shape))

    def by_group(cols):
        return pl.BlockSpec((tokens, cols), lambda i, at: (0, at[0] * per_half + at[2] + i))

    state_dims = (per_half, group_cols, states)
    half_dims = (per_half, per_group, width)
    half_scratch = [
        pltpu.VMEM((tokens, half_cols), BF16),
        pltpu.VMEM((tokens, per_half * states), BF16),
    ]

    inputs, step_size, log_decay, b_matrix = (
        pltpu.with_memory_space_constraint(array, pltpu.HBM) for array in (inputs, step_size, log_decay, b_matrix)
    )
    send, run, run_t, factor, total = pl.pallas_call(
        functools.partial(send_state_kernel, dims=state_dims),
        in_specs=[smem, hbm, hbm, hbm, hbm],
        out_specs=[vmem] * 5,
        out_shape=[
            jax.ShapeDtypeStruct((tall, half_cols), BF16),
            jax.ShapeDtypeStruct((tokens, heads), F32),
            jax.ShapeDtypeStruct((heads, tokens), F32),
            jax.ShapeDtypeStruct((tokens, heads), F32),
            jax.ShapeDtypeStruct((ROW_TILE, heads), F32),
        ],
        scratch_shapes=half_scratch
        + [pltpu.VMEM((heads, half_cols), BF16)]
        + [pltpu.VMEM((tokens, heads), F32)] * 2
        + [pltpu.SemaphoreType.DMA((2 * per_half + 2,))],
        compiler_params=plain_params(),
        name="send_state",
    )(other, inputs, b_matrix, step_size, log_decay)

    swap = [(0, 1), (1, 0)]
    got = lax.ppermute(send, core_axis, swap)

    own, matrix = small_call(
        functools.partial(own_state_kernel, dims=state_dims),
        [smem, hbm, hbm, vmem, vmem],
        [jax.ShapeDtypeStruct((tall, half_cols), BF16), jax.ShapeDtypeStruct((heads, half_cols), BF16)],
        half_scratch + [pltpu.SemaphoreType.DMA((2 * per_half,))],
    )(mine, inputs, b_matrix, factor, total)

    find_entering = entering_by_swaps if by_swaps else entering_by_all_to_all
    entering, base = find_entering(at, own, got, total, width, states, outer_axis, chip_axis)
    late = lax.ppermute(own, core_axis, swap[:1])

    def within(half, before, first):
        return pl.pallas_call(
            functools.partial(within_kernel, dims=half_dims),
            grid_spec=pltpu.PrefetchScalarGridSpec(
                num_scalar_prefetch=1,
                grid=(PER_CALL,),
                in_specs=[
                    by_group(group_cols),
                    by_group(states),
                    by_group(states),
                    whole((tokens, heads)),
                    whole((tokens, heads)),
                    whole((heads, tokens)),
                    whole((1, heads)),
                    pl.BlockSpec((states, group_cols), lambda i, at: (0, at[2] + i)),
                ],
                out_specs=pl.BlockSpec((tokens, group_cols), lambda i, at: (0, i)),
                scratch_shapes=[pltpu.VMEM((2 * per_group, group_cols), BF16)],
            ),
            out_shape=jax.ShapeDtypeStruct((tokens, PER_CALL * group_cols), BF16),
            compiler_params=params(),
            name="within",
        )(
            jnp.concatenate([half, mine, jnp.full((1,), first, jnp.int32)]),
            inputs,
            b_matrix,
            c_matrix,
            step_size,
            run,
            run_t,
            skip_gain.reshape(1, heads),
            before,
        )

    own_within = []
    other_within = []
    for first in range(0, per_half, PER_CALL):
        own_within.append(within(mine, got, first))
        other_within.append(within(other, late, first))

    got_entering = lax.ppermute(entering, core_axis, swap)
    mixed = jax.ShapeDtypeStruct((tokens, channels), BF16)
    final_scratch = [pltpu.VMEM((tokens, half_cols), BF16), pltpu.SemaphoreType.DMA((per_half,))]
    parts = len(own_within)
    final = functools.partial(final_kernel, dims=state_dims, parts=parts)
    (result,) = small_call(
        final, [smem] + [vmem] * (5 + parts), [mixed], final_scratch, [hbm]
    )(mine, c_matrix, entering, run, base, matrix, *own_within)
    return pl.pallas_call(
        final,
        in_specs=[smem] + [vmem] * (5 + parts) + [hbm],
        out_specs=hbm,
        out_shape=mixed,
        scratch_shapes=final_scratch,
        input_output_aliases={6 + parts: 0},
        compiler_params=plain_params(),
        name="finish_other",
    )(other, c_matrix, got_entering, run, base, matrix, *other_within, result)


def solution(mesh):
    outer, inner = mesh.axis_names
    chip_mesh = Mesh(
        mesh.devices.reshape(mesh.shape[outer], mesh.shape[inner] // CORES, CORES), (outer, "chip", "core")
    )
    placed = P((outer, "chip", "core"), None)

    def body(*args):
        return local(*args, outer_axis=outer, chip_axis="chip", core_axis="core")

    return jax.shard_map(body, mesh=chip_mesh, in_specs=(placed,) * 5 + (P(),), out_specs=placed, check_vma=False)
```

```python
import functools
import math

import jax
import jax.numpy as jnp
from jax import lax
from jax.experimental import pallas as pl
from jax.experimental.pallas import tpu as pltpu
from jax.sharding import Mesh, PartitionSpec as P


GROUPS = 8
CORES = 2
LANES = 128
TILE = 256
AHEAD = 2
CHUNKS = 2
PER_CALL = 2
ROW_TILE = 8
HALF_ROWS = 128
ROW_BLOCK = 16
VMEM_LIMIT = 24 * 1024 * 1024
LOG2E = 1.0 / math.log(2.0)

F32 = jnp.float32
BF16 = jnp.bfloat16


def dot(a, b, contract=(1, 0)):
    dims = (((contract[0],), (contract[1],)), ((), ()))
    return lax.dot_general(a, b, dims, preferred_element_type=F32)


def high_low(values):
    high = values.astype(BF16).astype(F32)
    return high, values - high


def spreader(heads, width):
    shape = (2 * heads, heads * width)
    row = lax.broadcasted_iota(jnp.int32, shape, 0)
    col = lax.broadcasted_iota(jnp.int32, shape, 1)
    row = jnp.where(row >= heads, row - heads, row)
    return jnp.where(row == col // width, 1.0, 0.0).astype(BF16)


def group_first(values, head):
    lanes = values.shape[1]
    return pltpu.roll(values, lax.rem(lanes - head, lanes), 1)


def packed(values, heads):
    high, low = high_low(values)
    lane = lax.broadcasted_iota(jnp.int32, values.shape, 1)
    return jnp.where(lane < heads, high, pltpu.roll(low, heads, 1)).astype(BF16)[:, : 2 * heads]


def half_spreader(matrix, width):
    lanes, cols = matrix.shape
    for start in range(0, cols, TILE):
        row = lax.broadcasted_iota(jnp.int32, (lanes, TILE), 0)
        col = start + lax.broadcasted_iota(jnp.int32, (lanes, TILE), 1)
        row = jnp.where(row >= lanes // 2, row - lanes // 2, row)
        matrix[:, start : start + TILE] = jnp.where(row == col // width, 1.0, 0.0).astype(BF16)


def packed_half(values, half):
    lanes = values.shape[1]
    values = group_first(values, half * (lanes // 2))
    high, low = high_low(values)
    lane = lax.broadcasted_iota(jnp.int32, values.shape, 1)
    return jnp.where(lane < lanes // 2, high, pltpu.roll(low, lanes // 2, 1)).astype(BF16)


def params():
    return pltpu.CompilerParams(dimension_semantics=("arbitrary",), vmem_limit_bytes=VMEM_LIMIT)


def plain_params():
    return pltpu.CompilerParams(vmem_limit_bytes=VMEM_LIMIT)


def state_copies(half, x, b, x_here, b_here, sems, dims):
    per_half, group_cols, states = dims
    copies = []
    for k in range(per_half):
        group = half * per_half + k
        copies.append(
            pltpu.make_async_copy(
                x.at[:, pl.ds(pl.multiple_of(group * group_cols, group_cols), group_cols)],
                x_here.at[:, pl.ds(k * group_cols, group_cols)],
                sems.at[2 * k],
            )
        )
        copies.append(
            pltpu.make_async_copy(
                b.at[:, pl.ds(pl.multiple_of(group * states, states), states)],
                b_here.at[:, pl.ds(k * states, states)],
                sems.at[2 * k + 1],
            )
        )
    return copies


def half_states(half, x_here, b_here, copies, factor, log_total, out, matrix, dims):
    _, group_cols, states = dims
    rows, heads = factor.shape
    row = lax.broadcasted_iota(jnp.int32, (ROW_TILE, TILE), 0)
    operand = packed_half(jnp.concatenate([factor, jnp.exp2(log_total)], axis=0), half)
    for copy in copies:
        copy.wait()
    tiles = out.shape[1] // TILE
    per_group = group_cols // TILE
    matrices = {}
    factors = {}
    scaled = {}
    for n in range(tiles + 2 * AHEAD):
        if n < tiles:
            factors[n] = dot(operand, matrix[:, n * TILE : (n + 1) * TILE])
        m = n - AHEAD
        if 0 <= m < tiles:
            cols = slice(m * TILE, (m + 1) * TILE)
            spread = factors.pop(m)
            scaled[m] = (x_here[:, cols].astype(F32) * spread[:rows, :]).astype(BF16)
            high, low = high_low(spread[rows:, :])
            tail = jnp.where(row == 0, high, low)
            if m == 0:
                high, low = high_low(log_total)
                middle, low = high_low(low)
                at = row[:, :heads]
                logs = jnp.where(at == 2, high, jnp.where(at == 3, middle, low))
                logs = jnp.where(at < 2, tail[:, :heads], logs)
                tail = jnp.concatenate([logs, tail[:, heads:]], axis=1)
            out[states:, cols] = tail.astype(BF16)
            if m % per_group == 0:
                k = m // per_group
                matrices[k] = b_here[:, k * states : (k + 1) * states].T
        m = n - 2 * AHEAD
        if m >= 0:
            out[:states, m * TILE : (m + 1) * TILE] = dot(matrices[m // per_group], scaled.pop(m)).astype(BF16)


def send_state_kernel(
    half,
    chip,
    outer,
    x,
    b,
    step,
    log,
    out,
    run_out,
    run_t_out,
    factor_out,
    total_out,
    x_here,
    b_here,
    matrix,
    step_here,
    log_here,
    sems,
    *,
    dims,
):
    del chip, outer
    first = pltpu.make_async_copy(log, log_here, sems.at[2 * dims[0]])
    second = pltpu.make_async_copy(step, step_here, sems.at[2 * dims[0] + 1])
    first.start()
    second.start()
    copies = state_copies(half[0], x, b, x_here, b_here, sems, dims)
    for copy in copies:
        copy.start()
    rows, heads = log_here.shape
    half_spreader(matrix, x_here.shape[1] * CORES // heads)
    upto = lax.broadcasted_iota(jnp.int32, (rows, rows), 1) <= lax.broadcasted_iota(jnp.int32, (rows, rows), 0)
    first.wait()
    high, rest = high_low(log_here[...])
    middle, low = high_low(rest)
    parts = jnp.concatenate([high, middle, low], axis=1).astype(BF16)
    sums = dot(jnp.where(upto, 1.0, 0.0).astype(BF16), parts)
    running = (sums[:, :heads] + sums[:, heads : 2 * heads] + sums[:, 2 * heads :]) * LOG2E
    last = running[rows - 1 :, :]
    run_out[...] = running
    run_t_out[...] = running.T
    second.wait()
    factor = step_here[...] * jnp.exp2(last - running)
    total = jnp.broadcast_to(last, total_out.shape)
    factor_out[...] = factor
    total_out[...] = total
    half_states(half[0], x_here, b_here, copies, factor, total, out, matrix, dims)


def own_state_kernel(half, x, b, factor, total, out, matrix, x_here, b_here, sems, *, dims):
    copies = state_copies(half[0], x, b, x_here, b_here, sems, dims)
    for copy in copies:
        copy.start()
    half_spreader(matrix, x_here.shape[1] * CORES // factor.shape[1])
    half_states(half[0], x_here, b_here, copies, factor[...], total[...], out, matrix, dims)


def mixing_rows(first, own, got, states, cols):
    own_tail = own[states : states + 2, cols].astype(F32)
    got_tail = got[states : states + 2, cols].astype(F32)
    decay = jnp.where(first, got_tail, own_tail)
    decay = decay[:1, :] + decay[1:, :]
    one = jnp.ones_like(decay)
    return jnp.where(first, decay, one), jnp.where(first, one, decay)


def side_by_side(values, half):
    high, low = high_low(values)
    lane = lax.broadcasted_iota(jnp.int32, values.shape, 1)
    return jnp.where(lane < half, high, pltpu.roll(low, half, 1))


def chip_decay(first, got, total, states, base_out):
    heads = total.shape[1]
    half = heads // CORES
    partner = got[states + 2 : states + 3, :heads].astype(F32) + got[states + 3 : states + 4, :heads].astype(F32)
    partner = partner + got[states + 4 : states + 5, :heads].astype(F32)
    partner = jnp.broadcast_to(partner, total.shape)
    base_out[...] = jnp.where(first, jnp.zeros_like(partner), partner)
    both = jnp.exp2(total[...] + partner)
    both = jnp.where(first, both, pltpu.roll(both, half, 1))
    return side_by_side(both, half)


def chip_total_kernel(at, own, got, total, out, base_out):
    first = at[0] == 0
    cols = own.shape[1]
    states = out.shape[0]
    on_own, on_got = mixing_rows(first, own, got, states, slice(0, cols))
    for row in range(0, states, ROW_BLOCK):
        rows = slice(row, row + ROW_BLOCK)
        out[rows, :cols] = (on_own * own[rows, :].astype(F32) + on_got * got[rows, :].astype(F32)).astype(BF16)
    packed_decay = chip_decay(first, got, total, states, base_out)
    out[:, cols:] = jnp.concatenate([packed_decay] * (states // ROW_TILE), axis=0).astype(BF16)


def placed(kernel):
    def body(core, chip, outer, *refs, **options):
        return kernel((core[0], chip[0], outer[0]), *refs, **options)

    return body


def pieces_kernel(at, own, got, total, *outs, states, chunk):
    base_out = outs[-1]
    first = at[0] == 0
    rows, cols = outs[0].shape
    cols = cols - total.shape[1]
    here = slice(chunk * cols, (chunk + 1) * cols)
    on_own, on_got = mixing_rows(first, own, got, states, here)
    packed_decay = chip_decay(first, got, total, states, base_out)
    for k, out in enumerate(outs[:-1]):
        start = pl.multiple_of(jnp.bitwise_xor(at[1], k) * rows, rows)
        for row in range(0, rows, ROW_BLOCK):
            take = pl.ds(start + row, ROW_BLOCK)
            mixed = on_own * own[take, here].astype(F32) + on_got * got[take, here].astype(F32)
            out[row : row + ROW_BLOCK, :cols] = mixed.astype(BF16)
        out[:, cols:] = jnp.concatenate([packed_decay] * (rows // ROW_TILE), axis=0).astype(BF16)


def decays_of(pieces, cols, first_head, width):
    lanes = pieces[0].shape[1] - cols
    sent = [piece[:ROW_TILE, cols:].astype(F32)[:1, :] for piece in pieces]
    sent = jnp.concatenate(sent + [jnp.zeros((ROW_TILE - len(sent), lanes), F32)], axis=0)
    values = sent + pltpu.roll(sent, lanes // CORES, 1)
    heads = cols // width
    here = pltpu.roll(values, lanes - first_head, 1) if first_head else values
    return values, dot(packed(here, heads), spreader(heads, width))


def column_kernel(at, *refs, first_head, width, count):
    pieces, out, decay_out = refs[:count], refs[count], refs[count + 1]
    cols = decay_out.shape[1]
    rows = out.shape[0]
    values, decay = decays_of(pieces, cols, first_head, width)
    decay_out[...] = decay
    for place in range(count):

        @pl.when(at[1] == place)
        def _():
            state = jnp.zeros((rows, cols), F32)
            for k in range(count):
                k = k ^ place
                state = decay[k : k + 1, :] * state + pieces[k][:, :cols].astype(F32)
            out[:, :cols] = state.astype(BF16)

    fill_decay(out, cols, values, count)


def fill_decay(out, cols, values, count):
    product = values[:1, :]
    for k in range(1, count):
        product = product * values[k : k + 1, :]
    product = side_by_side(jnp.broadcast_to(product, (ROW_TILE, product.shape[1])), product.shape[1] // CORES)
    out[:, cols:] = jnp.concatenate([product] * (out.shape[0] // ROW_TILE), axis=0).astype(BF16)


def pair_kernel(at, mine, theirs, out, *, first_head, width, cols):
    odd = jnp.bitwise_and(at[2], 1) == 1
    values, decay = decays_of((mine, theirs), cols, first_head, width)
    one = jnp.ones_like(decay[:1, :])
    on_mine = jnp.where(odd, one, decay[1:2, :])
    on_theirs = jnp.where(odd, decay[:1, :], one)
    out[:, :cols] = (on_mine * mine[:, :cols].astype(F32) + on_theirs * theirs[:, :cols].astype(F32)).astype(BF16)
    fill_decay(out, cols, values, 2)


def chips_kernel(at, neighbour, lower_pair, decay, *refs, first_head, width, count):
    pieces, outs = refs[:count], refs[count:]
    _, cols = outs[0].shape
    odd = jnp.bitwise_and(at[2], 1) == 1
    late = at[2] >= 2
    _, passed = decays_of((neighbour,), cols, first_head, width)
    on_pair = jnp.where(late, jnp.where(odd, passed[:1, :], jnp.ones_like(passed[:1, :])), 0.0)
    carry = on_pair * lower_pair[:, :cols].astype(F32) + jnp.where(odd, neighbour[:, :cols].astype(F32), 0.0)
    for place in range(count):

        @pl.when(at[1] == place)
        def _():
            state = carry
            for k in range(count):
                k = k ^ place
                outs[k][...] = state.astype(BF16)
                state = decay[k : k + 1, :] * state + pieces[k][:, :cols].astype(F32)


def assemble_kernel(at, *refs, count):
    out = refs[-1]
    for n, piece in enumerate(refs[:-1]):
        rows, cols = piece.shape
        start = pl.multiple_of(jnp.bitwise_xor(at[1], n % count) * rows, rows)
        out[pl.ds(start, rows), n // count * cols : (n // count + 1) * cols] = piece[...]


def prefix_kernel(sent, out, here, sems, *, width, blocks):
    chips, rows, cols = here.shape
    heads = sent.shape[2] - cols
    half = heads // CORES
    step = cols // blocks
    first_rows = jnp.concatenate([sent[k, :1, cols:].astype(F32) for k in range(chips)], axis=0)
    values = first_rows + pltpu.roll(first_rows, half, 1)
    matrix = spreader(step // width, width)
    copies = []
    for block in range(blocks):
        lanes = slice(block * step, (block + 1) * step)
        head = block * step // width
        decay = dot(packed(pltpu.roll(values, heads - head, 1) if head else values, step // width), matrix)
        state = jnp.zeros((rows, step), F32)
        for k in range(chips):
            here[k, :, lanes] = state.astype(BF16)
            state = decay[k : k + 1, :] * state + sent[k, :, lanes].astype(F32)
        copies.append(
            pltpu.make_async_copy(
                here.at[:, :, pl.ds(block * step, step)], out.at[:, :, pl.ds(block * step, step)], sems.at[block]
            )
        )
        copies[-1].start()
    for copy in copies:
        copy.wait()


def within_kernel(
    half, flag, x_ref, b_ref, c_ref, step_ref, run_ref, run_t_ref, skip_ref, before_ref, out, matrix, *, dims, first_group
):
    per_half, per_group, width = dims
    turn = pl.program_id(0)
    place = first_group + turn
    head = (half[0] * per_half + place) * per_group
    rows = x_ref.shape[0]
    pair = LANES // width
    group_cols = per_group * width
    states = b_ref.shape[1] // per_half
    x_ref = x_ref.at[:, pl.ds(pl.multiple_of(place * group_cols, group_cols), group_cols)]
    b_ref = b_ref.at[:, pl.ds(pl.multiple_of(place * states, states), states)]
    c_ref = c_ref.at[:, pl.ds(pl.multiple_of((half[0] * per_half + place) * states, states), states)]
    before_ref = before_ref.at[:states, pl.ds(pl.multiple_of(place * group_cols, group_cols), group_cols)]
    out = out.at[:, pl.ds(pl.multiple_of(turn * group_cols, group_cols), group_cols)]

    @pl.when(turn == 0)
    def _():
        matrix[...] = spreader(per_group, width)

    def spread(values):
        return dot(packed(values, per_group), matrix[...])

    step = group_first(step_ref[...], head)
    run = group_first(run_ref[...], head)
    skip = group_first(jnp.broadcast_to(skip_ref[...], (ROW_TILE, skip_ref.shape[1])), head)
    run_t = run_t_ref[pl.ds(pl.multiple_of(head, per_group), per_group), :]
    x = x_ref[...].astype(F32)
    scaled = (x * spread(step)).astype(BF16)
    before = dot(c_ref[...], before_ref[...] * flag[0].astype(BF16))
    outer = spread(skip)[:1, :] * x + spread(jnp.exp2(run)) * before
    lane = lax.broadcasted_iota(jnp.int32, (HALF_ROWS, LANES), 1) // width
    lower = lax.broadcasted_iota(jnp.int32, (HALF_ROWS, HALF_ROWS), 1) <= lax.broadcasted_iota(
        jnp.int32, (HALF_ROWS, HALF_ROWS), 0
    )
    b = b_ref[...]
    c = c_ref[...]
    for start in range(0, rows, HALF_ROWS):
        stop = start + HALF_ROWS
        scores = jnp.where(lower, dot(c[start:stop, :], b[start:stop, :], (1, 1)), 0.0)
        added = outer[start:stop, :]
        if start:
            edge = run[start - 1 : start, :]
            lead = spread(step[:start, :] * jnp.exp2(edge - run[:start, :]))
            lead = (x[:start, :] * lead).astype(BF16)
            cross = dot(c[start:stop, :], b[:start, :], (1, 1)).astype(BF16)
            added = added + spread(jnp.exp2(run[start:stop, :] - edge)) * dot(cross, lead)
        for first in range(0, per_group, pair):
            cols = slice(first * width, (first + pair) * width)
            here = scaled[start:stop, cols]
            weights = []
            values = []
            for k in range(pair):
                at = first + k
                gap = run[start:stop, at : at + 1] - run_t[at : at + 1, start:stop]
                weights.append((scores * jnp.exp2(jnp.minimum(gap, 0.0))).astype(BF16))
                values.append(jnp.where(lane == k, here, jnp.zeros_like(here)))
            part = dot(jnp.concatenate(weights, axis=1), jnp.concatenate(values, axis=0))
            out[start:stop, cols] = (added[:, cols] + part).astype(BF16)


def final_kernel(half, c, state, run, base, matrix, within, *refs, dims):
    out, result, sems = refs[-3:]
    per_half, group_cols, states, first = dims
    operand = packed_half(jnp.exp2(run[...] + base[:1, :]), half[0])
    copies = []
    for k in range(state.shape[1] // group_cols):
        group = half[0] * per_half + first + k
        rows = c[:, pl.ds(pl.multiple_of(group * states, states), states)]
        tiles = group_cols // TILE
        products = {}
        for n in range(tiles + AHEAD):
            if n < tiles:
                start = k * group_cols + n * TILE
                spread = matrix[:, first * group_cols + start : first * group_cols + start + TILE]
                products[n] = dot(rows, state[:, start : start + TILE]), dot(operand, spread)
            m = n - AHEAD
            if m >= 0:
                cols = slice(k * group_cols + m * TILE, k * group_cols + (m + 1) * TILE)
                carried, factor = products.pop(m)
                result[:, cols] = (within[:, cols].astype(F32) + factor * carried).astype(BF16)
        home = pl.multiple_of(group * group_cols, group_cols)
        copies.append(
            pltpu.make_async_copy(
                result.at[:, pl.ds(k * group_cols, group_cols)], out.at[:, pl.ds(home, group_cols)], sems.at[k]
            )
        )
        copies[-1].start()
    for copy in copies:
        copy.wait()


def small_call(kernel, in_specs, out_shape, scratch=(), out_specs=None):
    return pl.pallas_call(
        kernel,
        in_specs=in_specs,
        out_specs=out_specs or [pl.BlockSpec(memory_space=pltpu.VMEM)] * len(out_shape),
        out_shape=out_shape,
        scratch_shapes=list(scratch),
        compiler_params=plain_params(),
    )


def xor_route(size, k):
    return [(i, i ^ k) for i in range(size)]


def swapped(arrays, axis):
    size = lax.axis_size(axis)
    done = {0: arrays[0]}
    for k in range(1, size):
        done[k] = lax.ppermute(arrays[k], axis, xor_route(size, k))
    return [done[k] for k in range(size)]


def entering_by_swaps(at, own, got, total, width, states, outer_axis, chip_axis):
    half_cols = own.shape[1]
    heads = total.shape[1]
    count = lax.axis_size(chip_axis)
    rows = states // count
    cols = half_cols // CHUNKS
    smem = pl.BlockSpec(memory_space=pltpu.SMEM)
    vmem = pl.BlockSpec(memory_space=pltpu.VMEM)
    shape = jax.ShapeDtypeStruct
    gathered = []
    for chunk in range(CHUNKS):
        *pieces, base = small_call(
            functools.partial(placed(pieces_kernel), states=states, chunk=chunk),
            [smem] * 3 + [vmem] * 3,
            [shape((rows, cols + heads), BF16)] * count + [shape((ROW_TILE, heads), F32)],
        )(*at, own, got, total)
        gathered.append(swapped(pieces, chip_axis))
    entering = []
    for chunk in range(CHUNKS):
        first_head = chunk * cols // width
        pieces = gathered[chunk]
        column, decay = small_call(
            functools.partial(placed(column_kernel), first_head=first_head, width=width, count=count),
            [smem] * 3 + [vmem] * count,
            [shape((rows, cols + heads), BF16), shape((ROW_TILE, cols), F32)],
        )(*at, *pieces)
        neighbour = lax.ppermute(column, outer_axis, xor_route(4, 1))
        (pair,) = small_call(
            functools.partial(placed(pair_kernel), first_head=first_head, width=width, cols=cols),
            [smem] * 3 + [vmem] * 2,
            [shape((rows, cols + heads), BF16)],
        )(*at, column, neighbour)
        pair = lax.ppermute(pair, outer_axis, xor_route(4, 2))
        states_out = small_call(
            functools.partial(placed(chips_kernel), first_head=first_head, width=width, count=count),
            [smem] * 3 + [vmem] * (count + 3),
            [shape((rows, cols), BF16)] * count,
        )(*at, neighbour, pair, decay, *pieces)
        states_out = swapped(states_out, chip_axis)
        entering += small_call(
            functools.partial(placed(assemble_kernel), count=count),
            [smem] * 3 + [vmem] * count,
            [shape((states, cols), BF16)],
        )(*at, *states_out)
    return entering, base


def entering_by_all_to_all(at, own, got, total, width, states, outer_axis, chip_axis):
    half_cols = own.shape[1]
    heads = total.shape[1]
    chips = lax.axis_size((outer_axis, chip_axis))
    rows = states // chips
    smem = pl.BlockSpec(memory_space=pltpu.SMEM)
    vmem = pl.BlockSpec(memory_space=pltpu.VMEM)
    chip_total, base = small_call(
        placed(chip_total_kernel),
        [smem] * 3 + [vmem] * 3,
        [jax.ShapeDtypeStruct((states, half_cols + heads), BF16), jax.ShapeDtypeStruct((ROW_TILE, heads), F32)],
    )(*at, own, got, total)
    sent = lax.all_to_all(
        chip_total.reshape(chips, rows, half_cols + heads),
        (outer_axis, chip_axis),
        split_axis=0,
        concat_axis=0,
        tiled=True,
    )
    blocks = GROUPS // CORES
    (entering,) = small_call(
        functools.partial(prefix_kernel, width=width, blocks=blocks),
        [vmem],
        [pltpu.HBM((chips, rows, half_cols), BF16)],
        [pltpu.VMEM((chips, rows, half_cols), BF16), pltpu.SemaphoreType.DMA((blocks,))],
        [pl.BlockSpec(memory_space=pltpu.HBM)],
    )(sent)
    entering = lax.all_to_all(entering, (outer_axis, chip_axis), split_axis=0, concat_axis=0, tiled=True)
    entering = entering.reshape(states, half_cols)
    return jnp.split(entering, CHUNKS, axis=1), base


def local(inputs, step_size, log_decay, b_matrix, c_matrix, skip_gain, *, outer_axis, chip_axis, core_axis):
    tokens, channels = inputs.shape
    heads = step_size.shape[1]
    width = channels // heads
    states = b_matrix.shape[1] // GROUPS
    per_group = heads // GROUPS
    group_cols = per_group * width
    per_half = GROUPS // CORES
    half_cols = channels // CORES
    chips = lax.axis_size((outer_axis, chip_axis))
    by_swaps = lax.axis_size(outer_axis) == 4 and chips == 16
    tall = states + ROW_TILE

    core = lax.axis_index(core_axis).astype(jnp.int32)
    mine = core.reshape(1)
    other = (1 - core).reshape(1)
    at = (mine,) + tuple(lax.axis_index(axis).astype(jnp.int32).reshape(1) for axis in (chip_axis, outer_axis))

    smem = pl.BlockSpec(memory_space=pltpu.SMEM)
    vmem = pl.BlockSpec(memory_space=pltpu.VMEM)
    hbm = pl.BlockSpec(memory_space=pltpu.HBM)

    state_dims = (per_half, group_cols, states)
    half_dims = (per_half, per_group, width)
    half_inputs = [
        jax.ShapeDtypeStruct((tokens, half_cols), BF16),
        jax.ShapeDtypeStruct((tokens, per_half * states), BF16),
    ]

    whole_step = step_size
    inputs, step_size, log_decay, b_matrix = (
        pltpu.with_memory_space_constraint(array, pltpu.HBM) for array in (inputs, step_size, log_decay, b_matrix)
    )
    send, run, run_t, factor, total, other_x, other_b = pl.pallas_call(
        functools.partial(send_state_kernel, dims=state_dims),
        in_specs=[smem] * 3 + [hbm] * 4,
        out_specs=[vmem] * 7,
        out_shape=[
            jax.ShapeDtypeStruct((tall, half_cols), BF16),
            jax.ShapeDtypeStruct((tokens, heads), F32),
            jax.ShapeDtypeStruct((heads, tokens), F32),
            jax.ShapeDtypeStruct((tokens, heads), F32),
            jax.ShapeDtypeStruct((ROW_TILE, heads), F32),
        ]
        + half_inputs,
        scratch_shapes=[pltpu.VMEM((heads, half_cols), BF16)]
        + [pltpu.VMEM((tokens, heads), F32)] * 2
        + [pltpu.SemaphoreType.DMA((2 * per_half + 2,))],
        compiler_params=plain_params(),
        name="send_state",
    )(other, *at[1:], inputs, b_matrix, step_size, log_decay)

    swap = [(0, 1), (1, 0)]
    got = lax.ppermute(send, core_axis, swap)

    own, matrix, own_x, own_b = small_call(
        functools.partial(own_state_kernel, dims=state_dims),
        [smem, hbm, hbm, vmem, vmem],
        [jax.ShapeDtypeStruct((tall, half_cols), BF16), jax.ShapeDtypeStruct((heads, half_cols), BF16)] + half_inputs,
        [pltpu.SemaphoreType.DMA((2 * per_half,))],
    )(mine, inputs, b_matrix, factor, total)

    find_entering = entering_by_swaps if by_swaps else entering_by_all_to_all
    entering, base = find_entering(at, own, got, total, width, states, outer_axis, chip_axis)
    late = lax.ppermute(own, core_axis, swap[:1])

    def within(half, x, b, before, first):
        return pl.pallas_call(
            functools.partial(within_kernel, dims=half_dims, first_group=first),
            grid_spec=pltpu.PrefetchScalarGridSpec(
                num_scalar_prefetch=2,
                grid=(PER_CALL,),
                in_specs=[vmem] * 8,
                out_specs=vmem,
                scratch_shapes=[pltpu.VMEM((2 * per_group, group_cols), BF16)],
            ),
            out_shape=jax.ShapeDtypeStruct((tokens, PER_CALL * group_cols), BF16),
            compiler_params=params(),
            name="within",
        )(
            half,
            mine,
            x,
            b,
            c_matrix,
            whole_step,
            run,
            run_t,
            skip_gain.reshape(1, heads),
            before,
        )

    own_within = []
    other_within = []
    for first in range(0, per_half, PER_CALL):
        own_within.append(within(mine, own_x, own_b, got, first))
        other_within.append(within(other, other_x, other_b, late, first))

    mixed = jax.ShapeDtypeStruct((tokens, channels), BF16)

    def finish(half, chunk, state, part, *result):
        cols = PER_CALL * group_cols
        return pl.pallas_call(
            functools.partial(final_kernel, dims=state_dims + (chunk * PER_CALL,)),
            in_specs=[smem] + [vmem] * 6 + [hbm] * len(result),
            out_specs=hbm,
            out_shape=mixed,
            scratch_shapes=[pltpu.VMEM((tokens, cols), BF16), pltpu.SemaphoreType.DMA((PER_CALL,))],
            input_output_aliases={7: 0} if result else {},
            compiler_params=plain_params(),
            name="finish",
        )(half, c_matrix, state, run, base, matrix, part, *result)

    result = ()
    for chunk in reversed(range(CHUNKS)):
        got_entering = lax.ppermute(entering[chunk], core_axis, swap)
        result = (finish(mine, chunk, entering[chunk], own_within[chunk], *result),)
        result = (finish(other, chunk, got_entering, other_within[chunk], *result),)
    return result[0]


def solution(mesh):
    outer, inner = mesh.axis_names
    chip_mesh = Mesh(
        mesh.devices.reshape(mesh.shape[outer], mesh.shape[inner] // CORES, CORES), (outer, "chip", "core")
    )
    placed = P((outer, "chip", "core"), None)

    def body(*args):
        return local(*args, outer_axis=outer, chip_axis="chip", core_axis="core")

    return jax.shard_map(body, mesh=chip_mesh, in_specs=(placed,) * 5 + (P(),), out_specs=placed, check_vma=False)
```

```python
import functools
import math

import jax
import jax.numpy as jnp
from jax import lax
from jax.experimental import pallas as pl
from jax.experimental.pallas import tpu as pltpu
from jax.sharding import Mesh, PartitionSpec as P


GROUPS = 8
CORES = 2
LANES = 128
TILE = 256
AHEAD = 2
CHUNKS = 2
PER_CALL = 2
ROW_TILE = 8
HALF_ROWS = 128
ROW_BLOCK = 16
VMEM_LIMIT = 24 * 1024 * 1024
LOG2E = 1.0 / math.log(2.0)

F32 = jnp.float32
BF16 = jnp.bfloat16


def dot(a, b, contract=(1, 0)):
    dims = (((contract[0],), (contract[1],)), ((), ()))
    return lax.dot_general(a, b, dims, preferred_element_type=F32)


def high_low(values):
    high = values.astype(BF16).astype(F32)
    return high, values - high


def spreader(heads, width):
    shape = (2 * heads, heads * width)
    row = lax.broadcasted_iota(jnp.int32, shape, 0)
    col = lax.broadcasted_iota(jnp.int32, shape, 1)
    row = jnp.where(row >= heads, row - heads, row)
    return jnp.where(row == col // width, 1.0, 0.0).astype(BF16)


def group_first(values, head):
    lanes = values.shape[1]
    return pltpu.roll(values, lax.rem(lanes - head, lanes), 1)


def packed(values, heads):
    high, low = high_low(values)
    lane = lax.broadcasted_iota(jnp.int32, values.shape, 1)
    return jnp.where(lane < heads, high, pltpu.roll(low, heads, 1)).astype(BF16)[:, : 2 * heads]


def half_spreader(matrix, width):
    lanes, cols = matrix.shape
    for start in range(0, cols, TILE):
        row = lax.broadcasted_iota(jnp.int32, (lanes, TILE), 0)
        col = start + lax.broadcasted_iota(jnp.int32, (lanes, TILE), 1)
        row = jnp.where(row >= lanes // 2, row - lanes // 2, row)
        matrix[:, start : start + TILE] = jnp.where(row == col // width, 1.0, 0.0).astype(BF16)


def packed_half(values, half):
    lanes = values.shape[1]
    values = group_first(values, half * (lanes // 2))
    high, low = high_low(values)
    lane = lax.broadcasted_iota(jnp.int32, values.shape, 1)
    return jnp.where(lane < lanes // 2, high, pltpu.roll(low, lanes // 2, 1)).astype(BF16)


def params():
    return pltpu.CompilerParams(dimension_semantics=("arbitrary",), vmem_limit_bytes=VMEM_LIMIT)


def plain_params():
    return pltpu.CompilerParams(vmem_limit_bytes=VMEM_LIMIT)


def state_copies(half, x, b, x_here, b_here, sems, dims):
    per_half, group_cols, states = dims
    copies = []
    for k in range(per_half):
        group = half * per_half + k
        copies.append(
            pltpu.make_async_copy(
                x.at[:, pl.ds(pl.multiple_of(group * group_cols, group_cols), group_cols)],
                x_here.at[:, pl.ds(k * group_cols, group_cols)],
                sems.at[2 * k],
            )
        )
        copies.append(
            pltpu.make_async_copy(
                b.at[:, pl.ds(pl.multiple_of(group * states, states), states)],
                b_here.at[:, pl.ds(k * states, states)],
                sems.at[2 * k + 1],
            )
        )
    return copies


def half_states(half, x_here, b_here, copies, factor, log_total, out, matrix, dims):
    _, group_cols, states = dims
    rows, heads = factor.shape
    row = lax.broadcasted_iota(jnp.int32, (ROW_TILE, TILE), 0)
    operand = packed_half(jnp.concatenate([factor, jnp.exp2(log_total)], axis=0), half)
    for copy in copies:
        copy.wait()
    tiles = out.shape[1] // TILE
    per_group = group_cols // TILE
    matrices = {}
    factors = {}
    scaled = {}
    for n in range(tiles + 2 * AHEAD):
        if n < tiles:
            factors[n] = dot(operand, matrix[:, n * TILE : (n + 1) * TILE])
        m = n - AHEAD
        if 0 <= m < tiles:
            cols = slice(m * TILE, (m + 1) * TILE)
            spread = factors.pop(m)
            scaled[m] = (x_here[:, cols].astype(F32) * spread[:rows, :]).astype(BF16)
            high, low = high_low(spread[rows:, :])
            tail = jnp.where(row == 0, high, low)
            if m == 0:
                high, low = high_low(log_total)
                middle, low = high_low(low)
                at = row[:, :heads]
                logs = jnp.where(at == 2, high, jnp.where(at == 3, middle, low))
                logs = jnp.where(at < 2, tail[:, :heads], logs)
                tail = jnp.concatenate([logs, tail[:, heads:]], axis=1)
            out[states:, cols] = tail.astype(BF16)
            if m % per_group == 0:
                k = m // per_group
                matrices[k] = b_here[:, k * states : (k + 1) * states].T
        m = n - 2 * AHEAD
        if m >= 0:
            out[:states, m * TILE : (m + 1) * TILE] = dot(matrices[m // per_group], scaled.pop(m)).astype(BF16)


def send_state_kernel(
    half,
    chip,
    outer,
    x,
    b,
    step,
    log,
    out,
    run_out,
    run_t_out,
    factor_out,
    total_out,
    x_here,
    b_here,
    matrix,
    step_here,
    log_here,
    sems,
    *,
    dims,
):
    del chip, outer
    first = pltpu.make_async_copy(log, log_here, sems.at[2 * dims[0]])
    second = pltpu.make_async_copy(step, step_here, sems.at[2 * dims[0] + 1])
    first.start()
    second.start()
    copies = state_copies(half[0], x, b, x_here, b_here, sems, dims)
    for copy in copies:
        copy.start()
    rows, heads = log_here.shape
    half_spreader(matrix, x_here.shape[1] * CORES // heads)
    upto = lax.broadcasted_iota(jnp.int32, (rows, rows), 1) <= lax.broadcasted_iota(jnp.int32, (rows, rows), 0)
    first.wait()
    high, rest = high_low(log_here[...])
    middle, low = high_low(rest)
    parts = jnp.concatenate([high, middle, low], axis=1).astype(BF16)
    sums = dot(jnp.where(upto, 1.0, 0.0).astype(BF16), parts)
    running = (sums[:, :heads] + sums[:, heads : 2 * heads] + sums[:, 2 * heads :]) * LOG2E
    last = running[rows - 1 :, :]
    run_out[...] = running
    run_t_out[...] = running.T
    second.wait()
    factor = step_here[...] * jnp.exp2(last - running)
    total = jnp.broadcast_to(last, total_out.shape)
    factor_out[...] = factor
    total_out[...] = total
    half_states(half[0], x_here, b_here, copies, factor, total, out, matrix, dims)


def own_state_kernel(half, x, b, factor, total, out, matrix, x_here, b_here, sems, *, dims):
    copies = state_copies(half[0], x, b, x_here, b_here, sems, dims)
    for copy in copies:
        copy.start()
    half_spreader(matrix, x_here.shape[1] * CORES // factor.shape[1])
    half_states(half[0], x_here, b_here, copies, factor[...], total[...], out, matrix, dims)


def mixing_rows(first, own, got, states, cols):
    own_tail = own[states : states + 2, cols].astype(F32)
    got_tail = got[states : states + 2, cols].astype(F32)
    decay = jnp.where(first, got_tail, own_tail)
    decay = decay[:1, :] + decay[1:, :]
    one = jnp.ones_like(decay)
    return jnp.where(first, decay, one), jnp.where(first, one, decay)


def side_by_side(values, half):
    high, low = high_low(values)
    lane = lax.broadcasted_iota(jnp.int32, values.shape, 1)
    return jnp.where(lane < half, high, pltpu.roll(low, half, 1))


def chip_decay(first, got, total, states, base_out):
    heads = total.shape[1]
    half = heads // CORES
    partner = got[states + 2 : states + 3, :heads].astype(F32) + got[states + 3 : states + 4, :heads].astype(F32)
    partner = partner + got[states + 4 : states + 5, :heads].astype(F32)
    partner = jnp.broadcast_to(partner, total.shape)
    base_out[...] = jnp.where(first, jnp.zeros_like(partner), partner)
    both = jnp.exp2(total[...] + partner)
    both = jnp.where(first, both, pltpu.roll(both, half, 1))
    return side_by_side(both, half)


def chip_total_kernel(at, own, got, total, out, base_out):
    first = at[0] == 0
    cols = own.shape[1]
    states = out.shape[0]
    on_own, on_got = mixing_rows(first, own, got, states, slice(0, cols))
    for row in range(0, states, ROW_BLOCK):
        rows = slice(row, row + ROW_BLOCK)
        out[rows, :cols] = (on_own * own[rows, :].astype(F32) + on_got * got[rows, :].astype(F32)).astype(BF16)
    packed_decay = chip_decay(first, got, total, states, base_out)
    out[:, cols:] = jnp.concatenate([packed_decay] * (states // ROW_TILE), axis=0).astype(BF16)


def placed(kernel):
    def body(core, chip, outer, *refs, **options):
        return kernel((core[0], chip[0], outer[0]), *refs, **options)

    return body


def pieces_kernel(at, own, got, total, *outs, states, chunk):
    base_out = outs[-1]
    first = at[0] == 0
    rows, cols = outs[0].shape
    cols = cols - total.shape[1]
    here = slice(chunk * cols, (chunk + 1) * cols)
    on_own, on_got = mixing_rows(first, own, got, states, here)
    packed_decay = chip_decay(first, got, total, states, base_out)
    for k, out in enumerate(outs[:-1]):
        start = pl.multiple_of(jnp.bitwise_xor(at[1], k) * rows, rows)
        for row in range(0, rows, ROW_BLOCK):
            take = pl.ds(start + row, ROW_BLOCK)
            mixed = on_own * own[take, here].astype(F32) + on_got * got[take, here].astype(F32)
            out[row : row + ROW_BLOCK, :cols] = mixed.astype(BF16)
        out[:, cols:] = jnp.concatenate([packed_decay] * (rows // ROW_TILE), axis=0).astype(BF16)


def decays_of(pieces, cols, first_head, width):
    lanes = pieces[0].shape[1] - cols
    sent = [piece[:ROW_TILE, cols:].astype(F32)[:1, :] for piece in pieces]
    sent = jnp.concatenate(sent + [jnp.zeros((ROW_TILE - len(sent), lanes), F32)], axis=0)
    values = sent + pltpu.roll(sent, lanes // CORES, 1)
    heads = cols // width
    here = pltpu.roll(values, lanes - first_head, 1) if first_head else values
    return values, dot(packed(here, heads), spreader(heads, width))


def column_kernel(at, *refs, first_head, width, count):
    pieces, out, decay_out = refs[:count], refs[count], refs[count + 1]
    cols = decay_out.shape[1]
    rows = out.shape[0]
    values, decay = decays_of(pieces, cols, first_head, width)
    decay_out[...] = decay
    for place in range(count):

        @pl.when(at[1] == place)
        def _():
            state = jnp.zeros((rows, cols), F32)
            for k in range(count):
                k = k ^ place
                state = decay[k : k + 1, :] * state + pieces[k][:, :cols].astype(F32)
            out[:, :cols] = state.astype(BF16)

    fill_decay(out, cols, values, count)


def fill_decay(out, cols, values, count):
    product = values[:1, :]
    for k in range(1, count):
        product = product * values[k : k + 1, :]
    product = side_by_side(jnp.broadcast_to(product, (ROW_TILE, product.shape[1])), product.shape[1] // CORES)
    out[:, cols:] = jnp.concatenate([product] * (out.shape[0] // ROW_TILE), axis=0).astype(BF16)


def chips_kernel(at, *refs, first_head, width, count, blocks):
    others, decay = refs[: blocks - 1], refs[blocks - 1]
    pieces, outs, carry = refs[blocks : blocks + count], refs[blocks + count : -1], refs[-1]
    rows, cols = outs[0].shape
    _, passed = decays_of(others, cols, first_head, width)
    for place in range(blocks):

        @pl.when(at[2] == place)
        def _():
            state = jnp.zeros((rows, cols), F32)
            for k in range(place):
                k = (k ^ place) - 1
                state = passed[k : k + 1, :] * state + others[k][:, :cols].astype(F32)
            carry[...] = state

    for place in range(count):

        @pl.when(at[1] == place)
        def _():
            state = carry[...]
            for k in range(count):
                k = k ^ place
                outs[k][...] = state.astype(BF16)
                state = decay[k : k + 1, :] * state + pieces[k][:, :cols].astype(F32)


def assemble_kernel(at, *refs, count):
    out = refs[-1]
    for n, piece in enumerate(refs[:-1]):
        rows, cols = piece.shape
        start = pl.multiple_of(jnp.bitwise_xor(at[1], n % count) * rows, rows)
        out[pl.ds(start, rows), n // count * cols : (n // count + 1) * cols] = piece[...]


def prefix_kernel(sent, out, here, sems, *, width, blocks):
    chips, rows, cols = here.shape
    heads = sent.shape[2] - cols
    half = heads // CORES
    step = cols // blocks
    first_rows = jnp.concatenate([sent[k, :1, cols:].astype(F32) for k in range(chips)], axis=0)
    values = first_rows + pltpu.roll(first_rows, half, 1)
    matrix = spreader(step // width, width)
    copies = []
    for block in range(blocks):
        lanes = slice(block * step, (block + 1) * step)
        head = block * step // width
        decay = dot(packed(pltpu.roll(values, heads - head, 1) if head else values, step // width), matrix)
        state = jnp.zeros((rows, step), F32)
        for k in range(chips):
            here[k, :, lanes] = state.astype(BF16)
            state = decay[k : k + 1, :] * state + sent[k, :, lanes].astype(F32)
        copies.append(
            pltpu.make_async_copy(
                here.at[:, :, pl.ds(block * step, step)], out.at[:, :, pl.ds(block * step, step)], sems.at[block]
            )
        )
        copies[-1].start()
    for copy in copies:
        copy.wait()


def within_kernel(
    half, flag, x_ref, b_ref, c_ref, step_ref, run_ref, run_t_ref, skip_ref, before_ref, out, matrix, *, dims, first_group
):
    per_half, per_group, width = dims
    turn = pl.program_id(0)
    place = first_group + turn
    head = (half[0] * per_half + place) * per_group
    rows = x_ref.shape[0]
    pair = LANES // width
    group_cols = per_group * width
    states = b_ref.shape[1] // per_half
    x_ref = x_ref.at[:, pl.ds(pl.multiple_of(place * group_cols, group_cols), group_cols)]
    b_ref = b_ref.at[:, pl.ds(pl.multiple_of(place * states, states), states)]
    c_ref = c_ref.at[:, pl.ds(pl.multiple_of((half[0] * per_half + place) * states, states), states)]
    before_ref = before_ref.at[:states, pl.ds(pl.multiple_of(place * group_cols, group_cols), group_cols)]
    out = out.at[:, pl.ds(pl.multiple_of(turn * group_cols, group_cols), group_cols)]

    @pl.when(turn == 0)
    def _():
        matrix[...] = spreader(per_group, width)

    def spread(values):
        return dot(packed(values, per_group), matrix[...])

    step = group_first(step_ref[...], head)
    run = group_first(run_ref[...], head)
    skip = group_first(jnp.broadcast_to(skip_ref[...], (ROW_TILE, skip_ref.shape[1])), head)
    run_t = run_t_ref[pl.ds(pl.multiple_of(head, per_group), per_group), :]
    x = x_ref[...].astype(F32)
    scaled = (x * spread(step)).astype(BF16)
    before = dot(c_ref[...], before_ref[...] * flag[0].astype(BF16))
    outer = spread(skip)[:1, :] * x + spread(jnp.exp2(run)) * before
    lane = lax.broadcasted_iota(jnp.int32, (HALF_ROWS, LANES), 1) // width
    lower = lax.broadcasted_iota(jnp.int32, (HALF_ROWS, HALF_ROWS), 1) <= lax.broadcasted_iota(
        jnp.int32, (HALF_ROWS, HALF_ROWS), 0
    )
    b = b_ref[...]
    c = c_ref[...]
    for start in range(0, rows, HALF_ROWS):
        stop = start + HALF_ROWS
        scores = jnp.where(lower, dot(c[start:stop, :], b[start:stop, :], (1, 1)), 0.0)
        added = outer[start:stop, :]
        if start:
            edge = run[start - 1 : start, :]
            lead = spread(step[:start, :] * jnp.exp2(edge - run[:start, :]))
            lead = (x[:start, :] * lead).astype(BF16)
            cross = dot(c[start:stop, :], b[:start, :], (1, 1)).astype(BF16)
            added = added + spread(jnp.exp2(run[start:stop, :] - edge)) * dot(cross, lead)
        for first in range(0, per_group, pair):
            cols = slice(first * width, (first + pair) * width)
            here = scaled[start:stop, cols]
            weights = []
            values = []
            for k in range(pair):
                at = first + k
                gap = run[start:stop, at : at + 1] - run_t[at : at + 1, start:stop]
                weights.append((scores * jnp.exp2(jnp.minimum(gap, 0.0))).astype(BF16))
                values.append(jnp.where(lane == k, here, jnp.zeros_like(here)))
            part = dot(jnp.concatenate(weights, axis=1), jnp.concatenate(values, axis=0))
            out[start:stop, cols] = (added[:, cols] + part).astype(BF16)


def final_kernel(half, c, state, run, base, matrix, within, *refs, dims):
    out, result, sems = refs[-3:]
    per_half, group_cols, states, first = dims
    operand = packed_half(jnp.exp2(run[...] + base[:1, :]), half[0])
    copies = []
    for k in range(state.shape[1] // group_cols):
        group = half[0] * per_half + first + k
        rows = c[:, pl.ds(pl.multiple_of(group * states, states), states)]
        tiles = group_cols // TILE
        products = {}
        for n in range(tiles + AHEAD):
            if n < tiles:
                start = k * group_cols + n * TILE
                spread = matrix[:, first * group_cols + start : first * group_cols + start + TILE]
                products[n] = dot(rows, state[:, start : start + TILE]), dot(operand, spread)
            m = n - AHEAD
            if m >= 0:
                cols = slice(k * group_cols + m * TILE, k * group_cols + (m + 1) * TILE)
                carried, factor = products.pop(m)
                result[:, cols] = (within[:, cols].astype(F32) + factor * carried).astype(BF16)
        home = pl.multiple_of(group * group_cols, group_cols)
        copies.append(
            pltpu.make_async_copy(
                result.at[:, pl.ds(k * group_cols, group_cols)], out.at[:, pl.ds(home, group_cols)], sems.at[k]
            )
        )
        copies[-1].start()
    for copy in copies:
        copy.wait()


def small_call(kernel, in_specs, out_shape, scratch=(), out_specs=None):
    return pl.pallas_call(
        kernel,
        in_specs=in_specs,
        out_specs=out_specs or [pl.BlockSpec(memory_space=pltpu.VMEM)] * len(out_shape),
        out_shape=out_shape,
        scratch_shapes=list(scratch),
        compiler_params=plain_params(),
    )


def xor_route(size, k):
    return [(i, i ^ k) for i in range(size)]


def swapped(arrays, axis):
    size = lax.axis_size(axis)
    done = {0: arrays[0]}
    for k in range(1, size):
        done[k] = lax.ppermute(arrays[k], axis, xor_route(size, k))
    return [done[k] for k in range(size)]


def entering_by_swaps(at, own, got, total, width, states, outer_axis, chip_axis):
    half_cols = own.shape[1]
    heads = total.shape[1]
    count = lax.axis_size(chip_axis)
    blocks = lax.axis_size(outer_axis)
    rows = states // count
    cols = half_cols // CHUNKS
    smem = pl.BlockSpec(memory_space=pltpu.SMEM)
    vmem = pl.BlockSpec(memory_space=pltpu.VMEM)
    shape = jax.ShapeDtypeStruct
    gathered = []
    for chunk in range(CHUNKS):
        *pieces, base = small_call(
            functools.partial(placed(pieces_kernel), states=states, chunk=chunk),
            [smem] * 3 + [vmem] * 3,
            [shape((rows, cols + heads), BF16)] * count + [shape((ROW_TILE, heads), F32)],
        )(*at, own, got, total)
        gathered.append(swapped(pieces, chip_axis))
    entering = []
    for chunk in range(CHUNKS):
        first_head = chunk * cols // width
        pieces = gathered[chunk]
        column, decay = small_call(
            functools.partial(placed(column_kernel), first_head=first_head, width=width, count=count),
            [smem] * 3 + [vmem] * count,
            [shape((rows, cols + heads), BF16), shape((ROW_TILE, cols), F32)],
        )(*at, *pieces)
        others = swapped([column] * blocks, outer_axis)[1:]
        states_out = small_call(
            functools.partial(
                placed(chips_kernel), first_head=first_head, width=width, count=count, blocks=blocks
            ),
            [smem] * 3 + [vmem] * (count + blocks),
            [shape((rows, cols), BF16)] * count,
            [pltpu.VMEM((rows, cols), F32)],
        )(*at, *others, decay, *pieces)
        states_out = swapped(states_out, chip_axis)
        entering += small_call(
            functools.partial(placed(assemble_kernel), count=count),
            [smem] * 3 + [vmem] * count,
            [shape((states, cols), BF16)],
        )(*at, *states_out)
    return entering, base


def entering_by_all_to_all(at, own, got, total, width, states, outer_axis, chip_axis):
    half_cols = own.shape[1]
    heads = total.shape[1]
    chips = lax.axis_size((outer_axis, chip_axis))
    rows = states // chips
    smem = pl.BlockSpec(memory_space=pltpu.SMEM)
    vmem = pl.BlockSpec(memory_space=pltpu.VMEM)
    chip_total, base = small_call(
        placed(chip_total_kernel),
        [smem] * 3 + [vmem] * 3,
        [jax.ShapeDtypeStruct((states, half_cols + heads), BF16), jax.ShapeDtypeStruct((ROW_TILE, heads), F32)],
    )(*at, own, got, total)
    sent = lax.all_to_all(
        chip_total.reshape(chips, rows, half_cols + heads),
        (outer_axis, chip_axis),
        split_axis=0,
        concat_axis=0,
        tiled=True,
    )
    blocks = GROUPS // CORES
    (entering,) = small_call(
        functools.partial(prefix_kernel, width=width, blocks=blocks),
        [vmem],
        [pltpu.HBM((chips, rows, half_cols), BF16)],
        [pltpu.VMEM((chips, rows, half_cols), BF16), pltpu.SemaphoreType.DMA((blocks,))],
        [pl.BlockSpec(memory_space=pltpu.HBM)],
    )(sent)
    entering = lax.all_to_all(entering, (outer_axis, chip_axis), split_axis=0, concat_axis=0, tiled=True)
    entering = entering.reshape(states, half_cols)
    return jnp.split(entering, CHUNKS, axis=1), base


def local(inputs, step_size, log_decay, b_matrix, c_matrix, skip_gain, *, outer_axis, chip_axis, core_axis):
    tokens, channels = inputs.shape
    heads = step_size.shape[1]
    width = channels // heads
    states = b_matrix.shape[1] // GROUPS
    per_group = heads // GROUPS
    group_cols = per_group * width
    per_half = GROUPS // CORES
    half_cols = channels // CORES
    chips = lax.axis_size((outer_axis, chip_axis))
    by_swaps = lax.axis_size(outer_axis) == 4 and chips == 16
    tall = states + ROW_TILE

    core = lax.axis_index(core_axis).astype(jnp.int32)
    mine = core.reshape(1)
    other = (1 - core).reshape(1)
    at = (mine,) + tuple(lax.axis_index(axis).astype(jnp.int32).reshape(1) for axis in (chip_axis, outer_axis))

    smem = pl.BlockSpec(memory_space=pltpu.SMEM)
    vmem = pl.BlockSpec(memory_space=pltpu.VMEM)
    hbm = pl.BlockSpec(memory_space=pltpu.HBM)

    state_dims = (per_half, group_cols, states)
    half_dims = (per_half, per_group, width)
    half_inputs = [
        jax.ShapeDtypeStruct((tokens, half_cols), BF16),
        jax.ShapeDtypeStruct((tokens, per_half * states), BF16),
    ]

    whole_step = step_size
    inputs, step_size, log_decay, b_matrix = (
        pltpu.with_memory_space_constraint(array, pltpu.HBM) for array in (inputs, step_size, log_decay, b_matrix)
    )
    send, run, run_t, factor, total, other_x, other_b = pl.pallas_call(
        functools.partial(send_state_kernel, dims=state_dims),
        in_specs=[smem] * 3 + [hbm] * 4,
        out_specs=[vmem] * 7,
        out_shape=[
            jax.ShapeDtypeStruct((tall, half_cols), BF16),
            jax.ShapeDtypeStruct((tokens, heads), F32),
            jax.ShapeDtypeStruct((heads, tokens), F32),
            jax.ShapeDtypeStruct((tokens, heads), F32),
            jax.ShapeDtypeStruct((ROW_TILE, heads), F32),
        ]
        + half_inputs,
        scratch_shapes=[pltpu.VMEM((heads, half_cols), BF16)]
        + [pltpu.VMEM((tokens, heads), F32)] * 2
        + [pltpu.SemaphoreType.DMA((2 * per_half + 2,))],
        compiler_params=plain_params(),
        name="send_state",
    )(other, *at[1:], inputs, b_matrix, step_size, log_decay)

    swap = [(0, 1), (1, 0)]
    got = lax.ppermute(send, core_axis, swap)

    own, matrix, own_x, own_b = small_call(
        functools.partial(own_state_kernel, dims=state_dims),
        [smem, hbm, hbm, vmem, vmem],
        [jax.ShapeDtypeStruct((tall, half_cols), BF16), jax.ShapeDtypeStruct((heads, half_cols), BF16)] + half_inputs,
        [pltpu.SemaphoreType.DMA((2 * per_half,))],
    )(mine, inputs, b_matrix, factor, total)

    find_entering = entering_by_swaps if by_swaps else entering_by_all_to_all
    entering, base = find_entering(at, own, got, total, width, states, outer_axis, chip_axis)
    late = lax.ppermute(own, core_axis, swap[:1])

    def within(half, x, b, before, first):
        return pl.pallas_call(
            functools.partial(within_kernel, dims=half_dims, first_group=first),
            grid_spec=pltpu.PrefetchScalarGridSpec(
                num_scalar_prefetch=2,
                grid=(PER_CALL,),
                in_specs=[vmem] * 8,
                out_specs=vmem,
                scratch_shapes=[pltpu.VMEM((2 * per_group, group_cols), BF16)],
            ),
            out_shape=jax.ShapeDtypeStruct((tokens, PER_CALL * group_cols), BF16),
            compiler_params=params(),
            name="within",
        )(
            half,
            mine,
            x,
            b,
            c_matrix,
            whole_step,
            run,
            run_t,
            skip_gain.reshape(1, heads),
            before,
        )

    own_within = []
    other_within = []
    for first in range(0, per_half, PER_CALL):
        own_within.append(within(mine, own_x, own_b, got, first))
        other_within.append(within(other, other_x, other_b, late, first))

    mixed = jax.ShapeDtypeStruct((tokens, channels), BF16)

    def finish(half, chunk, state, part, *result):
        cols = PER_CALL * group_cols
        return pl.pallas_call(
            functools.partial(final_kernel, dims=state_dims + (chunk * PER_CALL,)),
            in_specs=[smem] + [vmem] * 6 + [hbm] * len(result),
            out_specs=hbm,
            out_shape=mixed,
            scratch_shapes=[pltpu.VMEM((tokens, cols), BF16), pltpu.SemaphoreType.DMA((PER_CALL,))],
            input_output_aliases={7: 0} if result else {},
            compiler_params=plain_params(),
            name="finish",
        )(half, c_matrix, state, run, base, matrix, part, *result)

    result = ()
    for chunk in reversed(range(CHUNKS)):
        got_entering = lax.ppermute(entering[chunk], core_axis, swap)
        result = (finish(mine, chunk, entering[chunk], own_within[chunk], *result),)
        result = (finish(other, chunk, got_entering, other_within[chunk], *result),)
    return result[0]


def solution(mesh):
    outer, inner = mesh.axis_names
    chip_mesh = Mesh(
        mesh.devices.reshape(mesh.shape[outer], mesh.shape[inner] // CORES, CORES), (outer, "chip", "core")
    )
    placed = P((outer, "chip", "core"), None)

    def body(*args):
        return local(*args, outer_axis=outer, chip_axis="chip", core_axis="core")

    return jax.shard_map(body, mesh=chip_mesh, in_specs=(placed,) * 5 + (P(),), out_specs=placed, check_vma=False)
```

```python
import functools
import math

import jax
import jax.numpy as jnp
from jax import lax
from jax.experimental import pallas as pl
from jax.experimental.pallas import tpu as pltpu
from jax.sharding import Mesh, PartitionSpec as P


GROUPS = 8
CORES = 2
LANES = 128
TILE = 256
AHEAD = 2
CHUNKS = 2
PER_CALL = 2
ROW_TILE = 8
HALF_ROWS = 128
ROW_BLOCK = 16
VMEM_LIMIT = 24 * 1024 * 1024
LOG2E = 1.0 / math.log(2.0)

F32 = jnp.float32
BF16 = jnp.bfloat16


def dot(a, b, contract=(1, 0)):
    dims = (((contract[0],), (contract[1],)), ((), ()))
    return lax.dot_general(a, b, dims, preferred_element_type=F32)


def high_low(values):
    high = values.astype(BF16).astype(F32)
    return high, values - high


def spreader(heads, width):
    shape = (2 * heads, heads * width)
    row = lax.broadcasted_iota(jnp.int32, shape, 0)
    col = lax.broadcasted_iota(jnp.int32, shape, 1)
    row = jnp.where(row >= heads, row - heads, row)
    return jnp.where(row == col // width, 1.0, 0.0).astype(BF16)


def group_first(values, head):
    lanes = values.shape[1]
    return pltpu.roll(values, lax.rem(lanes - head, lanes), 1)


def packed(values, heads):
    high, low = high_low(values)
    lane = lax.broadcasted_iota(jnp.int32, values.shape, 1)
    return jnp.where(lane < heads, high, pltpu.roll(low, heads, 1)).astype(BF16)[:, : 2 * heads]


def half_spreader(matrix, width):
    lanes, cols = matrix.shape
    for start in range(0, cols, TILE):
        row = lax.broadcasted_iota(jnp.int32, (lanes, TILE), 0)
        col = start + lax.broadcasted_iota(jnp.int32, (lanes, TILE), 1)
        row = jnp.where(row >= lanes // 2, row - lanes // 2, row)
        matrix[:, start : start + TILE] = jnp.where(row == col // width, 1.0, 0.0).astype(BF16)


def packed_half(values, half):
    lanes = values.shape[1]
    values = group_first(values, half * (lanes // 2))
    high, low = high_low(values)
    lane = lax.broadcasted_iota(jnp.int32, values.shape, 1)
    return jnp.where(lane < lanes // 2, high, pltpu.roll(low, lanes // 2, 1)).astype(BF16)


def params():
    return pltpu.CompilerParams(dimension_semantics=("arbitrary",), vmem_limit_bytes=VMEM_LIMIT)


def plain_params():
    return pltpu.CompilerParams(vmem_limit_bytes=VMEM_LIMIT)


def state_copies(half, x, b, x_here, b_here, sems, dims):
    per_half, group_cols, states = dims
    copies = []
    for k in range(per_half):
        group = half * per_half + k
        copies.append(
            pltpu.make_async_copy(
                x.at[:, pl.ds(pl.multiple_of(group * group_cols, group_cols), group_cols)],
                x_here.at[:, pl.ds(k * group_cols, group_cols)],
                sems.at[2 * k],
            )
        )
        copies.append(
            pltpu.make_async_copy(
                b.at[:, pl.ds(pl.multiple_of(group * states, states), states)],
                b_here.at[:, pl.ds(k * states, states)],
                sems.at[2 * k + 1],
            )
        )
    return copies


def half_states(half, x_here, b_here, copies, factor, log_total, out, matrix, dims):
    _, group_cols, states = dims
    rows, heads = factor.shape
    row = lax.broadcasted_iota(jnp.int32, (ROW_TILE, TILE), 0)
    operand = packed_half(jnp.concatenate([factor, jnp.exp2(log_total)], axis=0), half)
    for copy in copies:
        copy.wait()
    tiles = out.shape[1] // TILE
    per_group = group_cols // TILE
    matrices = {}
    factors = {}
    scaled = {}
    for n in range(tiles + 2 * AHEAD):
        if n < tiles:
            factors[n] = dot(operand, matrix[:, n * TILE : (n + 1) * TILE])
        m = n - AHEAD
        if 0 <= m < tiles:
            cols = slice(m * TILE, (m + 1) * TILE)
            spread = factors.pop(m)
            scaled[m] = (x_here[:, cols].astype(F32) * spread[:rows, :]).astype(BF16)
            high, low = high_low(spread[rows:, :])
            tail = jnp.where(row == 0, high, low)
            if m == 0:
                high, low = high_low(log_total)
                middle, low = high_low(low)
                at = row[:, :heads]
                logs = jnp.where(at == 2, high, jnp.where(at == 3, middle, low))
                logs = jnp.where(at < 2, tail[:, :heads], logs)
                tail = jnp.concatenate([logs, tail[:, heads:]], axis=1)
            out[states:, cols] = tail.astype(BF16)
            if m % per_group == 0:
                k = m // per_group
                matrices[k] = b_here[:, k * states : (k + 1) * states].T
        m = n - 2 * AHEAD
        if m >= 0:
            out[:states, m * TILE : (m + 1) * TILE] = dot(matrices[m // per_group], scaled.pop(m)).astype(BF16)


def send_state_kernel(
    half,
    chip,
    outer,
    x,
    b,
    step,
    log,
    out,
    run_out,
    run_t_out,
    factor_out,
    total_out,
    x_here,
    b_here,
    matrix,
    step_here,
    log_here,
    sems,
    *,
    dims,
):
    del chip, outer
    first = pltpu.make_async_copy(log, log_here, sems.at[2 * dims[0]])
    second = pltpu.make_async_copy(step, step_here, sems.at[2 * dims[0] + 1])
    first.start()
    second.start()
    copies = state_copies(half[0], x, b, x_here, b_here, sems, dims)
    for copy in copies:
        copy.start()
    rows, heads = log_here.shape
    half_spreader(matrix, x_here.shape[1] * CORES // heads)
    upto = lax.broadcasted_iota(jnp.int32, (rows, rows), 1) <= lax.broadcasted_iota(jnp.int32, (rows, rows), 0)
    first.wait()
    high, rest = high_low(log_here[...])
    middle, low = high_low(rest)
    parts = jnp.concatenate([high, middle, low], axis=1).astype(BF16)
    sums = dot(jnp.where(upto, 1.0, 0.0).astype(BF16), parts)
    running = (sums[:, :heads] + sums[:, heads : 2 * heads] + sums[:, 2 * heads :]) * LOG2E
    last = running[rows - 1 :, :]
    run_out[...] = running
    run_t_out[...] = running.T
    second.wait()
    factor = step_here[...] * jnp.exp2(last - running)
    total = jnp.broadcast_to(last, total_out.shape)
    factor_out[...] = factor
    total_out[...] = total
    half_states(half[0], x_here, b_here, copies, factor, total, out, matrix, dims)


def own_state_kernel(half, x, b, factor, total, out, matrix, x_here, b_here, sems, *, dims):
    copies = state_copies(half[0], x, b, x_here, b_here, sems, dims)
    for copy in copies:
        copy.start()
    half_spreader(matrix, x_here.shape[1] * CORES // factor.shape[1])
    half_states(half[0], x_here, b_here, copies, factor[...], total[...], out, matrix, dims)


def mixing_rows(first, own, got, states, cols):
    own_tail = own[states : states + 2, cols].astype(F32)
    got_tail = got[states : states + 2, cols].astype(F32)
    decay = jnp.where(first, got_tail, own_tail)
    decay = decay[:1, :] + decay[1:, :]
    one = jnp.ones_like(decay)
    return jnp.where(first, decay, one), jnp.where(first, one, decay)


def side_by_side(values, half):
    high, low = high_low(values)
    lane = lax.broadcasted_iota(jnp.int32, values.shape, 1)
    return jnp.where(lane < half, high, pltpu.roll(low, half, 1))


def chip_decay(first, got, total, states, base_out):
    heads = total.shape[1]
    half = heads // CORES
    partner = got[states + 2 : states + 3, :heads].astype(F32) + got[states + 3 : states + 4, :heads].astype(F32)
    partner = partner + got[states + 4 : states + 5, :heads].astype(F32)
    partner = jnp.broadcast_to(partner, total.shape)
    base_out[...] = jnp.where(first, jnp.zeros_like(partner), partner)
    both = jnp.exp2(total[...] + partner)
    both = jnp.where(first, both, pltpu.roll(both, half, 1))
    return side_by_side(both, half)


def chip_total_kernel(at, own, got, total, out, base_out):
    first = at[0] == 0
    cols = own.shape[1]
    states = out.shape[0]
    on_own, on_got = mixing_rows(first, own, got, states, slice(0, cols))
    for row in range(0, states, ROW_BLOCK):
        rows = slice(row, row + ROW_BLOCK)
        out[rows, :cols] = (on_own * own[rows, :].astype(F32) + on_got * got[rows, :].astype(F32)).astype(BF16)
    packed_decay = chip_decay(first, got, total, states, base_out)
    out[:, cols:] = jnp.concatenate([packed_decay] * (states // ROW_TILE), axis=0).astype(BF16)


def placed(kernel):
    def body(core, chip, outer, *refs, **options):
        return kernel((core[0], chip[0], outer[0]), *refs, **options)

    return body


def pieces_kernel(at, own, got, total, *outs, states, chunk, with_decay):
    base_out = outs[-1]
    first = at[0] == 0
    rows, cols = outs[0].shape
    cols = cols - total.shape[1] if with_decay else cols
    here = slice(chunk * cols, (chunk + 1) * cols)
    on_own, on_got = mixing_rows(first, own, got, states, here)
    packed_decay = chip_decay(first, got, total, states, base_out)
    for k, out in enumerate(outs[:-1]):
        start = pl.multiple_of(jnp.bitwise_xor(at[1], k) * rows, rows)
        for row in range(0, rows, ROW_BLOCK):
            take = pl.ds(start + row, ROW_BLOCK)
            mixed = on_own * own[take, here].astype(F32) + on_got * got[take, here].astype(F32)
            out[row : row + ROW_BLOCK, :cols] = mixed.astype(BF16)
        if with_decay:
            out[:, cols:] = jnp.concatenate([packed_decay] * (rows // ROW_TILE), axis=0).astype(BF16)


def decays_of(pieces, cols, first_head, width):
    lanes = pieces[0].shape[1] - cols
    sent = [piece[:ROW_TILE, cols:].astype(F32)[:1, :] for piece in pieces]
    sent = jnp.concatenate(sent + [jnp.zeros((ROW_TILE - len(sent), lanes), F32)], axis=0)
    values = sent + pltpu.roll(sent, lanes // CORES, 1)
    heads = cols // width
    here = pltpu.roll(values, lanes - first_head, 1) if first_head else values
    return values, dot(packed(here, heads), spreader(heads, width))


def column_kernel(at, *refs, first_head, width, count, with_decay):
    pieces, tails, out, decay_out = refs[:count], refs[count:-2], refs[-2], refs[-1]
    cols = decay_out.shape[1]
    rows = out.shape[0]
    values, decay = decays_of(tails, cols, first_head, width)
    decay_out[...] = decay
    for place in range(count):

        @pl.when(at[1] == place)
        def _():
            state = jnp.zeros((rows, cols), F32)
            for k in range(count):
                k = k ^ place
                state = decay[k : k + 1, :] * state + pieces[k][:, :cols].astype(F32)
            out[:, :cols] = state.astype(BF16)

    if with_decay:
        fill_decay(out, cols, values, count)


def fill_decay(out, cols, values, count):
    product = values[:1, :]
    for k in range(1, count):
        product = product * values[k : k + 1, :]
    product = side_by_side(jnp.broadcast_to(product, (ROW_TILE, product.shape[1])), product.shape[1] // CORES)
    out[:, cols:] = jnp.concatenate([product] * (out.shape[0] // ROW_TILE), axis=0).astype(BF16)


def chips_kernel(at, *refs, first_head, width, count, blocks):
    others, refs = refs[: blocks - 1], refs[blocks - 1 :]
    tails, decay, refs = refs[: blocks - 1], refs[blocks - 1], refs[blocks:]
    pieces, outs, carry = refs[:count], refs[count:-1], refs[-1]
    rows, cols = outs[0].shape
    _, passed = decays_of(tails, cols, first_head, width)
    for place in range(blocks):

        @pl.when(at[2] == place)
        def _():
            state = jnp.zeros((rows, cols), F32)
            for k in range(place):
                k = (k ^ place) - 1
                state = passed[k : k + 1, :] * state + others[k][:, :cols].astype(F32)
            carry[...] = state

    for place in range(count):

        @pl.when(at[1] == place)
        def _():
            state = carry[...]
            for k in range(count):
                k = k ^ place
                outs[k][...] = state.astype(BF16)
                state = decay[k : k + 1, :] * state + pieces[k][:, :cols].astype(F32)


def assemble_kernel(at, *refs, count):
    out = refs[-1]
    for n, piece in enumerate(refs[:-1]):
        rows, cols = piece.shape
        start = pl.multiple_of(jnp.bitwise_xor(at[1], n % count) * rows, rows)
        out[pl.ds(start, rows), n // count * cols : (n // count + 1) * cols] = piece[...]


def prefix_kernel(sent, out, here, sems, *, width, blocks):
    chips, rows, cols = here.shape
    heads = sent.shape[2] - cols
    half = heads // CORES
    step = cols // blocks
    first_rows = jnp.concatenate([sent[k, :1, cols:].astype(F32) for k in range(chips)], axis=0)
    values = first_rows + pltpu.roll(first_rows, half, 1)
    matrix = spreader(step // width, width)
    copies = []
    for block in range(blocks):
        lanes = slice(block * step, (block + 1) * step)
        head = block * step // width
        decay = dot(packed(pltpu.roll(values, heads - head, 1) if head else values, step // width), matrix)
        state = jnp.zeros((rows, step), F32)
        for k in range(chips):
            here[k, :, lanes] = state.astype(BF16)
            state = decay[k : k + 1, :] * state + sent[k, :, lanes].astype(F32)
        copies.append(
            pltpu.make_async_copy(
                here.at[:, :, pl.ds(block * step, step)], out.at[:, :, pl.ds(block * step, step)], sems.at[block]
            )
        )
        copies[-1].start()
    for copy in copies:
        copy.wait()


def within_kernel(
    half, flag, x_ref, b_ref, c_ref, step_ref, run_ref, run_t_ref, skip_ref, before_ref, out, matrix, *, dims, first_group
):
    per_half, per_group, width = dims
    turn = pl.program_id(0)
    place = first_group + turn
    head = (half[0] * per_half + place) * per_group
    rows = x_ref.shape[0]
    pair = LANES // width
    group_cols = per_group * width
    states = b_ref.shape[1] // per_half
    x_ref = x_ref.at[:, pl.ds(pl.multiple_of(place * group_cols, group_cols), group_cols)]
    b_ref = b_ref.at[:, pl.ds(pl.multiple_of(place * states, states), states)]
    c_ref = c_ref.at[:, pl.ds(pl.multiple_of((half[0] * per_half + place) * states, states), states)]
    before_ref = before_ref.at[:states, pl.ds(pl.multiple_of(place * group_cols, group_cols), group_cols)]
    out = out.at[:, pl.ds(pl.multiple_of(turn * group_cols, group_cols), group_cols)]

    @pl.when(turn == 0)
    def _():
        matrix[...] = spreader(per_group, width)

    def spread(values):
        return dot(packed(values, per_group), matrix[...])

    step = group_first(step_ref[...], head)
    run = group_first(run_ref[...], head)
    skip = group_first(jnp.broadcast_to(skip_ref[...], (ROW_TILE, skip_ref.shape[1])), head)
    run_t = run_t_ref[pl.ds(pl.multiple_of(head, per_group), per_group), :]
    x = x_ref[...].astype(F32)
    scaled = (x * spread(step)).astype(BF16)
    before = dot(c_ref[...], before_ref[...] * flag[0].astype(BF16))
    outer = spread(skip)[:1, :] * x + spread(jnp.exp2(run)) * before
    lane = lax.broadcasted_iota(jnp.int32, (HALF_ROWS, LANES), 1) // width
    lower = lax.broadcasted_iota(jnp.int32, (HALF_ROWS, HALF_ROWS), 1) <= lax.broadcasted_iota(
        jnp.int32, (HALF_ROWS, HALF_ROWS), 0
    )
    b = b_ref[...]
    c = c_ref[...]
    for start in range(0, rows, HALF_ROWS):
        stop = start + HALF_ROWS
        scores = jnp.where(lower, dot(c[start:stop, :], b[start:stop, :], (1, 1)), 0.0)
        added = outer[start:stop, :]
        if start:
            edge = run[start - 1 : start, :]
            lead = spread(step[:start, :] * jnp.exp2(edge - run[:start, :]))
            lead = (x[:start, :] * lead).astype(BF16)
            cross = dot(c[start:stop, :], b[:start, :], (1, 1)).astype(BF16)
            added = added + spread(jnp.exp2(run[start:stop, :] - edge)) * dot(cross, lead)
        for first in range(0, per_group, pair):
            cols = slice(first * width, (first + pair) * width)
            here = scaled[start:stop, cols]
            weights = []
            values = []
            for k in range(pair):
                at = first + k
                gap = run[start:stop, at : at + 1] - run_t[at : at + 1, start:stop]
                weights.append((scores * jnp.exp2(jnp.minimum(gap, 0.0))).astype(BF16))
                values.append(jnp.where(lane == k, here, jnp.zeros_like(here)))
            part = dot(jnp.concatenate(weights, axis=1), jnp.concatenate(values, axis=0))
            out[start:stop, cols] = (added[:, cols] + part).astype(BF16)


def own_final_kernel(half, c, state, run, base, matrix, within, result, *, dims):
    add_carried(half[0], c, state, run, base, matrix, within, result, dims, lambda k: None)


def final_kernel(half, c, state, run, base, matrix, within, own_result, *refs, dims):
    out, result, sems = refs[-3:]
    per_half, group_cols, _, first = dims
    count = state.shape[1] // group_cols
    copies = []

    def send(source, side, k, sem):
        home = pl.multiple_of((side * per_half + first + k) * group_cols, group_cols)
        copies.append(
            pltpu.make_async_copy(
                source.at[:, pl.ds(k * group_cols, group_cols)], out.at[:, pl.ds(home, group_cols)], sems.at[sem]
            )
        )
        copies[-1].start()

    for k in range(count):
        send(own_result, 1 - half[0], k, count + k)
    add_carried(
        half[0], c, state, run, base, matrix, within, result, dims, lambda k: send(result, half[0], k, k)
    )
    for copy in copies:
        copy.wait()


def add_carried(half, c, state, run, base, matrix, within, result, dims, when_done):
    per_half, group_cols, states, first = dims
    operand = packed_half(jnp.exp2(run[...] + base[:1, :]), half)
    for k in range(state.shape[1] // group_cols):
        group = half * per_half + first + k
        rows = c[:, pl.ds(pl.multiple_of(group * states, states), states)]
        tiles = group_cols // TILE
        products = {}
        for n in range(tiles + AHEAD):
            if n < tiles:
                start = k * group_cols + n * TILE
                spread = matrix[:, first * group_cols + start : first * group_cols + start + TILE]
                products[n] = dot(rows, state[:, start : start + TILE]), dot(operand, spread)
            m = n - AHEAD
            if m >= 0:
                cols = slice(k * group_cols + m * TILE, k * group_cols + (m + 1) * TILE)
                carried, factor = products.pop(m)
                result[:, cols] = (within[:, cols].astype(F32) + factor * carried).astype(BF16)
        when_done(k)


def small_call(kernel, in_specs, out_shape, scratch=(), out_specs=None):
    return pl.pallas_call(
        kernel,
        in_specs=in_specs,
        out_specs=out_specs or [pl.BlockSpec(memory_space=pltpu.VMEM)] * len(out_shape),
        out_shape=out_shape,
        scratch_shapes=list(scratch),
        compiler_params=plain_params(),
    )


def xor_route(size, k):
    return [(i, i ^ k) for i in range(size)]


def swapped(arrays, axis):
    size = lax.axis_size(axis)
    done = {0: arrays[0]}
    for k in range(1, size):
        done[k] = lax.ppermute(arrays[k], axis, xor_route(size, k))
    return [done[k] for k in range(size)]


def entering_by_swaps(at, own, got, total, width, states, outer_axis, chip_axis):
    half_cols = own.shape[1]
    heads = total.shape[1]
    count = lax.axis_size(chip_axis)
    blocks = lax.axis_size(outer_axis)
    rows = states // count
    cols = half_cols // CHUNKS
    smem = pl.BlockSpec(memory_space=pltpu.SMEM)
    vmem = pl.BlockSpec(memory_space=pltpu.VMEM)
    shape = jax.ShapeDtypeStruct
    gathered = {}
    lead = CHUNKS - 1
    for chunk in reversed(range(CHUNKS)):
        extra = heads if chunk == lead else 0
        *pieces, base = small_call(
            functools.partial(placed(pieces_kernel), states=states, chunk=chunk, with_decay=chunk == lead),
            [smem] * 3 + [vmem] * 3,
            [shape((rows, cols + extra), BF16)] * count + [shape((ROW_TILE, heads), F32)],
        )(*at, own, got, total)
        gathered[chunk] = swapped(pieces, chip_axis)
    entering = {}
    for chunk in reversed(range(CHUNKS)):
        extra = heads if chunk == lead else 0
        first_head = chunk * cols // width
        pieces = gathered[chunk]
        column, decay = small_call(
            functools.partial(placed(column_kernel), first_head=first_head, width=width, count=count, with_decay=chunk == lead),
            [smem] * 3 + [vmem] * (2 * count),
            [shape((rows, cols + extra), BF16), shape((ROW_TILE, cols), F32)],
        )(*at, *pieces, *gathered[lead])
        others = swapped([column] * blocks, outer_axis)[1:]
        if chunk == lead:
            tails = others
        states_out = small_call(
            functools.partial(
                placed(chips_kernel), first_head=first_head, width=width, count=count, blocks=blocks
            ),
            [smem] * 3 + [vmem] * (count + 2 * blocks - 1),
            [shape((rows, cols), BF16)] * count,
            [pltpu.VMEM((rows, cols), F32)],
        )(*at, *others, *tails, decay, *pieces)
        states_out = swapped(states_out, chip_axis)
        (entering[chunk],) = small_call(
            functools.partial(placed(assemble_kernel), count=count),
            [smem] * 3 + [vmem] * count,
            [shape((states, cols), BF16)],
        )(*at, *states_out)
    return entering, base


def entering_by_all_to_all(at, own, got, total, width, states, outer_axis, chip_axis):
    half_cols = own.shape[1]
    heads = total.shape[1]
    chips = lax.axis_size((outer_axis, chip_axis))
    rows = states // chips
    smem = pl.BlockSpec(memory_space=pltpu.SMEM)
    vmem = pl.BlockSpec(memory_space=pltpu.VMEM)
    chip_total, base = small_call(
        placed(chip_total_kernel),
        [smem] * 3 + [vmem] * 3,
        [jax.ShapeDtypeStruct((states, half_cols + heads), BF16), jax.ShapeDtypeStruct((ROW_TILE, heads), F32)],
    )(*at, own, got, total)
    sent = lax.all_to_all(
        chip_total.reshape(chips, rows, half_cols + heads),
        (outer_axis, chip_axis),
        split_axis=0,
        concat_axis=0,
        tiled=True,
    )
    blocks = GROUPS // CORES
    (entering,) = small_call(
        functools.partial(prefix_kernel, width=width, blocks=blocks),
        [vmem],
        [pltpu.HBM((chips, rows, half_cols), BF16)],
        [pltpu.VMEM((chips, rows, half_cols), BF16), pltpu.SemaphoreType.DMA((blocks,))],
        [pl.BlockSpec(memory_space=pltpu.HBM)],
    )(sent)
    entering = lax.all_to_all(entering, (outer_axis, chip_axis), split_axis=0, concat_axis=0, tiled=True)
    entering = entering.reshape(states, half_cols)
    return jnp.split(entering, CHUNKS, axis=1), base


def local(inputs, step_size, log_decay, b_matrix, c_matrix, skip_gain, *, outer_axis, chip_axis, core_axis):
    tokens, channels = inputs.shape
    heads = step_size.shape[1]
    width = channels // heads
    states = b_matrix.shape[1] // GROUPS
    per_group = heads // GROUPS
    group_cols = per_group * width
    per_half = GROUPS // CORES
    half_cols = channels // CORES
    chips = lax.axis_size((outer_axis, chip_axis))
    by_swaps = lax.axis_size(outer_axis) == 4 and chips == 16
    tall = states + ROW_TILE

    core = lax.axis_index(core_axis).astype(jnp.int32)
    mine = core.reshape(1)
    other = (1 - core).reshape(1)
    at = (mine,) + tuple(lax.axis_index(axis).astype(jnp.int32).reshape(1) for axis in (chip_axis, outer_axis))

    smem = pl.BlockSpec(memory_space=pltpu.SMEM)
    vmem = pl.BlockSpec(memory_space=pltpu.VMEM)
    hbm = pl.BlockSpec(memory_space=pltpu.HBM)

    state_dims = (per_half, group_cols, states)
    half_dims = (per_half, per_group, width)
    half_inputs = [
        jax.ShapeDtypeStruct((tokens, half_cols), BF16),
        jax.ShapeDtypeStruct((tokens, per_half * states), BF16),
    ]

    whole_step = step_size
    inputs, step_size, log_decay, b_matrix = (
        pltpu.with_memory_space_constraint(array, pltpu.HBM) for array in (inputs, step_size, log_decay, b_matrix)
    )
    send, run, run_t, factor, total, other_x, other_b = pl.pallas_call(
        functools.partial(send_state_kernel, dims=state_dims),
        in_specs=[smem] * 3 + [hbm] * 4,
        out_specs=[vmem] * 7,
        out_shape=[
            jax.ShapeDtypeStruct((tall, half_cols), BF16),
            jax.ShapeDtypeStruct((tokens, heads), F32),
            jax.ShapeDtypeStruct((heads, tokens), F32),
            jax.ShapeDtypeStruct((tokens, heads), F32),
            jax.ShapeDtypeStruct((ROW_TILE, heads), F32),
        ]
        + half_inputs,
        scratch_shapes=[pltpu.VMEM((heads, half_cols), BF16)]
        + [pltpu.VMEM((tokens, heads), F32)] * 2
        + [pltpu.SemaphoreType.DMA((2 * per_half + 2,))],
        compiler_params=plain_params(),
        name="send_state",
    )(other, *at[1:], inputs, b_matrix, step_size, log_decay)

    swap = [(0, 1), (1, 0)]
    got = lax.ppermute(send, core_axis, swap)

    own, matrix, own_x, own_b = small_call(
        functools.partial(own_state_kernel, dims=state_dims),
        [smem, hbm, hbm, vmem, vmem],
        [jax.ShapeDtypeStruct((tall, half_cols), BF16), jax.ShapeDtypeStruct((heads, half_cols), BF16)] + half_inputs,
        [pltpu.SemaphoreType.DMA((2 * per_half,))],
    )(mine, inputs, b_matrix, factor, total)

    find_entering = entering_by_swaps if by_swaps else entering_by_all_to_all
    entering, base = find_entering(at, own, got, total, width, states, outer_axis, chip_axis)
    late = lax.ppermute(own, core_axis, swap[:1])

    def within(half, x, b, before, first):
        return pl.pallas_call(
            functools.partial(within_kernel, dims=half_dims, first_group=first),
            grid_spec=pltpu.PrefetchScalarGridSpec(
                num_scalar_prefetch=2,
                grid=(PER_CALL,),
                in_specs=[vmem] * 8,
                out_specs=vmem,
                scratch_shapes=[pltpu.VMEM((2 * per_group, group_cols), BF16)],
            ),
            out_shape=jax.ShapeDtypeStruct((tokens, PER_CALL * group_cols), BF16),
            compiler_params=params(),
            name="within",
        )(
            half,
            mine,
            x,
            b,
            c_matrix,
            whole_step,
            run,
            run_t,
            skip_gain.reshape(1, heads),
            before,
        )

    own_within = []
    other_within = []
    for first in range(0, per_half, PER_CALL):
        own_within.append(within(mine, own_x, own_b, got, first))
        other_within.append(within(other, other_x, other_b, late, first))

    mixed = jax.ShapeDtypeStruct((tokens, channels), BF16)

    cols = PER_CALL * group_cols

    def finish_own(chunk, state, part):
        return small_call(
            functools.partial(own_final_kernel, dims=state_dims + (chunk * PER_CALL,)),
            [smem] + [vmem] * 6,
            [jax.ShapeDtypeStruct((tokens, cols), BF16)],
        )(mine, c_matrix, state, run, base, matrix, part)

    def finish_other(chunk, state, part, own_result, *result):
        return pl.pallas_call(
            functools.partial(final_kernel, dims=state_dims + (chunk * PER_CALL,)),
            in_specs=[smem] + [vmem] * 7 + [hbm] * len(result),
            out_specs=hbm,
            out_shape=mixed,
            scratch_shapes=[pltpu.VMEM((tokens, cols), BF16), pltpu.SemaphoreType.DMA((2 * PER_CALL,))],
            input_output_aliases={8: 0} if result else {},
            compiler_params=plain_params(),
            name="finish_other",
        )(other, c_matrix, state, run, base, matrix, part, own_result, *result)

    result = ()
    for chunk in reversed(range(CHUNKS)):
        got_entering = lax.ppermute(entering[chunk], core_axis, swap)
        (own_result,) = finish_own(chunk, entering[chunk], own_within[chunk])
        result = (finish_other(chunk, got_entering, other_within[chunk], own_result, *result),)
    return result[0]


def solution(mesh):
    outer, inner = mesh.axis_names
    chip_mesh = Mesh(
        mesh.devices.reshape(mesh.shape[outer], mesh.shape[inner] // CORES, CORES), (outer, "chip", "core")
    )
    placed = P((outer, "chip", "core"), None)

    def body(*args):
        return local(*args, outer_axis=outer, chip_axis="chip", core_axis="core")

    return jax.shard_map(body, mesh=chip_mesh, in_specs=(placed,) * 5 + (P(),), out_specs=placed, check_vma=False)
```

```python
import functools
import math

import jax
import jax.numpy as jnp
from jax import lax
from jax.experimental import pallas as pl
from jax.experimental.pallas import tpu as pltpu
from jax.sharding import Mesh, PartitionSpec as P


GROUPS = 8
CORES = 2
LANES = 128
TILE = 256
AHEAD = 2
CHUNKS = 2
PER_CALL = 2
ROW_TILE = 8
HALF_ROWS = 128
ROW_BLOCK = 16
VMEM_LIMIT = 24 * 1024 * 1024
LOG2E = 1.0 / math.log(2.0)

F32 = jnp.float32
BF16 = jnp.bfloat16


def dot(a, b, contract=(1, 0)):
    dims = (((contract[0],), (contract[1],)), ((), ()))
    return lax.dot_general(a, b, dims, preferred_element_type=F32)


def high_low(values):
    high = values.astype(BF16).astype(F32)
    return high, values - high


def spreader(heads, width):
    shape = (2 * heads, heads * width)
    row = lax.broadcasted_iota(jnp.int32, shape, 0)
    col = lax.broadcasted_iota(jnp.int32, shape, 1)
    row = jnp.where(row >= heads, row - heads, row)
    return jnp.where(row == col // width, 1.0, 0.0).astype(BF16)


def group_first(values, head):
    lanes = values.shape[1]
    return pltpu.roll(values, lax.rem(lanes - head, lanes), 1)


def packed(values, heads):
    high, low = high_low(values)
    lane = lax.broadcasted_iota(jnp.int32, values.shape, 1)
    return jnp.where(lane < heads, high, pltpu.roll(low, heads, 1)).astype(BF16)[:, : 2 * heads]


def half_spreader(matrix, width):
    lanes, cols = matrix.shape
    for start in range(0, cols, TILE):
        row = lax.broadcasted_iota(jnp.int32, (lanes, TILE), 0)
        col = start + lax.broadcasted_iota(jnp.int32, (lanes, TILE), 1)
        row = jnp.where(row >= lanes // 2, row - lanes // 2, row)
        matrix[:, start : start + TILE] = jnp.where(row == col // width, 1.0, 0.0).astype(BF16)


def packed_half(values, half):
    lanes = values.shape[1]
    values = group_first(values, half * (lanes // 2))
    high, low = high_low(values)
    lane = lax.broadcasted_iota(jnp.int32, values.shape, 1)
    return jnp.where(lane < lanes // 2, high, pltpu.roll(low, lanes // 2, 1)).astype(BF16)


def params():
    return pltpu.CompilerParams(dimension_semantics=("arbitrary",), vmem_limit_bytes=VMEM_LIMIT)


def plain_params():
    return pltpu.CompilerParams(vmem_limit_bytes=VMEM_LIMIT)


def state_copies(half, x, b, x_here, b_here, sems, dims):
    per_half, group_cols, states = dims
    copies = []
    for k in range(per_half):
        group = half * per_half + k
        copies.append(
            pltpu.make_async_copy(
                x.at[:, pl.ds(pl.multiple_of(group * group_cols, group_cols), group_cols)],
                x_here.at[:, pl.ds(k * group_cols, group_cols)],
                sems.at[2 * k],
            )
        )
        copies.append(
            pltpu.make_async_copy(
                b.at[:, pl.ds(pl.multiple_of(group * states, states), states)],
                b_here.at[:, pl.ds(k * states, states)],
                sems.at[2 * k + 1],
            )
        )
    return copies


def half_states(half, x_here, b_here, copies, factor, log_total, out, matrix, dims):
    _, group_cols, states = dims
    rows, heads = factor.shape
    row = lax.broadcasted_iota(jnp.int32, (ROW_TILE, TILE), 0)
    operand = packed_half(jnp.concatenate([factor, jnp.exp2(log_total)], axis=0), half)
    for copy in copies:
        copy.wait()
    tiles = out.shape[1] // TILE
    per_group = group_cols // TILE
    matrices = {}
    factors = {}
    scaled = {}
    for n in range(tiles + 2 * AHEAD):
        if n < tiles:
            factors[n] = dot(operand, matrix[:, n * TILE : (n + 1) * TILE])
        m = n - AHEAD
        if 0 <= m < tiles:
            cols = slice(m * TILE, (m + 1) * TILE)
            spread = factors.pop(m)
            scaled[m] = (x_here[:, cols].astype(F32) * spread[:rows, :]).astype(BF16)
            high, low = high_low(spread[rows:, :])
            tail = jnp.where(row == 0, high, low)
            if m == 0:
                high, low = high_low(log_total)
                middle, low = high_low(low)
                at = row[:, :heads]
                logs = jnp.where(at == 2, high, jnp.where(at == 3, middle, low))
                logs = jnp.where(at < 2, tail[:, :heads], logs)
                tail = jnp.concatenate([logs, tail[:, heads:]], axis=1)
            out[states:, cols] = tail.astype(BF16)
            if m % per_group == 0:
                k = m // per_group
                matrices[k] = b_here[:, k * states : (k + 1) * states].T
        m = n - 2 * AHEAD
        if m >= 0:
            out[:states, m * TILE : (m + 1) * TILE] = dot(matrices[m // per_group], scaled.pop(m)).astype(BF16)


def send_state_kernel(
    half,
    chip,
    outer,
    x,
    b,
    step,
    log,
    out,
    run_out,
    run_t_out,
    factor_out,
    total_out,
    x_here,
    b_here,
    matrix,
    step_here,
    log_here,
    sems,
    *,
    dims,
):
    del chip, outer
    first = pltpu.make_async_copy(log, log_here, sems.at[2 * dims[0]])
    second = pltpu.make_async_copy(step, step_here, sems.at[2 * dims[0] + 1])
    first.start()
    second.start()
    copies = state_copies(half[0], x, b, x_here, b_here, sems, dims)
    for copy in copies:
        copy.start()
    rows, heads = log_here.shape
    half_spreader(matrix, x_here.shape[1] * CORES // heads)
    upto = lax.broadcasted_iota(jnp.int32, (rows, rows), 1) <= lax.broadcasted_iota(jnp.int32, (rows, rows), 0)
    first.wait()
    high, rest = high_low(log_here[...])
    middle, low = high_low(rest)
    parts = jnp.concatenate([high, middle, low], axis=1).astype(BF16)
    sums = dot(jnp.where(upto, 1.0, 0.0).astype(BF16), parts)
    running = (sums[:, :heads] + sums[:, heads : 2 * heads] + sums[:, 2 * heads :]) * LOG2E
    last = running[rows - 1 :, :]
    run_out[...] = running
    run_t_out[...] = running.T
    second.wait()
    factor = step_here[...] * jnp.exp2(last - running)
    total = jnp.broadcast_to(last, total_out.shape)
    factor_out[...] = factor
    total_out[...] = total
    half_states(half[0], x_here, b_here, copies, factor, total, out, matrix, dims)


def own_state_kernel(half, x, b, factor, total, out, matrix, x_here, b_here, sems, *, dims):
    copies = state_copies(half[0], x, b, x_here, b_here, sems, dims)
    for copy in copies:
        copy.start()
    half_spreader(matrix, x_here.shape[1] * CORES // factor.shape[1])
    half_states(half[0], x_here, b_here, copies, factor[...], total[...], out, matrix, dims)


def mixing_rows(first, own, got, states, cols):
    own_tail = own[states : states + 2, cols].astype(F32)
    got_tail = got[states : states + 2, cols].astype(F32)
    decay = jnp.where(first, got_tail, own_tail)
    decay = decay[:1, :] + decay[1:, :]
    one = jnp.ones_like(decay)
    return jnp.where(first, decay, one), jnp.where(first, one, decay)


def side_by_side(values, half):
    high, low = high_low(values)
    lane = lax.broadcasted_iota(jnp.int32, values.shape, 1)
    return jnp.where(lane < half, high, pltpu.roll(low, half, 1))


def chip_decay(first, got, total, states, base_out):
    heads = total.shape[1]
    half = heads // CORES
    partner = got[states + 2 : states + 3, :heads].astype(F32) + got[states + 3 : states + 4, :heads].astype(F32)
    partner = partner + got[states + 4 : states + 5, :heads].astype(F32)
    partner = jnp.broadcast_to(partner, total.shape)
    base_out[...] = jnp.where(first, jnp.zeros_like(partner), partner)
    both = jnp.exp2(total[...] + partner)
    both = jnp.where(first, both, pltpu.roll(both, half, 1))
    return side_by_side(both, half)


def chip_total_kernel(at, own, got, total, out, base_out):
    first = at[0] == 0
    cols = own.shape[1]
    states = out.shape[0]
    on_own, on_got = mixing_rows(first, own, got, states, slice(0, cols))
    for row in range(0, states, ROW_BLOCK):
        rows = slice(row, row + ROW_BLOCK)
        out[rows, :cols] = (on_own * own[rows, :].astype(F32) + on_got * got[rows, :].astype(F32)).astype(BF16)
    packed_decay = chip_decay(first, got, total, states, base_out)
    out[:, cols:] = jnp.concatenate([packed_decay] * (states // ROW_TILE), axis=0).astype(BF16)


def placed(kernel):
    def body(core, chip, outer, *refs, **options):
        return kernel((core[0], chip[0], outer[0]), *refs, **options)

    return body


def pieces_kernel(at, own, got, *refs, states, chunk, count):
    first = at[0] == 0
    outs = refs[-count - 1 : -1] if len(refs) > count else refs
    rows, cols = outs[0].shape
    if len(refs) > count:
        total, base_out = refs[0], refs[-1]
        cols = cols - total.shape[1]
        packed_decay = chip_decay(first, got, total, states, base_out)
        for out in outs:
            out[:, cols:] = jnp.concatenate([packed_decay] * (rows // ROW_TILE), axis=0).astype(BF16)
    here = slice(chunk * cols, (chunk + 1) * cols)
    on_own, on_got = mixing_rows(first, own, got, states, here)
    for k, out in enumerate(outs):
        start = pl.multiple_of(jnp.bitwise_xor(at[1], k) * rows, rows)
        for row in range(0, rows, ROW_BLOCK):
            take = pl.ds(start + row, ROW_BLOCK)
            mixed = on_own * own[take, here].astype(F32) + on_got * got[take, here].astype(F32)
            out[row : row + ROW_BLOCK, :cols] = mixed.astype(BF16)


def decays_of(pieces, cols, first_head, width):
    lanes = pieces[0].shape[1] - cols
    sent = [piece[:ROW_TILE, cols:].astype(F32)[:1, :] for piece in pieces]
    sent = jnp.concatenate(sent + [jnp.zeros((ROW_TILE - len(sent), lanes), F32)], axis=0)
    values = sent + pltpu.roll(sent, lanes // CORES, 1)
    heads = cols // width
    here = pltpu.roll(values, lanes - first_head, 1) if first_head else values
    return values, dot(packed(here, heads), spreader(heads, width))


def column_kernel(at, *refs, first_head, width, count, with_decay):
    pieces, tails, out, decay_out = refs[:count], refs[count:-2], refs[-2], refs[-1]
    cols = decay_out.shape[1]
    rows = out.shape[0]
    values, decay = decays_of(tails, cols, first_head, width)
    decay_out[...] = decay
    for place in range(count):

        @pl.when(at[1] == place)
        def _():
            state = jnp.zeros((rows, cols), F32)
            for k in range(count):
                k = k ^ place
                state = decay[k : k + 1, :] * state + pieces[k][:, :cols].astype(F32)
            out[:, :cols] = state.astype(BF16)

    if with_decay:
        fill_decay(out, cols, values, count)


def fill_decay(out, cols, values, count):
    product = values[:1, :]
    for k in range(1, count):
        product = product * values[k : k + 1, :]
    product = side_by_side(jnp.broadcast_to(product, (ROW_TILE, product.shape[1])), product.shape[1] // CORES)
    out[:, cols:] = jnp.concatenate([product] * (out.shape[0] // ROW_TILE), axis=0).astype(BF16)


def chips_kernel(at, *refs, first_head, width, count, blocks):
    others, refs = refs[: blocks - 1], refs[blocks - 1 :]
    tails, decay, refs = refs[: blocks - 1], refs[blocks - 1], refs[blocks:]
    pieces, outs, carry = refs[:count], refs[count:-1], refs[-1]
    rows, cols = outs[0].shape
    _, passed = decays_of(tails, cols, first_head, width)
    for place in range(blocks):

        @pl.when(at[2] == place)
        def _():
            state = jnp.zeros((rows, cols), F32)
            for k in range(place):
                k = (k ^ place) - 1
                state = passed[k : k + 1, :] * state + others[k][:, :cols].astype(F32)
            carry[...] = state

    for place in range(count):

        @pl.when(at[1] == place)
        def _():
            state = carry[...]
            for k in range(count):
                k = k ^ place
                outs[k][...] = state.astype(BF16)
                state = decay[k : k + 1, :] * state + pieces[k][:, :cols].astype(F32)


def assemble_kernel(at, *refs, count):
    out = refs[-1]
    for n, piece in enumerate(refs[:-1]):
        rows, cols = piece.shape
        start = pl.multiple_of(jnp.bitwise_xor(at[1], n % count) * rows, rows)
        out[pl.ds(start, rows), n // count * cols : (n // count + 1) * cols] = piece[...]


def prefix_kernel(sent, out, here, sems, *, width, blocks):
    chips, rows, cols = here.shape
    heads = sent.shape[2] - cols
    half = heads // CORES
    step = cols // blocks
    first_rows = jnp.concatenate([sent[k, :1, cols:].astype(F32) for k in range(chips)], axis=0)
    values = first_rows + pltpu.roll(first_rows, half, 1)
    matrix = spreader(step // width, width)
    copies = []
    for block in range(blocks):
        lanes = slice(block * step, (block + 1) * step)
        head = block * step // width
        decay = dot(packed(pltpu.roll(values, heads - head, 1) if head else values, step // width), matrix)
        state = jnp.zeros((rows, step), F32)
        for k in range(chips):
            here[k, :, lanes] = state.astype(BF16)
            state = decay[k : k + 1, :] * state + sent[k, :, lanes].astype(F32)
        copies.append(
            pltpu.make_async_copy(
                here.at[:, :, pl.ds(block * step, step)], out.at[:, :, pl.ds(block * step, step)], sems.at[block]
            )
        )
        copies[-1].start()
    for copy in copies:
        copy.wait()


def within_kernel(
    half, flag, x_ref, b_ref, c_ref, step_ref, run_ref, run_t_ref, skip_ref, before_ref, out, matrix, *, dims, first_group
):
    per_half, per_group, width = dims
    turn = pl.program_id(0)
    place = first_group + turn
    head = (half[0] * per_half + place) * per_group
    rows = x_ref.shape[0]
    pair = LANES // width
    group_cols = per_group * width
    states = b_ref.shape[1] // per_half
    x_ref = x_ref.at[:, pl.ds(pl.multiple_of(place * group_cols, group_cols), group_cols)]
    b_ref = b_ref.at[:, pl.ds(pl.multiple_of(place * states, states), states)]
    c_ref = c_ref.at[:, pl.ds(pl.multiple_of((half[0] * per_half + place) * states, states), states)]
    before_ref = before_ref.at[:states, pl.ds(pl.multiple_of(place * group_cols, group_cols), group_cols)]
    out = out.at[:, pl.ds(pl.multiple_of(turn * group_cols, group_cols), group_cols)]

    @pl.when(turn == 0)
    def _():
        matrix[...] = spreader(per_group, width)

    def spread(values):
        return dot(packed(values, per_group), matrix[...])

    step = group_first(step_ref[...], head)
    run = group_first(run_ref[...], head)
    skip = group_first(jnp.broadcast_to(skip_ref[...], (ROW_TILE, skip_ref.shape[1])), head)
    run_t = run_t_ref[pl.ds(pl.multiple_of(head, per_group), per_group), :]
    x = x_ref[...].astype(F32)
    scaled = (x * spread(step)).astype(BF16)
    before = dot(c_ref[...], before_ref[...] * flag[0].astype(BF16))
    outer = spread(skip)[:1, :] * x + spread(jnp.exp2(run)) * before
    lane = lax.broadcasted_iota(jnp.int32, (HALF_ROWS, LANES), 1) // width
    lower = lax.broadcasted_iota(jnp.int32, (HALF_ROWS, HALF_ROWS), 1) <= lax.broadcasted_iota(
        jnp.int32, (HALF_ROWS, HALF_ROWS), 0
    )
    b = b_ref[...]
    c = c_ref[...]
    for start in range(0, rows, HALF_ROWS):
        stop = start + HALF_ROWS
        scores = jnp.where(lower, dot(c[start:stop, :], b[start:stop, :], (1, 1)), 0.0)
        added = outer[start:stop, :]
        if start:
            edge = run[start - 1 : start, :]
            lead = spread(step[:start, :] * jnp.exp2(edge - run[:start, :]))
            lead = (x[:start, :] * lead).astype(BF16)
            cross = dot(c[start:stop, :], b[:start, :], (1, 1)).astype(BF16)
            added = added + spread(jnp.exp2(run[start:stop, :] - edge)) * dot(cross, lead)
        for first in range(0, per_group, pair):
            cols = slice(first * width, (first + pair) * width)
            here = scaled[start:stop, cols]
            weights = []
            values = []
            for k in range(pair):
                at = first + k
                gap = run[start:stop, at : at + 1] - run_t[at : at + 1, start:stop]
                weights.append((scores * jnp.exp2(jnp.minimum(gap, 0.0))).astype(BF16))
                values.append(jnp.where(lane == k, here, jnp.zeros_like(here)))
            part = dot(jnp.concatenate(weights, axis=1), jnp.concatenate(values, axis=0))
            out[start:stop, cols] = (added[:, cols] + part).astype(BF16)


def own_final_kernel(half, c, state, run, base, matrix, within, result, *, dims):
    add_carried(half[0], c, state, run, base, matrix, within, result, dims, lambda k: None)


def final_kernel(half, c, state, run, base, matrix, within, own_result, *refs, dims):
    out, result, sems = refs[-3:]
    per_half, group_cols, _, first = dims
    count = state.shape[1] // group_cols
    copies = []

    def send(source, side, k, sem):
        home = pl.multiple_of((side * per_half + first + k) * group_cols, group_cols)
        copies.append(
            pltpu.make_async_copy(
                source.at[:, pl.ds(k * group_cols, group_cols)], out.at[:, pl.ds(home, group_cols)], sems.at[sem]
            )
        )
        copies[-1].start()

    for k in range(count):
        send(own_result, 1 - half[0], k, count + k)
    add_carried(
        half[0], c, state, run, base, matrix, within, result, dims, lambda k: send(result, half[0], k, k)
    )
    for copy in copies:
        copy.wait()


def add_carried(half, c, state, run, base, matrix, within, result, dims, when_done):
    per_half, group_cols, states, first = dims
    operand = packed_half(jnp.exp2(run[...] + base[:1, :]), half)
    for k in range(state.shape[1] // group_cols):
        group = half * per_half + first + k
        rows = c[:, pl.ds(pl.multiple_of(group * states, states), states)]
        tiles = group_cols // TILE
        products = {}
        for n in range(tiles + AHEAD):
            if n < tiles:
                start = k * group_cols + n * TILE
                spread = matrix[:, first * group_cols + start : first * group_cols + start + TILE]
                products[n] = dot(rows, state[:, start : start + TILE]), dot(operand, spread)
            m = n - AHEAD
            if m >= 0:
                cols = slice(k * group_cols + m * TILE, k * group_cols + (m + 1) * TILE)
                carried, factor = products.pop(m)
                result[:, cols] = (within[:, cols].astype(F32) + factor * carried).astype(BF16)
        when_done(k)


def small_call(kernel, in_specs, out_shape, scratch=(), out_specs=None):
    return pl.pallas_call(
        kernel,
        in_specs=in_specs,
        out_specs=out_specs or [pl.BlockSpec(memory_space=pltpu.VMEM)] * len(out_shape),
        out_shape=out_shape,
        scratch_shapes=list(scratch),
        compiler_params=plain_params(),
    )


def xor_route(size, k):
    return [(i, i ^ k) for i in range(size)]


def swapped(arrays, axis):
    size = lax.axis_size(axis)
    done = {0: arrays[0]}
    for k in range(1, size):
        done[k] = lax.ppermute(arrays[k], axis, xor_route(size, k))
    return [done[k] for k in range(size)]


def entering_by_swaps(at, own, got, total, width, states, outer_axis, chip_axis):
    half_cols = own.shape[1]
    heads = total.shape[1]
    count = lax.axis_size(chip_axis)
    blocks = lax.axis_size(outer_axis)
    rows = states // count
    cols = half_cols // CHUNKS
    smem = pl.BlockSpec(memory_space=pltpu.SMEM)
    vmem = pl.BlockSpec(memory_space=pltpu.VMEM)
    shape = jax.ShapeDtypeStruct
    gathered = {}
    lead = CHUNKS - 1
    for chunk in reversed(range(CHUNKS)):
        extra = heads if chunk == lead else 0
        taken = [total] if chunk == lead else []
        given = [shape((ROW_TILE, heads), F32)] if chunk == lead else []
        pieces = small_call(
            functools.partial(placed(pieces_kernel), states=states, chunk=chunk, count=count),
            [smem] * 3 + [vmem] * (2 + len(taken)),
            [shape((rows, cols + extra), BF16)] * count + given,
        )(*at, own, got, *taken)
        if chunk == lead:
            *pieces, base = pieces
        gathered[chunk] = swapped(pieces, chip_axis)
    entering = {}
    for chunk in reversed(range(CHUNKS)):
        extra = heads if chunk == lead else 0
        first_head = chunk * cols // width
        pieces = gathered[chunk]
        column, decay = small_call(
            functools.partial(placed(column_kernel), first_head=first_head, width=width, count=count, with_decay=chunk == lead),
            [smem] * 3 + [vmem] * (2 * count),
            [shape((rows, cols + extra), BF16), shape((ROW_TILE, cols), F32)],
        )(*at, *pieces, *gathered[lead])
        others = swapped([column] * blocks, outer_axis)[1:]
        if chunk == lead:
            tails = others
        states_out = small_call(
            functools.partial(
                placed(chips_kernel), first_head=first_head, width=width, count=count, blocks=blocks
            ),
            [smem] * 3 + [vmem] * (count + 2 * blocks - 1),
            [shape((rows, cols), BF16)] * count,
            [pltpu.VMEM((rows, cols), F32)],
        )(*at, *others, *tails, decay, *pieces)
        states_out = swapped(states_out, chip_axis)
        (entering[chunk],) = small_call(
            functools.partial(placed(assemble_kernel), count=count),
            [smem] * 3 + [vmem] * count,
            [shape((states, cols), BF16)],
        )(*at, *states_out)
    return entering, base


def entering_by_all_to_all(at, own, got, total, width, states, outer_axis, chip_axis):
    half_cols = own.shape[1]
    heads = total.shape[1]
    chips = lax.axis_size((outer_axis, chip_axis))
    rows = states // chips
    smem = pl.BlockSpec(memory_space=pltpu.SMEM)
    vmem = pl.BlockSpec(memory_space=pltpu.VMEM)
    chip_total, base = small_call(
        placed(chip_total_kernel),
        [smem] * 3 + [vmem] * 3,
        [jax.ShapeDtypeStruct((states, half_cols + heads), BF16), jax.ShapeDtypeStruct((ROW_TILE, heads), F32)],
    )(*at, own, got, total)
    sent = lax.all_to_all(
        chip_total.reshape(chips, rows, half_cols + heads),
        (outer_axis, chip_axis),
        split_axis=0,
        concat_axis=0,
        tiled=True,
    )
    blocks = GROUPS // CORES
    (entering,) = small_call(
        functools.partial(prefix_kernel, width=width, blocks=blocks),
        [vmem],
        [pltpu.HBM((chips, rows, half_cols), BF16)],
        [pltpu.VMEM((chips, rows, half_cols), BF16), pltpu.SemaphoreType.DMA((blocks,))],
        [pl.BlockSpec(memory_space=pltpu.HBM)],
    )(sent)
    entering = lax.all_to_all(entering, (outer_axis, chip_axis), split_axis=0, concat_axis=0, tiled=True)
    entering = entering.reshape(states, half_cols)
    return jnp.split(entering, CHUNKS, axis=1), base


def local(inputs, step_size, log_decay, b_matrix, c_matrix, skip_gain, *, outer_axis, chip_axis, core_axis):
    tokens, channels = inputs.shape
    heads = step_size.shape[1]
    width = channels // heads
    states = b_matrix.shape[1] // GROUPS
    per_group = heads // GROUPS
    group_cols = per_group * width
    per_half = GROUPS // CORES
    half_cols = channels // CORES
    chips = lax.axis_size((outer_axis, chip_axis))
    by_swaps = lax.axis_size(outer_axis) == 4 and chips == 16
    tall = states + ROW_TILE

    core = lax.axis_index(core_axis).astype(jnp.int32)
    mine = core.reshape(1)
    other = (1 - core).reshape(1)
    at = (mine,) + tuple(lax.axis_index(axis).astype(jnp.int32).reshape(1) for axis in (chip_axis, outer_axis))

    smem = pl.BlockSpec(memory_space=pltpu.SMEM)
    vmem = pl.BlockSpec(memory_space=pltpu.VMEM)
    hbm = pl.BlockSpec(memory_space=pltpu.HBM)

    state_dims = (per_half, group_cols, states)
    half_dims = (per_half, per_group, width)
    half_inputs = [
        jax.ShapeDtypeStruct((tokens, half_cols), BF16),
        jax.ShapeDtypeStruct((tokens, per_half * states), BF16),
    ]

    whole_step = step_size
    inputs, step_size, log_decay, b_matrix = (
        pltpu.with_memory_space_constraint(array, pltpu.HBM) for array in (inputs, step_size, log_decay, b_matrix)
    )
    send, run, run_t, factor, total, other_x, other_b = pl.pallas_call(
        functools.partial(send_state_kernel, dims=state_dims),
        in_specs=[smem] * 3 + [hbm] * 4,
        out_specs=[vmem] * 7,
        out_shape=[
            jax.ShapeDtypeStruct((tall, half_cols), BF16),
            jax.ShapeDtypeStruct((tokens, heads), F32),
            jax.ShapeDtypeStruct((heads, tokens), F32),
            jax.ShapeDtypeStruct((tokens, heads), F32),
            jax.ShapeDtypeStruct((ROW_TILE, heads), F32),
        ]
        + half_inputs,
        scratch_shapes=[pltpu.VMEM((heads, half_cols), BF16)]
        + [pltpu.VMEM((tokens, heads), F32)] * 2
        + [pltpu.SemaphoreType.DMA((2 * per_half + 2,))],
        compiler_params=plain_params(),
        name="send_state",
    )(other, *at[1:], inputs, b_matrix, step_size, log_decay)

    swap = [(0, 1), (1, 0)]
    got = lax.ppermute(send, core_axis, swap)

    own, matrix, own_x, own_b = small_call(
        functools.partial(own_state_kernel, dims=state_dims),
        [smem, hbm, hbm, vmem, vmem],
        [jax.ShapeDtypeStruct((tall, half_cols), BF16), jax.ShapeDtypeStruct((heads, half_cols), BF16)] + half_inputs,
        [pltpu.SemaphoreType.DMA((2 * per_half,))],
    )(mine, inputs, b_matrix, factor, total)

    find_entering = entering_by_swaps if by_swaps else entering_by_all_to_all
    entering, base = find_entering(at, own, got, total, width, states, outer_axis, chip_axis)
    late = lax.ppermute(own, core_axis, swap[:1])

    def within(half, x, b, before, first):
        return pl.pallas_call(
            functools.partial(within_kernel, dims=half_dims, first_group=first),
            grid_spec=pltpu.PrefetchScalarGridSpec(
                num_scalar_prefetch=2,
                grid=(PER_CALL,),
                in_specs=[vmem] * 8,
                out_specs=vmem,
                scratch_shapes=[pltpu.VMEM((2 * per_group, group_cols), BF16)],
            ),
            out_shape=jax.ShapeDtypeStruct((tokens, PER_CALL * group_cols), BF16),
            compiler_params=params(),
            name="within",
        )(
            half,
            mine,
            x,
            b,
            c_matrix,
            whole_step,
            run,
            run_t,
            skip_gain.reshape(1, heads),
            before,
        )

    own_within = []
    other_within = []
    for first in range(0, per_half, PER_CALL):
        own_within.append(within(mine, own_x, own_b, got, first))
        other_within.append(within(other, other_x, other_b, late, first))

    mixed = jax.ShapeDtypeStruct((tokens, channels), BF16)

    cols = PER_CALL * group_cols

    def finish_own(chunk, state, part):
        return small_call(
            functools.partial(own_final_kernel, dims=state_dims + (chunk * PER_CALL,)),
            [smem] + [vmem] * 6,
            [jax.ShapeDtypeStruct((tokens, cols), BF16)],
        )(mine, c_matrix, state, run, base, matrix, part)

    def finish_other(chunk, state, part, own_result, *result):
        return pl.pallas_call(
            functools.partial(final_kernel, dims=state_dims + (chunk * PER_CALL,)),
            in_specs=[smem] + [vmem] * 7 + [hbm] * len(result),
            out_specs=hbm,
            out_shape=mixed,
            scratch_shapes=[pltpu.VMEM((tokens, cols), BF16), pltpu.SemaphoreType.DMA((2 * PER_CALL,))],
            input_output_aliases={8: 0} if result else {},
            compiler_params=plain_params(),
            name="finish_other",
        )(other, c_matrix, state, run, base, matrix, part, own_result, *result)

    result = ()
    for chunk in reversed(range(CHUNKS)):
        got_entering = lax.ppermute(entering[chunk], core_axis, swap)
        (own_result,) = finish_own(chunk, entering[chunk], own_within[chunk])
        result = (finish_other(chunk, got_entering, other_within[chunk], own_result, *result),)
    return result[0]


def solution(mesh):
    outer, inner = mesh.axis_names
    chip_mesh = Mesh(
        mesh.devices.reshape(mesh.shape[outer], mesh.shape[inner] // CORES, CORES), (outer, "chip", "core")
    )
    placed = P((outer, "chip", "core"), None)

    def body(*args):
        return local(*args, outer_axis=outer, chip_axis="chip", core_axis="core")

    return jax.shard_map(body, mesh=chip_mesh, in_specs=(placed,) * 5 + (P(),), out_specs=placed, check_vma=False)
```
